32 devices in a mesh: gx: 2 (over y), gy: 4 (over z), gz: 4 (over x, core).
Axes of the slice: x: 2, y: 2, z: 4, core: 2. Of those that a mesh axis runs over, the one named last changes fastest.
Arguments:
- couplings: float32 [18, 16, 32, 512], P(None, 'gx', 'gy', 'gz'), may hold values from 0.05 to 2
- diagonal: float32 [3, 16, 32, 512], P(None, 'gx', 'gy', 'gz'), may hold values from 0.01 to 0.1
- right_side: float32 [3, 16, 32, 512], P(None, 'gx', 'gy', 'gz'), may hold values from -6 to 6
- guess: float32 [3, 16, 32, 512], P(None, 'gx', 'gy', 'gz'), may hold values from -4 to 4
Outputs:
- solution: float32 [3, 16, 32, 512], P(None, 'gx', 'gy', 'gz')
The draws below stay inside these ranges and needn't reach their ends.
All inputs are finite; a program needn't handle non-finite values.
Results may differ from the reference program's by a relative error of at most 0.00011.
Values sent between devices are 32-bit elements; how exact they have to be, the bound alone decides.
A program may use at most 128 MiB of HBM per device.

```python
import math
import jax
import jax.numpy as jnp

LEVELS = 4
SWEEPS = 2
COARSE_SWEEPS = 8
NX = 16
NY = 32
NZ = 512


def smooth_field(base_key, number):
    field_key = jax.random.fold_in(base_key, number)
    freq_key, angle_key, sign_key = jax.random.split(field_key, 3)
    freqs = jax.random.uniform(freq_key, (3, 3), jnp.float32, 0.5, 2.0)
    signs = jnp.where(jax.random.bernoulli(sign_key, 0.5, (3, 3)), 1.0, -1.0).astype(jnp.float32)
    freqs = freqs * signs
    angles = jax.random.uniform(angle_key, (3,), jnp.float32, 0.0, 2.0 * math.pi)
    coord_x = (jnp.arange(NX, dtype=jnp.float32) + 0.5) / NX
    coord_y = (jnp.arange(NY, dtype=jnp.float32) + 0.5) / NY
    coord_z = (jnp.arange(NZ, dtype=jnp.float32) + 0.5) / NZ
    result = jnp.zeros((NX, NY, NZ), jnp.float32)
    for wave in range(3):
        argument = freqs[wave, 0] * coord_x[:, None, None] + freqs[wave, 1] * coord_y[None, :, None] + freqs[wave, 2] * coord_z[None, None, :]
        result = result + jnp.cos(2.0 * math.pi * argument + angles[wave])
    return result / math.sqrt(1.5)


def draw_couplings(key, part):
    field_key = jax.random.fold_in(key, 1101)
    rough_key = jax.random.fold_in(key, 1102)
    sharpness = 3.0
    low_log = math.log(0.05)
    span_log = math.log(2.0) - math.log(0.05)
    planes = []
    for equation in range(3):
        fields = jnp.stack([smooth_field(field_key, 3 * equation + axis_number) for axis_number in range(3)])
        shares = jax.nn.softmax(sharpness * fields, axis=0)
        for axis_number in range(3):
            for side in range(2):
                uniform_part = jax.random.uniform(jax.random.fold_in(rough_key, 6 * equation + 2 * axis_number + side), (NX, NY, NZ), jnp.float32, 0.0, 1.0)
                exponent = 0.76 * shares[axis_number] + 0.24 * uniform_part
                planes.append(jnp.exp(low_log + span_log * exponent))
    return jnp.stack(planes).astype(jnp.float32)


def draw_diagonal(key, part):
    field_key = jax.random.fold_in(key, 2201)
    rough_key = jax.random.fold_in(key, 2202)
    power = 3.0
    planes = []
    for equation in range(3):
        region = jax.nn.sigmoid(2.0 * smooth_field(field_key, equation)) ** power
        uniform_part = jax.random.uniform(jax.random.fold_in(rough_key, equation), (NX, NY, NZ), jnp.float32, 0.0, 1.0)
        exponent = 0.68 * region + 0.32 * uniform_part
        planes.append(0.01 * jnp.exp(math.log(10.0) * exponent))
    return jnp.stack(planes).astype(jnp.float32)


def shard_levels(stream_key, shape, cuts, low, top_value):
    level = 1.0
    for dim, parts in cuts:
        steps = jax.random.uniform(jax.random.fold_in(jax.random.fold_in(stream_key, 6), dim), (parts,), jnp.float32, low / len(cuts), top_value / len(cuts))
        level = level * jnp.repeat(jnp.exp(steps), shape[dim] // parts).reshape((-1,) + (1,) * (len(shape) - 1 - dim))
    return level


def normal_values(key, shape, deviation, most, shards=(), held_as=jnp.bfloat16):
    gain = shard_levels(key, shape, shards, -0.22, 0.18) if shards else 1.0
    values = jax.random.normal(key, shape, jnp.float32) * deviation * gain
    return jnp.minimum(jnp.maximum(values, -most), most).astype(held_as)


def setup_inputs(seed: int = 0) -> dict:
    streams_of = jax.random.split(jax.random.key(seed), 5)
    couplings = draw_couplings(jax.random.fold_in(streams_of[4], 71), 0)
    diagonal = draw_diagonal(jax.random.fold_in(streams_of[4], 71), 0)
    right_side = normal_values(streams_of[2], (3, NX, NY, NZ), 1.0, 6.0, ((1, 2), (2, 4), (3, 4)), jnp.float32)
    guess = normal_values(streams_of[3], (3, NX, NY, NZ), 0.5, 4.0, ((1, 2), (2, 4), (3, 4)), jnp.float32)
    return {"couplings": couplings, "diagonal": diagonal, "right_side": right_side, "guess": guess}


damping = 0.8


def pad_zero(field):
    return jnp.pad(field, ((0, 0), (1, 1), (1, 1), (1, 1)))


def operate(field, padded, weights, total):
    near = [padded[:, 2:, 1:-1, 1:-1], padded[:, :-2, 1:-1, 1:-1],
            padded[:, 1:-1, 2:, 1:-1], padded[:, 1:-1, :-2, 1:-1],
            padded[:, 1:-1, 1:-1, 2:], padded[:, 1:-1, 1:-1, :-2]]
    offdiag = weights[:, 0] * near[0]
    for index in range(1, 6):
        offdiag = offdiag + weights[:, index] * near[index]
    return total * field - offdiag


def coarsen(array):
    shape = array.shape
    count = len(shape)
    blocks = array.reshape(shape[:-3] + (shape[-3] // 2, 2, shape[-2] // 2, 2, shape[-1] // 2, 2))
    return jnp.mean(blocks, axis=(count - 2, count, count + 2))


def refine(array):
    return jnp.repeat(jnp.repeat(jnp.repeat(array, 2, axis=-3), 2, axis=-2), 2, axis=-1)


def hierarchy(couplings, diagonal):
    weights = couplings.reshape((3, 6) + diagonal.shape[1:])
    local_diag = diagonal
    result = []
    for level in range(LEVELS):
        if level > 0:
            weights = coarsen(weights) * 0.25
            local_diag = coarsen(local_diag)
        result.append((weights, local_diag + jnp.sum(weights, axis=1)))
    return result


def reference(couplings, diagonal, right_side, guess):
    levels = hierarchy(couplings, diagonal)

    def cycle(level, field, rhs):
        weights, total = levels[level]

        def sweep(value):
            return value + damping * (rhs - operate(value, pad_zero(value), weights, total)) / total

        if level == LEVELS - 1:
            for step in range(COARSE_SWEEPS):
                field = sweep(field)
            return field
        for step in range(SWEEPS):
            field = sweep(field)
        resid = rhs - operate(field, pad_zero(field), weights, total)
        coarse_rhs = coarsen(resid)
        correction = cycle(level + 1, jnp.zeros_like(coarse_rhs), coarse_rhs)
        field = field + refine(correction)
        for step in range(SWEEPS):
            field = sweep(field)
        return field

    return cycle(0, guess, right_side)
```

```python
import functools

import jax
import jax.numpy as jnp
from jax import lax
from jax.experimental import pallas as pl
from jax.experimental.pallas import tpu as pltpu
from jax.sharding import PartitionSpec as P

SWEEPS = 2
COARSE_SWEEPS = 8
DAMP = 0.8
EQ = 3
MESH = pl.DeviceIdType.MESH
HIGH = lax.Precision.HIGHEST


def roll(value, shift, axis):
    size = value.shape[axis]
    shift = shift % size
    return value if shift == 0 else pltpu.roll(value, shift, axis)


def iota(shape, axis):
    return lax.broadcasted_iota(jnp.int32, shape, axis)


def kernel(
    dims, cores, w_hbm, d_hbm, b_hbm, g_hbm, out_ref,
    w_ref, d_ref, b_ref, g_ref, field, halo_x, halo_y, pack_s, pack_r, tot0, c0, w1, tot1, c1, b1,
    wsend, wall, bsend, ball, e2, lines,
    s_sem, r_sem, ws_sem, wr_sem, bs_sem, br_sem, l_sem, i_sem,
):
    ngx, ngy, ngz = dims
    nx, ny, nz = g_ref.shape[1:]
    qx, qy, qz = nx // 4, ny // 4, nz // 4
    rows = ngx * ngy
    nX = ngz // cores
    gx, gy, gz = lax.axis_index("gx"), lax.axis_index("gy"), lax.axis_index("gz")
    X, core = gz // cores, gz % cores
    row = gy * ngx + gx
    axes = (("gx", gx, ngx), ("gy", gy, ngy), ("gz", gz, ngz))

    def device(name, index):
        here = {"gx": gx, "gy": gy, "gz": gz}
        here[name] = index
        return (here["gx"], here["gy"], here["gz"])

    barrier = pltpu.get_barrier_semaphore()
    close = ngy <= 4 and ngz <= 4
    awaited = 0
    for name, index, count in axes:
        if close and name != "gx":
            for step in (-1, 1):
                @pl.when((index + step >= 0) & (index + step < count))
                def _():
                    pl.semaphore_signal(
                        barrier, inc=1, device_id=device(name, jnp.clip(index + step, 0, count - 1)),
                        device_id_type=MESH,
                    )
            awaited = awaited + (index > 0).astype(jnp.int32) + (index < count - 1).astype(jnp.int32)
        else:
            for step in range(1, count):
                pl.semaphore_signal(
                    barrier, inc=1, device_id=device(name, (index + step) % count), device_id_type=MESH
                )
            awaited = awaited + (count - 1)

    loads = [
        pltpu.make_async_copy(a, z, i_sem.at[slot])
        for slot, (a, z) in enumerate(
            ((g_hbm, g_ref), (w_hbm, w_ref), (d_hbm, d_ref), (b_hbm, b_ref))
        )
    ]
    for load in loads:
        load.start()

    rounds = field.shape[0]
    for name, index, count in axes:
        for side in range(2):
            @pl.when(index == (0 if side == 0 else count - 1))
            def _():
                for r in range(rounds):
                    if name == "gx":
                        halo_x[r, side] = jnp.zeros(halo_x.shape[2:], jnp.float32)
                    elif name == "gy":
                        lo = 0 if side == 0 else ny // 2
                        halo_y[r, :, :, lo : lo + ny // 2] = jnp.zeros(
                            (EQ, nx, ny // 2, nz), jnp.float32
                        )
                    else:
                        pack_r[r, side] = jnp.zeros(pack_r.shape[2:], jnp.float32)

    lane2 = iota((ny, nz), 1)

    def copies(r, n, s):
        src = g_ref if r == 0 else field.at[r]
        made = []
        for side in range(2):
            other = 1 - side
            for place, (name, index, count) in enumerate(axes):
                if name == "gx":
                    a = src.at[:, 0 if side == 0 else n - 1]
                    z = halo_x.at[r, other]
                elif name == "gy":
                    a = src.at[:, 0:n, pl.ds(0 if side == 0 else ny - s, s)]
                    z = halo_y.at[r, :, 0:n, pl.ds(ny - s if side == 0 else 0, s)]
                else:
                    a = pack_s.at[r, side]
                    z = pack_r.at[r, other]
                target = index - 1 if side == 0 else index + 1
                has_target = index > 0 if side == 0 else index < count - 1
                has_source = index < count - 1 if side == 0 else index > 0
                slot = 2 * place + side
                made.append((
                    pltpu.make_async_remote_copy(
                        src_ref=a, dst_ref=z,
                        send_sem=s_sem.at[r, slot], recv_sem=r_sem.at[r, slot],
                        device_id=device(name, jnp.clip(target, 0, count - 1)),
                        device_id_type=MESH,
                    ),
                    has_target, has_source, name,
                ))
        return made

    def send(r, value, n, s):
        made = copies(r, n, s)
        if r > 0:
            for e in range(EQ):
                field[r, e, 0:n] = value[e]
        def begin(along_z):
            for copy, has_target, _, name in made:
                if (name == "gz") == along_z:
                    @pl.when(has_target)
                    def _():
                        copy.start()

        if r > 0:
            begin(False)
        low = jnp.zeros((ny, nz), jnp.float32)
        high = jnp.zeros((ny, nz), jnp.float32)
        for e in range(EQ):
            for i in range(n):
                here = lane2 == e * n + i
                low = jnp.where(here, jnp.broadcast_to(value[e][i, :, 0:1], (ny, nz)), low)
                high = jnp.where(here, jnp.broadcast_to(value[e][i, :, nz - 1 : nz], (ny, nz)), high)
        pack_s[r, 0] = low
        pack_s[r, 1] = high
        if r == 0:
            pl.semaphore_wait(barrier, awaited)
            begin(False)
        begin(True)

    def receive(r, n, s):
        for copy, _, has_source, _ in copies(r, n, s):
            @pl.when(has_source)
            def _():
                copy.wait_recv()

    def before(v, e, n, s, weight, base, scale):
        shape = (n, ny, nz)
        y, z = iota(shape, 1), iota(shape, 2)
        edge = jnp.zeros((1, ny, nz), jnp.float32)
        near = [
            jnp.concatenate([v[1:], edge], axis=0),
            jnp.concatenate([edge, v[:-1]], axis=0),
            jnp.where(y >= ny - s, 0.0, roll(v, -s, 1)),
            jnp.where(y < s, 0.0, roll(v, s, 1)),
            jnp.where(z >= nz - s, 0.0, roll(v, -s, 2)),
            jnp.where(z < s, 0.0, roll(v, s, 2)),
        ]
        w = [weight(e, k) for k in range(6)]
        total = w[0] * near[0]
        for k in range(1, 6):
            total = total + w[k] * near[k]
        wy = jnp.where(y >= ny - s, w[2], jnp.where(y < s, w[3], 0.0))
        wz = jnp.where(z >= nz - s, w[4], jnp.where(z < s, w[5], 0.0))
        up, down = w[0][n - 1], w[1][0]
        if scale is not None:
            total, wy, wz = scale * total, scale * wy, scale * wz
            up, down = scale[n - 1] * up, scale[0] * down
        return base + total, up, down, wy, wz

    def after(r, e, n, s, ready):
        total, up, down, wy, wz = ready
        shape = (n, ny, nz)
        y, z = iota(shape, 1), iota(shape, 2)
        low = pack_r[r, 0]
        high = pack_r[r, 1]
        zl = jnp.stack([jnp.broadcast_to(low[:, e * n + i : e * n + i + 1], (ny, nz)) for i in range(n)])
        zh = jnp.stack([jnp.broadcast_to(high[:, e * n + i : e * n + i + 1], (ny, nz)) for i in range(n)])
        hy = jnp.where((y < s) | (y >= ny - s), halo_y[r, e, 0:n], 0.0)
        total = total + wy * hy + wz * jnp.where(z < s, zl, zh)
        first = total[0] + down * halo_x[r, 0, e]
        last = total[n - 1] + up * halo_x[r, 1, e]
        return jnp.concatenate([first[None], total[1 : n - 1], last[None]], axis=0)

    def coarsen(a, s):
        n = a.shape[0]
        a = jnp.stack([a[2 * i] + a[2 * i + 1] for i in range(n // 2)])
        y, z = iota(a.shape, 1), iota(a.shape, 2)
        a = a + jnp.where((y // s) % 2 == 0, roll(a, -s, 1), roll(a, s, 1))
        a = a + jnp.where((z // s) % 2 == 0, roll(a, -s, 2), roll(a, s, 2))
        return a * 0.125

    def spread(a):
        return jnp.stack([a[i // 2] for i in range(2 * a.shape[0])])

    def weight0(e, k):
        return w_ref[6 * e + k]

    def weight1(e, k):
        return w1[6 * e + k]

    source = iota((nz, nz), 0)
    target = iota((nz, nz), 1)
    squeeze = jnp.where(source == 4 * (target % qz), 1.0, 0.0).astype(jnp.float32)

    def to_rows(a):
        m = a.shape[0]
        c = jnp.dot(a.reshape(m * qx * ny, nz), squeeze, precision=HIGH,
                    preferred_element_type=jnp.float32).reshape(m, qx, ny, nz)
        shape = (m, ny, nz)
        lane = iota(shape, 2)
        got = jnp.zeros(shape, jnp.float32)
        for x in range(qx):
            for y in range(qy):
                part = roll(c[:, x], -4 * y, 1)
                got = jnp.where(lane // qz == x * qy + y, part, got)
        return got

    def own(small, whole, sem):
        return pltpu.make_async_copy(
            small.at[:, pl.ds(0, 1)], whole.at[X, core, :, pl.ds(row, 1)], sem
        )

    def stage(number, small, whole, ss, rs):
        made = []
        if number == 0:
            for step in range(1, ngx):
                made.append((small.at[:, pl.ds(0, 1)], whole.at[X, core, :, pl.ds(row, 1)],
                             step, device("gx", (gx + step) % ngx)))
        elif number == 1:
            block = whole.at[X, core, :, pl.ds(gy * ngx, ngx)]
            for step in range(1, ngy):
                made.append((block, block, step, device("gy", (gy + step) % ngy)))
        elif number == 2:
            block = whole.at[X, core]
            for step in range(1, nX):
                made.append((block, block, step, device("gz", ((X + step) % nX) * cores + core)))
        else:
            block = whole.at[:, core]
            for step in range(1, cores):
                made.append((block, block, step, device("gz", X * cores + (core + step) % cores)))
        return [
            pltpu.make_async_remote_copy(
                src_ref=a, dst_ref=z, send_sem=ss.at[number, step], recv_sem=rs.at[number, step],
                device_id=where, device_id_type=MESH,
            )
            for a, z, step, where in made
        ]

    wargs = (wsend, wall, ws_sem, wr_sem)

    def everyone():
        made = []
        for az in range(ngz):
            for ay in range(ngy):
                for ax in range(ngx):
                    if ax + ay + az == 0:
                        continue
                    made.append(pltpu.make_async_remote_copy(
                        src_ref=bsend.at[:, pl.ds(0, 1)],
                        dst_ref=ball.at[X, core, :, pl.ds(row, 1)],
                        send_sem=bs_sem, recv_sem=br_sem,
                        device_id=((gx + ax) % ngx, (gy + ay) % ngy, (gz + az) % ngz),
                        device_id_type=MESH,
                    ))
        return made

    def start(number, args):
        for copy in stage(number, *args):
            copy.start()

    def finish(number, args):
        for copy in stage(number, *args):
            copy.wait_recv()

    loads[0].wait()
    v = [g_ref[e] for e in range(EQ)]
    send(0, v, nx, 1)
    for load in loads[1:]:
        load.wait()
    for e in range(EQ):
        total = d_ref[e]
        for k in range(6):
            total = total + w_ref[6 * e + k]
        tot0[e] = total
        c0[e] = DAMP / total
        total = coarsen(d_ref[e], 1)
        wsend_d = coarsen(total, 2)
        for k in range(6):
            w = 0.25 * coarsen(w_ref[6 * e + k], 1)
            w1[6 * e + k] = w
            total = total + w
            wsend[6 * e + k] = to_rows((0.25 * coarsen(w, 2))[None])[0]
        wsend[6 * EQ + e] = to_rows(wsend_d[None])[0]
        tot1[e] = total
        c1[e] = DAMP / total
    own(wsend, wall, l_sem.at[0]).start()
    start(0, wargs)

    keep = 1.0 - DAMP

    def apply(r, v, n, s, weight, base, scale):
        ready = [
            before(v[e], e, n, s, weight, base(e), None if scale is None else scale[e])
            for e in range(EQ)
        ]
        if r != 5:
            receive(r, n, s)
        return [after(r, e, n, s, ready[e]) for e in range(EQ)]

    def smooth0(r, v):
        return apply(r, v, nx, 1, weight0, lambda e: keep * v[e] + c0[e] * b_ref[e], c0)

    def smooth1(r, v):
        return apply(r, v, nx // 2, 2, weight1, lambda e: keep * v[e] + c1[e] * b1[e], c1)

    v = smooth0(0, v)
    send(1, v, nx, 1)
    v = smooth0(1, v)
    own(wsend, wall, l_sem.at[0]).wait()
    finish(0, wargs)
    send(2, v, nx, 1)
    start(1, wargs)
    u = []
    rest = apply(2, v, nx, 1, weight0, lambda e: b_ref[e] - tot0[e] * v[e], None)
    for e in range(EQ):
        b = coarsen(rest[e], 1)
        b1[e] = b
        u.append(c1[e] * b)
    half = nx // 2
    send(3, u, half, 2)
    u = smooth1(3, u)
    finish(1, wargs)
    send(4, u, half, 2)
    start(2, wargs)
    rest = apply(4, u, half, 2, weight1, lambda e: b1[e] - tot1[e] * u[e], None)
    bsend[...] = to_rows(jnp.stack([coarsen(rest[e], 2) for e in range(EQ)]))
    for copy in reversed(everyone()):
        copy.start()
    own(bsend, ball, br_sem).start()
    finish(2, wargs)
    start(3, wargs)
    finish(3, wargs)

    shape = (ngz, rows, nz)
    r_i, l_i = iota(shape, 1), iota(shape, 2)
    g_i = iota(shape, 0)
    zi, yi, xi = l_i % qz, (l_i // qz) % qy, l_i // (qz * qy)
    gyi, gxi = r_i // ngx, r_i % ngx
    inside = [
        ~((xi == qx - 1) & (gxi == ngx - 1)), ~((xi == 0) & (gxi == 0)),
        ~((yi == qy - 1) & (gyi == ngy - 1)), ~((yi == 0) & (gyi == 0)),
        ~((zi == qz - 1) & (g_i == ngz - 1)), ~((zi == 0) & (g_i == 0)),
    ]

    def whole(ref, index):
        return ref[:, :, index].reshape(shape)

    def next_of(v):
        return jnp.concatenate([v[1:], v[:1]], axis=0)

    def prev_of(v):
        return jnp.concatenate([v[-1:], v[:-1]], axis=0)

    def near2(v):
        sy, sx = qz, qz * qy
        return [
            jnp.where(xi == qx - 1, roll(roll(v, (qx - 1) * sx, 2), -1, 1), roll(v, -sx, 2)),
            jnp.where(xi == 0, roll(roll(v, -(qx - 1) * sx, 2), 1, 1), roll(v, sx, 2)),
            jnp.where(yi == qy - 1, roll(roll(v, (qy - 1) * sy, 2), -ngx, 1), roll(v, -sy, 2)),
            jnp.where(yi == 0, roll(roll(v, -(qy - 1) * sy, 2), ngx, 1), roll(v, sy, 2)),
            jnp.where(zi == qz - 1, roll(next_of(v), qz - 1, 2), roll(v, -1, 2)),
            jnp.where(zi == 0, roll(prev_of(v), -(qz - 1), 2), roll(v, 1, 2)),
        ]

    def dot_near(weights, near):
        total = weights[0] * near[0]
        for k in range(1, 6):
            total = total + weights[k] * near[k]
        return total

    def pair(a):
        sy, sx = qz, qz * qy
        a = a + jnp.where(xi % 2 == 0, roll(a, -sx, 2), roll(a, sx, 2))
        a = a + jnp.where(yi % 2 == 0, roll(a, -sy, 2), roll(a, sy, 2))
        a = a + jnp.where(zi % 2 == 0, roll(a, -1, 2), roll(a, 1, 2))
        return a * 0.125

    groups = qx * qy
    tiles = ngz // groups
    shape3 = (tiles, rows, nz)
    r3, l3, t3 = iota(shape3, 1), iota(shape3, 2), iota(shape3, 0)
    inside3 = [
        r3 % ngx < ngx - 1, r3 % ngx > 0, r3 // ngx < ngy - 1, r3 // ngx > 0,
        ~((l3 >= nz - 2) & (t3 == tiles - 1)), ~((l3 < 2) & (t3 == 0)),
    ]

    def join(a):
        a = a.reshape(tiles, groups, rows, nz)
        got = a[:, 0]
        for j in range(1, groups):
            got = jnp.where(l3 // qz == j, a[:, j], got)
        return got

    def part(a):
        parts = []
        for j in range(groups):
            mine = jnp.where(l3 // qz == j, a, 0.0)
            size = qz
            while size < nz:
                mine = mine + roll(mine, size, 2)
                size *= 2
            parts.append(mine)
        return jnp.stack(parts, axis=1).reshape(shape)

    def near3(v):
        if tiles == 1:
            up, down = roll(v, -2, 2), roll(v, 2, 2)
        else:
            up = jnp.where(l3 >= nz - 2, roll(next_of(v), -2, 2), roll(v, -2, 2))
            down = jnp.where(l3 < 2, roll(prev_of(v), 2, 2), roll(v, 2, 2))
        return [roll(v, -1, 1), roll(v, 1, 1), roll(v, -ngx, 1), roll(v, ngx, 1), up, down]

    w2, t2, w3, t3s = [], [], [], []
    for e in range(EQ):
        plain = [whole(wall, 6 * e + k) for k in range(6)]
        d2 = whole(wall, 6 * EQ + e)
        total = d2
        for k in range(6):
            total = total + plain[k]
        t2.append(total)
        w2.append([jnp.where(inside[k], plain[k], 0.0) for k in range(6)])
        plain3 = [0.25 * join(pair(plain[k])) for k in range(6)]
        total = join(pair(d2))
        for k in range(6):
            total = total + plain3[k]
        t3s.append(total)
        w3.append([jnp.where(inside3[k], plain3[k], 0.0) for k in range(6)])
    c2 = [DAMP / t for t in t2]
    c3 = [DAMP / t for t in t3s]

    pltpu.make_async_copy(ball, ball, br_sem).wait()

    every = range(EQ)
    rhs = [whole(ball, e) for e in every]

    def smooth2(v):
        return [keep * v[e] + c2[e] * (rhs[e] + dot_near(w2[e], near2(v[e]))) for e in every]

    v2 = [c2[e] * rhs[e] for e in every]
    for step in range(SWEEPS - 1):
        v2 = smooth2(v2)
    rest = [rhs[e] - t2[e] * v2[e] + dot_near(w2[e], near2(v2[e])) for e in every]
    rhs3 = [join(pair(rest[e])) for e in every]
    v3 = [c3[e] * rhs3[e] for e in every]
    for step in range(COARSE_SWEEPS - 1):
        v3 = [keep * v3[e] + c3[e] * (rhs3[e] + dot_near(w3[e], near3(v3[e]))) for e in every]
    v2 = [v2[e] + part(v3[e]) for e in every]
    for step in range(SWEEPS):
        v2 = smooth2(v2)
    for e in every:
        e2[e] = v2[e]

    wide = groups * nz
    source = iota((nz, wide), 0)
    target = iota((nz, wide), 1)
    widen = jnp.where(source == (target // nz) * qz + (target % nz) // 4, 1.0, 0.0).astype(jnp.float32)
    around = [(gx, gy, gz, None)]
    for axis, index, count in ((0, gx, ngx), (1, gy, ngy), (2, gz, ngz)):
        for step in (-1, 1):
            at = [gx, gy, gz]
            at[axis] = jnp.clip(index + step, 0, count - 1)
            has = index > 0 if step < 0 else index < count - 1
            around.append((at[0], at[1], at[2], has))
    for e in range(EQ):
        for j, (ax, ay, az, has) in enumerate(around):
            line = e2[e, az, pl.ds(ay * ngx + ax, 1), :]
            if has is not None:
                line = jnp.where(has, line, 0.0)
            lines[e * 7 + j : e * 7 + j + 1, :] = line
    for j in range(EQ * 7, lines.shape[0]):
        lines[j : j + 1, :] = jnp.zeros((1, nz), jnp.float32)
    back = jnp.dot(lines[...], widen, precision=HIGH, preferred_element_type=jnp.float32)
    ysel = iota((ny, nz), 0) // 4

    def strip(e, j, x, y):
        col = (x * qy + y) * nz
        return jnp.broadcast_to(back[e * 7 + j : e * 7 + j + 1, col : col + nz], (ny, nz))

    def plane(e, j, x):
        got = strip(e, j, x, 0)
        for y in range(1, qy):
            got = jnp.where(ysel == y, strip(e, j, x, y), got)
        return got

    low, high = pack_r[4, 0], pack_r[4, 1]
    for e in range(EQ):
        halo_x[5, 0, e] = halo_x[4, 0, e] + plane(e, 1, qx - 1)
        halo_x[5, 1, e] = halo_x[4, 1, e] + plane(e, 2, 0)
        for x in range(qx):
            edge = jnp.where(ysel < qy // 2, strip(e, 3, x, qy - 1), strip(e, 4, x, 0))
            below, above = plane(e, 5, x), plane(e, 6, x)
            for i in (2 * x, 2 * x + 1):
                halo_y[5, e, i] = halo_y[4, e, i] + edge
                here = lane2 == e * half + i
                low = jnp.where(here, low + jnp.broadcast_to(below[:, nz - 1 : nz], (ny, nz)), low)
                high = jnp.where(here, high + jnp.broadcast_to(above[:, 0:1], (ny, nz)), high)
        u[e] = u[e] + spread(jnp.stack([plane(e, 0, x) for x in range(qx)]))
    pack_r[5, 0] = low
    pack_r[5, 1] = high
    u = smooth1(5, u)
    send(6, u, half, 2)
    u = smooth1(6, u)
    v = [field[2, e] + spread(u[e]) for e in range(EQ)]
    send(7, v, nx, 1)
    v = smooth0(7, v)
    send(8, v, nx, 1)
    v = smooth0(8, v)
    for e in range(EQ):
        out_ref[e] = v[e]

    for r in range(rounds):
        if r == 5:
            continue
        n, s = (half, 2) if 3 <= r <= 6 else (nx, 1)
        for copy, has_target, _, _ in copies(r, n, s):
            @pl.when(has_target)
            def _():
                copy.wait_send()
    for number in range(4):
        for copy in stage(number, *wargs):
            copy.wait_send()
    for copy in everyone():
        copy.wait_send()


def per_device(dims, cores, couplings, diagonal, right_side, guess):
    ngx, ngy, ngz = dims
    brick = guess.shape[1:]
    nx, ny, nz = brick
    half = nx // 2
    rows = ngx * ngy
    nX = ngz // cores
    rounds = 9
    peers = max(ngx, ngy, nX, cores)
    f32 = jnp.float32
    vmem = pltpu.VMEM
    dma = pltpu.SemaphoreType.DMA
    return pl.pallas_call(
        functools.partial(kernel, dims, cores),
        out_shape=vmem(guess.shape, f32),
        in_specs=[pl.BlockSpec(memory_space=pl.ANY)] * 4,
        out_specs=pl.BlockSpec(memory_space=vmem),
        scratch_shapes=[
            vmem(couplings.shape, f32),
            vmem(diagonal.shape, f32),
            vmem(right_side.shape, f32),
            vmem(guess.shape, f32),
            vmem((rounds, EQ) + brick, f32),
            vmem((rounds, 2, EQ, ny, nz), f32),
            vmem((rounds, EQ) + brick, f32),
            vmem((rounds, 2, ny, nz), f32),
            vmem((rounds, 2, ny, nz), f32),
            vmem((EQ,) + brick, f32),
            vmem((EQ,) + brick, f32),
            vmem((6 * EQ, half, ny, nz), f32),
            vmem((EQ, half, ny, nz), f32),
            vmem((EQ, half, ny, nz), f32),
            vmem((EQ, half, ny, nz), f32),
            vmem((7 * EQ, ny, nz), f32),
            vmem((nX, cores, 7 * EQ, rows, nz), f32),
            vmem((EQ, ny, nz), f32),
            vmem((nX, cores, EQ, rows, nz), f32),
            vmem((EQ, ngz, rows, nz), f32),
            vmem((-(-EQ * 7 // 8) * 8, nz), f32),
            dma((rounds, 6)),
            dma((rounds, 6)),
            dma((4, peers)),
            dma((4, peers)),
            dma,
            dma,
            dma((1,)),
            dma((4,)),
        ],
        compiler_params=pltpu.CompilerParams(
            collective_id=0, has_side_effects=True, vmem_limit_bytes=60 * 1024 * 1024
        ),
    )(couplings, diagonal, right_side, guess)


def solution(mesh):
    dims = (mesh.shape["gx"], mesh.shape["gy"], mesh.shape["gz"])
    cores = 2 if dims[2] % 2 == 0 else 1
    spec = P(None, "gx", "gy", "gz")
    return jax.shard_map(
        functools.partial(per_device, dims, cores),
        mesh=mesh,
        in_specs=(spec,) * 4,
        out_specs=spec,
        check_vma=False,
    )
```

```python
import functools

import jax
import jax.numpy as jnp
from jax import lax
from jax.experimental import pallas as pl
from jax.experimental.pallas import tpu as pltpu
from jax.sharding import PartitionSpec as P

SWEEPS = 2
COARSE_SWEEPS = 8
DAMP = 0.8
KEEP = 1.0 - DAMP
EQ = 3
MESH = pl.DeviceIdType.MESH
HIGH = lax.Precision.HIGHEST
DEEP = (False, True, True, False, True)
FINE = (True, True, False, False, True)


def roll(value, shift, axis):
    size = value.shape[axis]
    shift = shift % size
    return value if shift == 0 else pltpu.roll(value, shift, axis)


def iota(shape, axis):
    return lax.broadcasted_iota(jnp.int32, shape, axis)


class Level:
    def __init__(self, n, s, refs):
        self.n, self.s = n, s
        (self.cw, self.st, self.xw, self.cb, self.tot, self.zs,
         self.xt, self.xst, self.yst, self.yxw, self.zst, self.r_sem) = refs


def kernel(
    dims, cores, w_hbm, d_hbm, b_hbm, g_hbm, out_ref,
    w_ref, d_ref, b_ref, g_ref,
    tally, field, pfield, zpack, hx, hy, hz, px, py, pz, exy, exz, eyz, w1, *rest,
):
    level_refs = (rest[:12], rest[12:24])
    (wsend, wall, bsend, ball, e2, lines,
     s_sem, r_sem, ws_sem, wr_sem, bs_sem, br_sem, l_sem, i_sem, know) = rest[24:]
    ngx, ngy, ngz = dims
    nx, ny, nz = g_ref.shape[1:]
    half = nx // 2
    qx, qy, qz = nx // 4, ny // 4, nz // 4
    rows = ngx * ngy
    nX = ngz // cores
    gx, gy, gz = lax.axis_index("gx"), lax.axis_index("gy"), lax.axis_index("gz")
    X, core = gz // cores, gz % cores
    row = gy * ngx + gx
    axes = (("gx", gx, ngx), ("gy", gy, ngy), ("gz", gz, ngz))
    L0 = Level(nx, 1, level_refs[0])
    L1 = Level(half, 2, level_refs[1])
    tile = (ny, nz)
    yi, zi = iota(tile, 0), iota(tile, 1)
    every = range(EQ)

    def device(**change):
        here = {"gx": gx, "gy": gy, "gz": gz}
        here.update(change)
        return (here["gx"], here["gy"], here["gz"])

    barrier = pltpu.get_barrier_semaphore()
    close = ngy <= 4 and ngz <= 4
    awaited = 0

    def greet(ok, where):
        @pl.when(ok)
        def _():
            pl.semaphore_signal(barrier, inc=1, device_id=where, device_id_type=MESH)
        return ok.astype(jnp.int32)

    for name, index, count in axes:
        if close and name != "gx":
            steps = (-1, 1) if name == "gy" or cores == 1 else (-1, 1, -cores, cores)
            for step in steps:
                ok = (index + step >= 0) & (index + step < count)
                awaited = awaited + greet(ok, device(**{name: jnp.clip(index + step, 0, count - 1)}))
        else:
            for step in range(1, count):
                pl.semaphore_signal(
                    barrier, inc=1, device_id=device(**{name: (index + step) % count}),
                    device_id_type=MESH,
                )
            awaited = awaited + (count - 1)

    loads = [
        pltpu.make_async_copy(a, z, i_sem.at[slot])
        for slot, (a, z) in enumerate(
            ((g_hbm, g_ref), (w_hbm, w_ref), (d_hbm, d_ref), (b_hbm, b_ref))
        )
    ]
    for load in loads:
        load.start()

    there = {
        name: (index > 0, index < count - 1) for name, index, count in axes
    }
    beside = {
        name: (jnp.maximum(index - 1, 0), jnp.minimum(index + 1, count - 1))
        for name, index, count in axes
    }

    def edge_rows(s, lo, hi):
        return (yi < jnp.where(lo, s, 0)) | (yi >= jnp.where(hi, ny - s, ny))

    def remote(a, z, ss, rs, where):
        return pltpu.make_async_remote_copy(
            src_ref=a, dst_ref=z, send_sem=ss, recv_sem=rs,
            device_id=where, device_id_type=MESH,
        )

    def rows_of(side, s):
        return pl.ds(0 if side == 0 else ny - s, s)

    counts = [
        [k for k in (0, 1, 2) if (k > 0 or count == 1) and k < count and (k == 2 or count <= 2 or k == 1)]
        for _, _, count in axes
    ]
    found = [
        there[name][0].astype(jnp.int32) + there[name][1].astype(jnp.int32) for name, _, _ in axes
    ]
    cases = []
    for cx in counts[0]:
        for cy in counts[1]:
            for cz in counts[2]:
                cases.append(((cx, cy, cz), (found[0] == cx) & (found[1] == cy) & (found[2] == cz)))

    def await_rows(sem, number):
        if number > 0:
            part = next(k for k in (8, 4, 2, 1) if number % k == 0)
            ref = tally.at[pl.ds(0, number // part), pl.ds(0, part)]
            pltpu.make_async_copy(ref, ref, sem).wait()

    def await_all(sem, groups):
        for (cx, cy, cz), ok in cases:
            many = {"x": cx, "y": cy, "z": cz, "xy": cx * cy, "xz": cx * cz, "yz": cy * cz}
            number = sum(many[kind] * size for g in groups for kind, size in g.sizes.items())
            if len(cases) == 1:
                await_rows(sem, number)
            else:
                @pl.when(ok)
                def _():
                    await_rows(sem, number)

    class Group:
        def __init__(self, sem):
            self.sem, self.copies, self.sizes = sem, [], {}

        def add(self, kind, side, a, z, where, goes):
            self.copies.append((remote(a, z, s_sem, self.sem, where), goes))
            if side == 0:
                size = 1
                for d in z.shape[:-1]:
                    size *= d
                self.sizes[kind] = self.sizes.get(kind, 0) + size

    def plan(r):
        n, s = (nx, 1) if FINE[r] else (half, 2)
        src = g_ref if r == 0 else field.at[r]
        groups = {k: Group(r_sem.at[r, "vdp".index(k)]) for k in "vdp"}
        kinds = [("v", src, 0, hx, hy, hz)]
        if DEEP[r]:
            kinds.append(("p", pfield.at[r], 1, px, py, pz))
        for side in range(2):
            other = 1 - side
            for group, a, which, zx, zy, zz in kinds:
                g = groups[group]
                g.add("x", side, a.at[:, 0 if side == 0 else n - 1], zx.at[r, other],
                      device(gx=beside["gx"][side]), there["gx"][side])
                g.add("y", side, a.at[:, 0:n, rows_of(side, s)], zy.at[r, :, 0:n, rows_of(other, s)],
                      device(gy=beside["gy"][side]), there["gy"][side])
                g.add("z", side, zpack.at[r, which], zz.at[r, other],
                      device(gz=beside["gz"][side]), there["gz"][side])
        if DEEP[r]:
            g = groups["d"]
            for i in range(2):
                for j in range(2):
                    g.add("xy", 2 * i + j, src.at[:, 0 if i == 0 else n - 1, rows_of(j, s)],
                          exy.at[r, 1 - i, :, rows_of(1 - j, s)],
                          device(gx=beside["gx"][i], gy=beside["gy"][j]),
                          there["gx"][i] & there["gy"][j])
                    g.add("xz", 2 * i + j, zpack.at[r, 0], exz.at[r, 1 - i, 1 - j],
                          device(gx=beside["gx"][i], gz=beside["gz"][j]),
                          there["gx"][i] & there["gz"][j])
                    g.add("yz", 2 * i + j, zpack.at[r, 0, rows_of(i, s)], eyz.at[r, 1 - j, rows_of(1 - i, s)],
                          device(gy=beside["gy"][i], gz=beside["gz"][j]),
                          there["gy"][i] & there["gz"][j])
        return groups

    plans = [plan(r) for r in range(len(DEEP))]

    def plan_constants(L):
        g = Group(L.r_sem)
        for side in range(2):
            other = 1 - side
            x_at, x_ok = device(gx=beside["gx"][side]), there["gx"][side]
            y_at, y_ok = device(gy=beside["gy"][side]), there["gy"][side]
            g.add("x", side, L.xw.at[:, side], L.xt.at[other], x_at, x_ok)
            g.add("x", side, L.st.at[:, :, 0 if side == 0 else L.n - 1], L.xst.at[other], x_at, x_ok)
            g.add("y", side, L.st.at[:, :, :, rows_of(side, L.s)],
                  L.yst.at[:, :, :, rows_of(other, L.s)], y_at, y_ok)
            g.add("y", side, L.xw.at[:, :, rows_of(side, L.s)], L.yxw.at[:, :, rows_of(other, L.s)], y_at, y_ok)
            g.add("z", side, L.zs, L.zst.at[other], device(gz=beside["gz"][side]), there["gz"][side])
        return g

    constants = [plan_constants(L0), plan_constants(L1)]

    def begin(*groups):
        for g in groups:
            for copy, goes in g.copies:
                @pl.when(goes)
                def _():
                    copy.start()

    def arrive(*groups):
        for g in groups:
            await_all(g.sem, [g])

    def pack(L, get, planes=None):
        got = jnp.zeros(tile, jnp.float32)
        for e in every:
            for i in (range(L.n) if planes is None else planes):
                j = e * L.n + i
                got = jnp.where(zi // (2 * L.s) == j, roll(get(e, i), 2 * L.s * j + L.s, 1), got)
        return got

    def unpack(L, tile_of, e, i):
        return roll(tile_of, -(2 * L.s * (e * L.n + i) + L.s), 1)

    def combine(L, low, high, ok=None):
        s = L.s
        up = zi % (2 * s) < s
        has_low, has_high = there["gz"]
        if ok is not None:
            has_low, has_high = has_low & ok, has_high & ok
        code = jnp.where(up, jnp.where(has_high, 1, 0), jnp.where(has_low, 2, 0))
        return jnp.where(code == 1, roll(high, -s, 1), jnp.where(code == 2, roll(low, s, 1), 0.0))

    def local(L, get, e, i):
        n, s = L.n, L.s
        v = get(e, i)
        q = L.cw[e, 2, i] * roll(v, -s, 0) + L.cw[e, 3, i] * roll(v, s, 0)
        q = q + L.cw[e, 4, i] * roll(v, -s, 1) + L.cw[e, 5, i] * roll(v, s, 1)
        if i < n - 1:
            q = q + L.cw[e, 0, i] * get(e, i + 1)
        if i > 0:
            q = q + L.cw[e, 1, i] * get(e, i - 1)
        return q + L.cb[e, i]

    def border(L, q, halo, e, i):
        gx_of, gy_of, gz_of = halo
        q = q + L.st[e, 0, i] * gy_of(e, i) + L.st[e, 1, i] * gz_of(e, i)
        if i == 0:
            q = q + L.xw[e, 0] * gx_of(0, e)
        if i == L.n - 1:
            q = q + L.xw[e, 1] * gx_of(1, e)
        return q

    def received(L, r, x_ref, y_ref, z_ref):
        my = edge_rows(L.s, *there["gy"])
        c = combine(L, z_ref[r, 0], z_ref[r, 1])
        return (
            lambda side, e: jnp.where(there["gx"][side], x_ref[r, side, e], 0.0),
            lambda e, i: jnp.where(my, y_ref[r, e, i], 0.0),
            lambda e, i: unpack(L, c, e, i),
        )

    def ring(L, r, get, own):
        n, s = L.n, L.s
        my = edge_rows(s, *there["gy"])
        lines_of = []
        columns_of = []
        for side in range(2):
            ok = there["gx"][side]
            mask = edge_rows(s, ok & there["gy"][0], ok & there["gy"][1])
            lines_of.append([jnp.where(mask, exy[r, side, e], 0.0) for e in every])
            columns_of.append(combine(L, exz[r, side, 0], exz[r, side, 1], ok))
        cy = jnp.where(my, combine(L, eyz[r, 0], eyz[r, 1]), 0.0)
        rx = [
            [
                jnp.where(
                    there["gx"][side],
                    px[r, side, e] + L.xt[side, e] * get(e, 0 if side == 0 else n - 1)
                    + L.xst[side, e, 0] * lines_of[side][e]
                    + L.xst[side, e, 1] * unpack(L, columns_of[side], e, n - 1 if side == 0 else 0),
                    0.0,
                )
                for e in every
            ]
            for side in range(2)
        ]

        def ry(e, i):
            got = py[r, e, i] + L.yst[e, 0, i] * get(e, i) + L.yst[e, 1, i] * unpack(L, cy, e, i)
            if i == 0:
                got = got + L.yxw[e, 0] * lines_of[0][e]
            if i == n - 1:
                got = got + L.yxw[e, 1] * lines_of[1][e]
            return jnp.where(my, got, 0.0)

        far = 2 * s * (n - 1)
        sideways = jnp.where(
            zi // (2 * s) % n == 0, roll(columns_of[0], -far, 1), roll(columns_of[1], far, 1)
        )
        toward, along_y, along_x = [combine(L, L.zst[0, k], L.zst[1, k]) for k in range(3)]
        c = combine(L, pz[r, 0], pz[r, 1]) + toward * own + along_y * cy + along_x * sideways
        c = jnp.where(zi < 2 * s * EQ * n, c, 0.0)
        return (
            lambda side, e: rx[side][e],
            ry,
            lambda e, i: unpack(L, c, e, i),
        )

    def put(r, L, v):
        for e in every:
            for i in range(L.n):
                field[r, e, i] = v[e][i]

    def planes(f, L):
        return [[f(e, i) for i in range(L.n)] for e in every]

    def deep(r, L):
        get = lambda e, i: field[r, e, i]
        own = pack(L, get)
        zpack[r, 0] = own
        begin(plans[r]["d"], plans[r]["v"])
        for e in every:
            for i in range(L.n):
                pfield[r, e, i] = KEEP * get(e, i) + local(L, get, e, i)
        zpack[r, 1] = pack(L, lambda e, i: pfield[r, e, i])
        begin(plans[r]["p"])

        def finish():
            arrive(plans[r]["v"])
            halo = received(L, r, hx, hy, hz)
            new = planes(lambda e, i: border(L, pfield[r, e, i], halo, e, i), L)

            def outer():
                arrive(plans[r]["d"], plans[r]["p"])
                return ring(L, r, get, zpack[r, 0])

            return new, outer

        return finish

    def coarsen(a, s):
        n = a.shape[0]
        a = jnp.stack([a[2 * i] + a[2 * i + 1] for i in range(n // 2)])
        y, z = iota(a.shape, 1), iota(a.shape, 2)
        a = a + jnp.where((y // s) % 2 == 0, roll(a, -s, 1), roll(a, s, 1))
        a = a + jnp.where((z // s) % 2 == 0, roll(a, -s, 2), roll(a, s, 2))
        return a * 0.125

    source = iota((nz, nz), 0)
    target = iota((nz, nz), 1)
    squeeze = jnp.where(source == 4 * (target % qz), 1.0, 0.0).astype(jnp.float32)

    def to_rows(a):
        m = a.shape[0]
        c = jnp.dot(a.reshape(m * qx * ny, nz), squeeze, precision=HIGH,
                    preferred_element_type=jnp.float32).reshape(m, qx, ny, nz)
        shape = (m, ny, nz)
        lane = iota(shape, 2)
        got = jnp.zeros(shape, jnp.float32)
        for x in range(qx):
            for y in range(qy):
                part = roll(c[:, x], -4 * y, 1)
                got = jnp.where(lane // qz == x * qy + y, part, got)
        return got

    def own(small, whole, sem):
        return pltpu.make_async_copy(
            small.at[:, pl.ds(0, 1)], whole.at[X, core, :, pl.ds(row, 1)], sem
        )

    def stage(number, small, whole, rs):
        made = []
        if number == 0:
            for step in range(1, ngx):
                made.append((small.at[:, pl.ds(0, 1)], whole.at[X, core, :, pl.ds(row, 1)],
                             step, device(gx=(gx + step) % ngx)))
        elif number == 1:
            block = whole.at[X, core, :, pl.ds(gy * ngx, ngx)]
            for step in range(1, ngy):
                made.append((block, block, step, device(gy=(gy + step) % ngy)))
        elif number == 2:
            block = whole.at[X, core]
            for step in range(1, nX):
                made.append((block, block, step, device(gz=((X + step) % nX) * cores + core)))
        else:
            block = whole.at[:, core]
            for step in range(1, cores):
                made.append((block, block, step, device(gz=X * cores + (core + step) % cores)))
        return [
            remote(a, z, ws_sem.at[number], rs.at[number], where)
            for a, z, _, where in made
        ]

    wargs = (wsend, wall, wr_sem)

    def everyone():
        made = []
        for az in range(ngz):
            for ay in range(ngy):
                for ax in range(ngx):
                    if ax + ay + az == 0:
                        continue
                    made.append(remote(
                        bsend.at[:, pl.ds(0, 1)], ball.at[X, core, :, pl.ds(row, 1)],
                        bs_sem, br_sem,
                        ((gx + ax) % ngx, (gy + ay) % ngy, (gz + az) % ngz),
                    ))
        return made

    def start(number):
        for copy in stage(number, *wargs):
            copy.start()

    def stage_rows(number):
        return 7 * EQ * (
            ngx - 1, ngx * (ngy - 1), rows * (nX - 1), nX * rows * (cores - 1)
        )[number]

    def done(number):
        await_rows(wr_sem.at[number], stage_rows(number))

    def scale(L, get_w, get_d, e, i):
        n, s = L.n, L.s
        raw = [get_w(e, k, i) for k in range(6)]
        total = get_d(e, i)
        for k in range(6):
            total = total + raw[k]
        c = DAMP / total
        w = [c * raw[k] for k in range(6)]
        L.tot[e, i] = (1.0 / DAMP) * total
        last_y, first_y, last_z, first_z = yi >= ny - s, yi < s, zi >= nz - s, zi < s
        L.cw[e, 0, i] = w[0]
        L.cw[e, 1, i] = w[1]
        L.cw[e, 2, i] = jnp.where(last_y, 0.0, w[2])
        L.cw[e, 3, i] = jnp.where(first_y, 0.0, w[3])
        L.cw[e, 4, i] = jnp.where(last_z, 0.0, w[4])
        L.cw[e, 5, i] = jnp.where(first_z, 0.0, w[5])
        L.st[e, 0, i] = jnp.where(last_y, w[2], jnp.where(first_y, w[3], 0.0))
        L.st[e, 1, i] = jnp.where(last_z, w[4], jnp.where(first_z, w[5], 0.0))
        if i == 0:
            L.xw[e, 0] = w[1]
        if i == n - 1:
            L.xw[e, 1] = w[0]
        return c

    def pack_constants(L):
        L.zs[0] = pack(L, lambda e, i: L.st[e, 1, i])
        L.zs[1] = pack(L, lambda e, i: L.st[e, 0, i])
        L.zs[2] = pack(L, lambda e, i: L.xw[e, 0 if i == 0 else 1], (0, L.n - 1))

    loads[0].wait()
    guess = lambda e, i: g_ref[e, i]
    zpack[0, 0] = pack(L0, guess)
    pl.semaphore_wait(barrier, awaited)
    begin(plans[0]["v"])
    hear = there["gy"][0].astype(jnp.int32) + there["gy"][1].astype(jnp.int32)

    def tell(k):
        for side in range(2):
            @pl.when(there["gy"][side])
            def _():
                pl.semaphore_signal(
                    know.at[k], inc=1, device_id=device(gy=beside["gy"][side]), device_id_type=MESH
                )

    if close:
        tell(0)
    for load in loads[1:]:
        load.wait()
    for e in every:
        for i in range(nx):
            c = scale(L0, lambda e, k, i: w_ref[6 * e + k, i], lambda e, i: d_ref[e, i], e, i)
            L0.cb[e, i] = c * b_ref[e, i]
    pack_constants(L0)
    begin(constants[0])
    if close:
        pl.semaphore_wait(know.at[0], hear)
        tell(1)
    for e in every:
        for i in range(nx):
            pfield[0, e, i] = KEEP * guess(e, i) + local(L0, guess, e, i)
    for e in every:
        d1 = coarsen(d_ref[e], 1)
        wsend[6 * EQ + e] = to_rows(coarsen(d1, 2)[None])[0]
        for k in range(6):
            w = 0.25 * coarsen(w_ref[6 * e + k], 1)
            w1[6 * e + k] = w
            wsend[6 * e + k] = to_rows((0.25 * coarsen(w, 2))[None])[0]
        for i in range(half):
            c = scale(L1, lambda e, k, i: w1[6 * e + k, i], lambda e, i: d1[i], e, i)
            w1[6 * EQ + e, i] = c
    own(wsend, wall, l_sem).start()
    start(0)
    pack_constants(L1)
    begin(constants[1])

    arrive(plans[0]["v"])
    halo = received(L0, 0, hx, hy, hz)
    put(1, L0, planes(lambda e, i: border(L0, pfield[0, e, i], halo, e, i), L0))
    finish = deep(1, L0)
    own(wsend, wall, l_sem).wait()
    done(0)
    if close:
        pl.semaphore_wait(know.at[1], hear)
    start(1)
    arrive(constants[0])
    v, outer = finish()
    kept0 = field.at[0]
    for e in every:
        for i in range(nx):
            kept0[e, i] = v[e][i]
    get = lambda e, i: kept0[e, i]
    q = planes(lambda e, i: local(L0, get, e, i), L0)
    halo = outer()
    first = []
    for e in every:
        r = jnp.stack([
            L0.tot[e, i] * (border(L0, q[e][i], halo, e, i) - DAMP * get(e, i)) for i in range(nx)
        ])
        b = coarsen(r, 1)
        first.append([])
        for i in range(half):
            u = w1[6 * EQ + e, i] * b[i]
            L1.cb[e, i] = u
            first[e].append(u)
    put(2, L1, first)
    finish = deep(2, L1)
    done(1)
    start(2)
    arrive(constants[1])
    u, outer = finish()
    kept1 = pfield.at[3]
    for e in every:
        for i in range(half):
            kept1[e, i] = u[e][i]
    get = lambda e, i: kept1[e, i]
    q = planes(lambda e, i: local(L1, get, e, i), L1)
    halo = outer()
    rest = []
    for e in every:
        r = jnp.stack([
            L1.tot[e, i] * (border(L1, q[e][i], halo, e, i) - DAMP * get(e, i)) for i in range(half)
        ])
        rest.append(coarsen(r, 2))
    bsend[...] = to_rows(jnp.stack(rest))
    for copy in reversed(everyone()):
        copy.start()
    own(bsend, ball, br_sem).start()
    done(2)
    start(3)
    done(3)

    shape = (ngz, rows, nz)
    r_i, l_i = iota(shape, 1), iota(shape, 2)
    g_i = iota(shape, 0)
    zc, yc, xc = l_i % qz, (l_i // qz) % qy, l_i // (qz * qy)
    gyi, gxi = r_i // ngx, r_i % ngx
    inside = [
        ~((xc == qx - 1) & (gxi == ngx - 1)), ~((xc == 0) & (gxi == 0)),
        ~((yc == qy - 1) & (gyi == ngy - 1)), ~((yc == 0) & (gyi == 0)),
        ~((zc == qz - 1) & (g_i == ngz - 1)), ~((zc == 0) & (g_i == 0)),
    ]

    def whole(ref, index):
        return ref[:, :, index].reshape(shape)

    def next_of(v):
        return jnp.concatenate([v[1:], v[:1]], axis=0)

    def prev_of(v):
        return jnp.concatenate([v[-1:], v[:-1]], axis=0)

    def near2(v):
        sy, sx = qz, qz * qy
        return [
            jnp.where(xc == qx - 1, roll(roll(v, (qx - 1) * sx, 2), -1, 1), roll(v, -sx, 2)),
            jnp.where(xc == 0, roll(roll(v, -(qx - 1) * sx, 2), 1, 1), roll(v, sx, 2)),
            jnp.where(yc == qy - 1, roll(roll(v, (qy - 1) * sy, 2), -ngx, 1), roll(v, -sy, 2)),
            jnp.where(yc == 0, roll(roll(v, -(qy - 1) * sy, 2), ngx, 1), roll(v, sy, 2)),
            jnp.where(zc == qz - 1, roll(next_of(v), qz - 1, 2), roll(v, -1, 2)),
            jnp.where(zc == 0, roll(prev_of(v), -(qz - 1), 2), roll(v, 1, 2)),
        ]

    def dot_near(weights, near):
        total = weights[0] * near[0]
        for k in range(1, 6):
            total = total + weights[k] * near[k]
        return total

    def pair(a):
        sy, sx = qz, qz * qy
        a = a + jnp.where(xc % 2 == 0, roll(a, -sx, 2), roll(a, sx, 2))
        a = a + jnp.where(yc % 2 == 0, roll(a, -sy, 2), roll(a, sy, 2))
        a = a + jnp.where(zc % 2 == 0, roll(a, -1, 2), roll(a, 1, 2))
        return a * 0.125

    groups = qx * qy
    tiles = ngz // groups
    shape3 = (tiles, rows, nz)
    r3, l3, t3 = iota(shape3, 1), iota(shape3, 2), iota(shape3, 0)
    inside3 = [
        r3 % ngx < ngx - 1, r3 % ngx > 0, r3 // ngx < ngy - 1, r3 // ngx > 0,
        ~((l3 >= nz - 2) & (t3 == tiles - 1)), ~((l3 < 2) & (t3 == 0)),
    ]

    def join(a):
        a = a.reshape(tiles, groups, rows, nz)
        got = a[:, 0]
        for j in range(1, groups):
            got = jnp.where(l3 // qz == j, a[:, j], got)
        return got

    def part(a):
        parts = []
        for j in range(groups):
            mine = jnp.where(l3 // qz == j, a, 0.0)
            size = qz
            while size < nz:
                mine = mine + roll(mine, size, 2)
                size *= 2
            parts.append(mine)
        return jnp.stack(parts, axis=1).reshape(shape)

    def near3(v):
        if tiles == 1:
            up, down = roll(v, -2, 2), roll(v, 2, 2)
        else:
            up = jnp.where(l3 >= nz - 2, roll(next_of(v), -2, 2), roll(v, -2, 2))
            down = jnp.where(l3 < 2, roll(prev_of(v), 2, 2), roll(v, 2, 2))
        return [roll(v, -1, 1), roll(v, 1, 1), roll(v, -ngx, 1), roll(v, ngx, 1), up, down]

    w2, t2, w3, t3s = [], [], [], []
    for e in range(EQ):
        plain = [whole(wall, 6 * e + k) for k in range(6)]
        d2 = whole(wall, 6 * EQ + e)
        total = d2
        for k in range(6):
            total = total + plain[k]
        t2.append(total)
        w2.append([jnp.where(inside[k], plain[k], 0.0) for k in range(6)])
        plain3 = [0.25 * join(pair(plain[k])) for k in range(6)]
        total = join(pair(d2))
        for k in range(6):
            total = total + plain3[k]
        t3s.append(total)
        w3.append([jnp.where(inside3[k], plain3[k], 0.0) for k in range(6)])
    c2 = [DAMP / t for t in t2]
    c3 = [DAMP / t for t in t3s]

    pltpu.make_async_copy(ball, ball, br_sem).wait()

    rhs = [whole(ball, e) for e in every]

    def smooth2(v):
        return [KEEP * v[e] + c2[e] * (rhs[e] + dot_near(w2[e], near2(v[e]))) for e in every]

    v2 = [c2[e] * rhs[e] for e in every]
    for step in range(SWEEPS - 1):
        v2 = smooth2(v2)
    rest = [rhs[e] - t2[e] * v2[e] + dot_near(w2[e], near2(v2[e])) for e in every]
    rhs3 = [join(pair(rest[e])) for e in every]
    v3 = [c3[e] * rhs3[e] for e in every]
    for step in range(COARSE_SWEEPS - 1):
        v3 = [KEEP * v3[e] + c3[e] * (rhs3[e] + dot_near(w3[e], near3(v3[e]))) for e in every]
    v2 = [v2[e] + part(v3[e]) for e in every]
    for step in range(SWEEPS):
        v2 = smooth2(v2)
    for e in every:
        e2[e] = v2[e]

    wide = groups * nz
    source = iota((nz, wide), 0)
    target = iota((nz, wide), 1)
    widen = jnp.where(source == (target // nz) * qz + (target % nz) // 4, 1.0, 0.0).astype(jnp.float32)
    around = [(gx, gy, gz, None)]
    for axis, index, count in ((0, gx, ngx), (1, gy, ngy), (2, gz, ngz)):
        for step in (-1, 1):
            at = [gx, gy, gz]
            at[axis] = jnp.clip(index + step, 0, count - 1)
            has = index > 0 if step < 0 else index < count - 1
            around.append((at[0], at[1], at[2], has))
    for e in range(EQ):
        for j, (ax, ay, az, has) in enumerate(around):
            line = e2[e, az, pl.ds(ay * ngx + ax, 1), :]
            if has is not None:
                line = jnp.where(has, line, 0.0)
            lines[e * 7 + j : e * 7 + j + 1, :] = line
    for j in range(EQ * 7, lines.shape[0]):
        lines[j : j + 1, :] = jnp.zeros((1, nz), jnp.float32)
    back = jnp.dot(lines[...], widen, precision=HIGH, preferred_element_type=jnp.float32)
    ysel = iota((ny, nz), 0) // 4

    def strip(e, j, x, y):
        col = (x * qy + y) * nz
        return jnp.broadcast_to(back[e * 7 + j : e * 7 + j + 1, col : col + nz], (ny, nz))

    def plane(e, j, x):
        got = strip(e, j, x, 0)
        for y in range(1, qy):
            got = jnp.where(ysel == y, strip(e, j, x, y), got)
        return got

    left, behind, through = halo

    def add_x(side, e):
        return left(side, e) + plane(e, 1 + side, qx - 1 if side == 0 else 0)

    def add_y(e, i):
        x = i // 2
        return behind(e, i) + jnp.where(
            ysel < qy // 2, strip(e, 3, x, qy - 1), strip(e, 4, x, 0)
        )

    def add_z(e, i):
        x = i // 2
        return through(e, i) + jnp.where(
            zi < nz // 2, roll(plane(e, 5, x), 2, 1), roll(plane(e, 6, x), -2, 1)
        )

    corrected = planes(lambda e, i: kept1[e, i] + plane(e, 0, i // 2), L1)
    get = lambda e, i: corrected[e][i]
    put(3, L1, planes(
        lambda e, i: KEEP * get(e, i) + border(L1, local(L1, get, e, i), (add_x, add_y, add_z), e, i), L1
    ))
    get = lambda e, i: field[3, e, i]
    zpack[3, 0] = pack(L1, get)
    begin(plans[3]["v"])
    q = planes(lambda e, i: KEEP * get(e, i) + local(L1, get, e, i), L1)
    arrive(plans[3]["v"])
    halo = received(L1, 3, hx, hy, hz)
    u = planes(lambda e, i: border(L1, q[e][i], halo, e, i), L1)
    put(4, L0, planes(lambda e, i: kept0[e, i] + u[e][i // 2], L0))
    finish = deep(4, L0)
    v, outer = finish()
    last = pfield.at[0]
    for e in every:
        for i in range(nx):
            last[e, i] = v[e][i]
    get = lambda e, i: last[e, i]
    q = planes(lambda e, i: KEEP * get(e, i) + local(L0, get, e, i), L0)
    halo = outer()
    for e in every:
        for i in range(nx):
            out_ref[e, i] = border(L0, q[e][i], halo, e, i)
    await_all(s_sem, [g for p in plans for g in p.values()] + constants)
    for number in range(4):
        await_rows(ws_sem.at[number], stage_rows(number))
    await_rows(bs_sem, EQ * (rows * ngz - 1))


def per_device(dims, cores, couplings, diagonal, right_side, guess):
    ngx, ngy, ngz = dims
    brick = guess.shape[1:]
    nx, ny, nz = brick
    half = nx // 2
    rows = ngx * ngy
    nX = ngz // cores
    rounds = len(DEEP)
    f32 = jnp.float32
    vmem = pltpu.VMEM
    dma = pltpu.SemaphoreType.DMA

    def level(n):
        return [
            vmem((EQ, 6, n, ny, nz), f32),
            vmem((EQ, 2, n, ny, nz), f32),
            vmem((EQ, 2, ny, nz), f32),
            vmem((EQ, n, ny, nz), f32),
            vmem((EQ, n, ny, nz), f32),
            vmem((3, ny, nz), f32),
            vmem((2, EQ, ny, nz), f32),
            vmem((2, EQ, 2, ny, nz), f32),
            vmem((EQ, 2, n, ny, nz), f32),
            vmem((EQ, 2, ny, nz), f32),
            vmem((2, 3, ny, nz), f32),
            dma,
        ]

    faces = [
        vmem((rounds, 2, EQ, ny, nz), f32),
        vmem((rounds, EQ) + brick, f32),
        vmem((rounds, 2, ny, nz), f32),
    ]
    return pl.pallas_call(
        functools.partial(kernel, dims, cores),
        out_shape=vmem(guess.shape, f32),
        in_specs=[pl.BlockSpec(memory_space=pl.ANY)] * 4,
        out_specs=pl.BlockSpec(memory_space=vmem),
        scratch_shapes=[
            vmem(couplings.shape, f32),
            vmem(diagonal.shape, f32),
            vmem(right_side.shape, f32),
            vmem(guess.shape, f32),
            vmem((max(2048, nX * rows * 7 * EQ * (cores - 1) // 8, rows * (nX - 1) * 7 * EQ // 8), 8, nz), f32),
            vmem((rounds, EQ) + brick, f32),
            vmem((rounds, EQ) + brick, f32),
            vmem((rounds, 2, ny, nz), f32),
            *faces,
            *faces,
            vmem((rounds, 2, EQ, ny, nz), f32),
            vmem((rounds, 2, 2, ny, nz), f32),
            vmem((rounds, 2, ny, nz), f32),
            vmem((7 * EQ, half, ny, nz), f32),
            *level(nx),
            *level(half),
            vmem((7 * EQ, ny, nz), f32),
            vmem((nX, cores, 7 * EQ, rows, nz), f32),
            vmem((EQ, ny, nz), f32),
            vmem((nX, cores, EQ, rows, nz), f32),
            vmem((EQ, ngz, rows, nz), f32),
            vmem((-(-EQ * 7 // 8) * 8, nz), f32),
            dma,
            dma((rounds, 3)),
            dma((4,)),
            dma((4,)),
            dma,
            dma,
            dma,
            dma((4,)),
            pltpu.SemaphoreType.REGULAR((2,)),
        ],
        compiler_params=pltpu.CompilerParams(
            collective_id=0, has_side_effects=True, vmem_limit_bytes=60 * 1024 * 1024
        ),
    )(couplings, diagonal, right_side, guess)


def solution(mesh):
    dims = (mesh.shape["gx"], mesh.shape["gy"], mesh.shape["gz"])
    cores = 2 if dims[2] % 2 == 0 else 1
    spec = P(None, "gx", "gy", "gz")
    return jax.shard_map(
        functools.partial(per_device, dims, cores),
        mesh=mesh,
        in_specs=(spec,) * 4,
        out_specs=spec,
        check_vma=False,
    )
```

```python
import functools

import jax
import jax.numpy as jnp
from jax import lax
from jax.experimental import pallas as pl
from jax.experimental.pallas import tpu as pltpu
from jax.sharding import PartitionSpec as P

SWEEPS = 2
COARSE_SWEEPS = 8
DAMP = 0.8
KEEP = 1.0 - DAMP
EQ = 3
MESH = pl.DeviceIdType.MESH
HIGH = lax.Precision.HIGHEST
DEEP = (False, True, True, False, True)
FINE = (True, True, False, False, True)


def roll(value, shift, axis):
    size = value.shape[axis]
    shift = shift % size
    return value if shift == 0 else pltpu.roll(value, shift, axis)


def iota(shape, axis):
    return lax.broadcasted_iota(jnp.int32, shape, axis)


class Level:
    def __init__(self, n, s, refs):
        self.n, self.s = n, s
        (self.cw, self.st, self.xw, self.cb, self.tot, self.zs,
         self.xt, self.xst, self.yst, self.yxw, self.zst, self.r_sem) = refs


def kernel(
    dims, cores, w_hbm, d_hbm, b_hbm, g_hbm, out_ref,
    w_ref, d_ref, b_ref, g_ref,
    tally, field, pfield, zpack, hx, hy, hz, px, py, pz, exy, exz, eyz, w1, co, cos, cox, coy, coz, zco, *rest,
):
    level_refs = (rest[:12], rest[12:24])
    (wsend, wall, bsend, ball, e2, lines, broad, beyond, outside,
     s_sem, r_sem, co_sem, ws_sem, wr_sem, bs_sem, br_sem, l_sem, i_sem, know) = rest[24:]
    ngx, ngy, ngz = dims
    nx, ny, nz = g_ref.shape[1:]
    half = nx // 2
    qx, qy, qz = nx // 4, ny // 4, nz // 4
    rows = ngx * ngy
    nX = ngz // cores
    gx, gy, gz = lax.axis_index("gx"), lax.axis_index("gy"), lax.axis_index("gz")
    X, core = gz // cores, gz % cores
    row = gy * ngx + gx
    axes = (("gx", gx, ngx), ("gy", gy, ngy), ("gz", gz, ngz))
    L0 = Level(nx, 1, level_refs[0])
    L1 = Level(half, 2, level_refs[1])
    tile = (ny, nz)
    yi, zi = iota(tile, 0), iota(tile, 1)
    every = range(EQ)

    def device(**change):
        here = {"gx": gx, "gy": gy, "gz": gz}
        here.update(change)
        return (here["gx"], here["gy"], here["gz"])

    barrier = pltpu.get_barrier_semaphore()
    close = ngy <= 4 and ngz <= 4
    awaited = 0

    def greet(ok, where):
        @pl.when(ok)
        def _():
            pl.semaphore_signal(barrier, inc=1, device_id=where, device_id_type=MESH)
        return ok.astype(jnp.int32)

    for name, index, count in axes:
        if close and name != "gx":
            steps = (-1, 1) if name == "gy" or cores == 1 else (-1, 1, -cores, cores)
            for step in steps:
                ok = (index + step >= 0) & (index + step < count)
                awaited = awaited + greet(ok, device(**{name: jnp.clip(index + step, 0, count - 1)}))
        else:
            for step in range(1, count):
                pl.semaphore_signal(
                    barrier, inc=1, device_id=device(**{name: (index + step) % count}),
                    device_id_type=MESH,
                )
            awaited = awaited + (count - 1)

    loads = [
        pltpu.make_async_copy(a, z, i_sem.at[slot])
        for slot, (a, z) in enumerate(
            ((g_hbm, g_ref), (w_hbm, w_ref), (d_hbm, d_ref), (b_hbm, b_ref))
        )
    ]
    for load in loads:
        load.start()

    there = {
        name: (index > 0, index < count - 1) for name, index, count in axes
    }
    beside = {
        name: (jnp.maximum(index - 1, 0), jnp.minimum(index + 1, count - 1))
        for name, index, count in axes
    }

    def edge_rows(s, lo, hi):
        return (yi < jnp.where(lo, s, 0)) | (yi >= jnp.where(hi, ny - s, ny))

    def remote(a, z, ss, rs, where):
        return pltpu.make_async_remote_copy(
            src_ref=a, dst_ref=z, send_sem=ss, recv_sem=rs,
            device_id=where, device_id_type=MESH,
        )

    def rows_of(side, s):
        return pl.ds(0 if side == 0 else ny - s, s)

    counts = [
        [k for k in (0, 1, 2) if (k > 0 or count == 1) and k < count and (k == 2 or count <= 2 or k == 1)]
        for _, _, count in axes
    ]
    found = [
        there[name][0].astype(jnp.int32) + there[name][1].astype(jnp.int32) for name, _, _ in axes
    ]
    cases = []
    for cx in counts[0]:
        for cy in counts[1]:
            for cz in counts[2]:
                cases.append(((cx, cy, cz), (found[0] == cx) & (found[1] == cy) & (found[2] == cz)))

    def await_rows(sem, number):
        if number > 0:
            part = next(k for k in (8, 4, 2, 1) if number % k == 0)
            ref = tally.at[pl.ds(0, number // part), pl.ds(0, part)]
            pltpu.make_async_copy(ref, ref, sem).wait()

    def await_all(sem, groups):
        for (cx, cy, cz), ok in cases:
            many = {"x": cx, "y": cy, "z": cz, "xy": cx * cy, "xz": cx * cz, "yz": cy * cz}
            number = sum(many[kind] * size for g in groups for kind, size in g.sizes.items())
            if len(cases) == 1:
                await_rows(sem, number)
            else:
                @pl.when(ok)
                def _():
                    await_rows(sem, number)

    class Group:
        def __init__(self, sem):
            self.sem, self.copies, self.sizes = sem, [], {}

        def add(self, kind, side, a, z, where, goes):
            self.copies.append((remote(a, z, s_sem, self.sem, where), goes))
            if side == 0:
                size = 1
                for d in z.shape[:-1]:
                    size *= d
                self.sizes[kind] = self.sizes.get(kind, 0) + size

    def plan(r):
        n, s = (nx, 1) if FINE[r] else (half, 2)
        src = g_ref if r == 0 else field.at[r]
        groups = {k: Group(r_sem.at[r, "vdp".index(k)]) for k in "vdp"}
        kinds = [("v", src, 0, hx, hy, hz)]
        if DEEP[r]:
            kinds.append(("p", pfield.at[r], 1, px, py, pz))
        for side in range(2):
            other = 1 - side
            for group, a, which, zx, zy, zz in kinds:
                g = groups[group]
                g.add("x", side, a.at[:, 0 if side == 0 else n - 1], zx.at[r, other],
                      device(gx=beside["gx"][side]), there["gx"][side])
                g.add("y", side, a.at[:, 0:n, rows_of(side, s)], zy.at[r, :, 0:n, rows_of(other, s)],
                      device(gy=beside["gy"][side]), there["gy"][side])
                g.add("z", side, zpack.at[r, which], zz.at[r, other],
                      device(gz=beside["gz"][side]), there["gz"][side])
        if DEEP[r]:
            g = groups["d"]
            for i in range(2):
                for j in range(2):
                    g.add("xy", 2 * i + j, src.at[:, 0 if i == 0 else n - 1, rows_of(j, s)],
                          exy.at[r, 1 - i, :, rows_of(1 - j, s)],
                          device(gx=beside["gx"][i], gy=beside["gy"][j]),
                          there["gx"][i] & there["gy"][j])
                    g.add("xz", 2 * i + j, zpack.at[r, 0], exz.at[r, 1 - i, 1 - j],
                          device(gx=beside["gx"][i], gz=beside["gz"][j]),
                          there["gx"][i] & there["gz"][j])
                    g.add("yz", 2 * i + j, zpack.at[r, 0, rows_of(i, s)], eyz.at[r, 1 - j, rows_of(1 - i, s)],
                          device(gy=beside["gy"][i], gz=beside["gz"][j]),
                          there["gy"][i] & there["gz"][j])
        return groups

    plans = [plan(r) for r in range(len(DEEP))]

    def plan_constants(L):
        g = Group(L.r_sem)
        for side in range(2):
            other = 1 - side
            x_at, x_ok = device(gx=beside["gx"][side]), there["gx"][side]
            y_at, y_ok = device(gy=beside["gy"][side]), there["gy"][side]
            g.add("x", side, L.xw.at[:, side], L.xt.at[other], x_at, x_ok)
            g.add("x", side, L.st.at[:, :, 0 if side == 0 else L.n - 1], L.xst.at[other], x_at, x_ok)
            g.add("y", side, L.st.at[:, :, :, rows_of(side, L.s)],
                  L.yst.at[:, :, :, rows_of(other, L.s)], y_at, y_ok)
            g.add("y", side, L.xw.at[:, :, rows_of(side, L.s)], L.yxw.at[:, :, rows_of(other, L.s)], y_at, y_ok)
            g.add("z", side, L.zs, L.zst.at[other], device(gz=beside["gz"][side]), there["gz"][side])
        return g

    def plan_spreads():
        g = Group(co_sem)
        s = L1.s
        for side in range(2):
            other = 1 - side
            g.add("x", side, co.at[:, :, 0 if side == 0 else half - 1], cox.at[other],
                  device(gx=beside["gx"][side]), there["gx"][side])
            g.add("y", side, co.at[:, :, :, rows_of(side, s)], coy.at[:, :, :, rows_of(other, s)],
                  device(gy=beside["gy"][side]), there["gy"][side])
            g.add("z", side, cos, coz.at[other], device(gz=beside["gz"][side]), there["gz"][side])
        return g

    spreads = plan_spreads()
    constants = [plan_constants(L0), plan_constants(L1)]

    def begin(*groups):
        for g in groups:
            for copy, goes in g.copies:
                @pl.when(goes)
                def _():
                    copy.start()

    def arrive(*groups):
        for g in groups:
            await_all(g.sem, [g])

    def pack(L, get, planes=None):
        got = jnp.zeros(tile, jnp.float32)
        for e in every:
            for i in (range(L.n) if planes is None else planes):
                j = e * L.n + i
                got = jnp.where(zi // (2 * L.s) == j, roll(get(e, i), 2 * L.s * j + L.s, 1), got)
        return got

    def unpack(L, tile_of, e, i):
        return roll(tile_of, -(2 * L.s * (e * L.n + i) + L.s), 1)

    def combine(L, low, high, ok=None):
        s = L.s
        up = zi % (2 * s) < s
        has_low, has_high = there["gz"]
        if ok is not None:
            has_low, has_high = has_low & ok, has_high & ok
        code = jnp.where(up, jnp.where(has_high, 1, 0), jnp.where(has_low, 2, 0))
        return jnp.where(code == 1, roll(high, -s, 1), jnp.where(code == 2, roll(low, s, 1), 0.0))

    def local(L, get, e, i):
        n, s = L.n, L.s
        v = get(e, i)
        q = L.cw[e, 2, i] * roll(v, -s, 0) + L.cw[e, 3, i] * roll(v, s, 0)
        q = q + L.cw[e, 4, i] * roll(v, -s, 1) + L.cw[e, 5, i] * roll(v, s, 1)
        if i < n - 1:
            q = q + L.cw[e, 0, i] * get(e, i + 1)
        if i > 0:
            q = q + L.cw[e, 1, i] * get(e, i - 1)
        return q + L.cb[e, i]

    def border(L, q, halo, e, i):
        gx_of, gy_of, gz_of = halo
        q = q + L.st[e, 0, i] * gy_of(e, i) + L.st[e, 1, i] * gz_of(e, i)
        if i == 0:
            q = q + L.xw[e, 0] * gx_of(0, e)
        if i == L.n - 1:
            q = q + L.xw[e, 1] * gx_of(1, e)
        return q

    def received(L, r, x_ref, y_ref, z_ref):
        my = edge_rows(L.s, *there["gy"])
        c = combine(L, z_ref[r, 0], z_ref[r, 1])
        return (
            lambda side, e: jnp.where(there["gx"][side], x_ref[r, side, e], 0.0),
            lambda e, i: jnp.where(my, y_ref[r, e, i], 0.0),
            lambda e, i: unpack(L, c, e, i),
        )

    def ring(L, r, get, own):
        n, s = L.n, L.s
        my = edge_rows(s, *there["gy"])
        lines_of = []
        columns_of = []
        for side in range(2):
            ok = there["gx"][side]
            mask = edge_rows(s, ok & there["gy"][0], ok & there["gy"][1])
            lines_of.append([jnp.where(mask, exy[r, side, e], 0.0) for e in every])
            columns_of.append(combine(L, exz[r, side, 0], exz[r, side, 1], ok))
        cy = jnp.where(my, combine(L, eyz[r, 0], eyz[r, 1]), 0.0)
        rx = [
            [
                jnp.where(
                    there["gx"][side],
                    px[r, side, e] + L.xt[side, e] * get(e, 0 if side == 0 else n - 1)
                    + L.xst[side, e, 0] * lines_of[side][e]
                    + L.xst[side, e, 1] * unpack(L, columns_of[side], e, n - 1 if side == 0 else 0),
                    0.0,
                )
                for e in every
            ]
            for side in range(2)
        ]

        def ry(e, i):
            got = py[r, e, i] + L.yst[e, 0, i] * get(e, i) + L.yst[e, 1, i] * unpack(L, cy, e, i)
            if i == 0:
                got = got + L.yxw[e, 0] * lines_of[0][e]
            if i == n - 1:
                got = got + L.yxw[e, 1] * lines_of[1][e]
            return jnp.where(my, got, 0.0)

        far = 2 * s * (n - 1)
        sideways = jnp.where(
            zi // (2 * s) % n == 0, roll(columns_of[0], -far, 1), roll(columns_of[1], far, 1)
        )
        toward, along_y, along_x = [combine(L, L.zst[0, k], L.zst[1, k]) for k in range(3)]
        c = combine(L, pz[r, 0], pz[r, 1]) + toward * own + along_y * cy + along_x * sideways
        c = jnp.where(zi < 2 * s * EQ * n, c, 0.0)
        return (
            lambda side, e: rx[side][e],
            ry,
            lambda e, i: unpack(L, c, e, i),
        )

    def put(r, L, v):
        for e in every:
            for i in range(L.n):
                field[r, e, i] = v[e][i]

    def planes(f, L):
        return [[f(e, i) for i in range(L.n)] for e in every]

    def deep(r, L):
        get = lambda e, i: field[r, e, i]
        own = pack(L, get)
        zpack[r, 0] = own
        begin(plans[r]["d"], plans[r]["v"])
        for e in every:
            for i in range(L.n):
                pfield[r, e, i] = KEEP * get(e, i) + local(L, get, e, i)
        zpack[r, 1] = pack(L, lambda e, i: pfield[r, e, i])
        begin(plans[r]["p"])

        def finish():
            arrive(plans[r]["v"])
            halo = received(L, r, hx, hy, hz)
            new = planes(lambda e, i: border(L, pfield[r, e, i], halo, e, i), L)

            def outer():
                arrive(plans[r]["d"], plans[r]["p"])
                return ring(L, r, get, zpack[r, 0])

            return new, outer

        return finish

    def coarsen(a, s):
        n = a.shape[0]
        a = jnp.stack([a[2 * i] + a[2 * i + 1] for i in range(n // 2)])
        y, z = iota(a.shape, 1), iota(a.shape, 2)
        a = a + jnp.where((y // s) % 2 == 0, roll(a, -s, 1), roll(a, s, 1))
        a = a + jnp.where((z // s) % 2 == 0, roll(a, -s, 2), roll(a, s, 2))
        return a * 0.125

    source = iota((nz, nz), 0)
    target = iota((nz, nz), 1)
    squeeze = jnp.where(source == 4 * (target % qz), 1.0, 0.0).astype(jnp.float32)

    def to_rows(a):
        m = a.shape[0]
        c = jnp.dot(a.reshape(m * qx * ny, nz), squeeze, precision=HIGH,
                    preferred_element_type=jnp.float32).reshape(m, qx, ny, nz)
        shape = (m, ny, nz)
        lane = iota(shape, 2)
        got = jnp.zeros(shape, jnp.float32)
        for x in range(qx):
            for y in range(qy):
                part = roll(c[:, x], -4 * y, 1)
                got = jnp.where(lane // qz == x * qy + y, part, got)
        return got

    def own(small, whole, sem):
        return pltpu.make_async_copy(
            small.at[:, pl.ds(0, 1)], whole.at[X, core, :, pl.ds(row, 1)], sem
        )

    def stage(number, small, whole, rs):
        made = []
        if number == 0:
            for step in range(1, ngx):
                made.append((small.at[:, pl.ds(0, 1)], whole.at[X, core, :, pl.ds(row, 1)],
                             step, device(gx=(gx + step) % ngx)))
        elif number == 1:
            block = whole.at[X, core, :, pl.ds(gy * ngx, ngx)]
            for step in range(1, ngy):
                made.append((block, block, step, device(gy=(gy + step) % ngy)))
        elif number == 2:
            block = whole.at[X, core]
            for step in range(1, nX):
                made.append((block, block, step, device(gz=((X + step) % nX) * cores + core)))
        else:
            block = whole.at[:, core]
            for step in range(1, cores):
                made.append((block, block, step, device(gz=X * cores + (core + step) % cores)))
        return [
            remote(a, z, ws_sem.at[number], rs.at[number], where)
            for a, z, _, where in made
        ]

    wargs = (wsend, wall, wr_sem)

    def everyone():
        made = []
        for az in range(ngz):
            for ay in range(ngy):
                for ax in range(ngx):
                    if ax + ay + az == 0:
                        continue
                    made.append(remote(
                        bsend.at[:, pl.ds(0, 1)], ball.at[X, core, :, pl.ds(row, 1)],
                        bs_sem, br_sem,
                        ((gx + ax) % ngx, (gy + ay) % ngy, (gz + az) % ngz),
                    ))
        return made

    def start(number):
        for copy in stage(number, *wargs):
            copy.start()

    def stage_rows(number):
        return 7 * EQ * (
            ngx - 1, ngx * (ngy - 1), rows * (nX - 1), nX * rows * (cores - 1)
        )[number]

    def done(number):
        await_rows(wr_sem.at[number], stage_rows(number))

    def scale(L, get_w, get_d, e, i):
        n, s = L.n, L.s
        raw = [get_w(e, k, i) for k in range(6)]
        total = get_d(e, i)
        for k in range(6):
            total = total + raw[k]
        c = DAMP / total
        w = [c * raw[k] for k in range(6)]
        L.tot[e, i] = (1.0 / DAMP) * total
        last_y, first_y, last_z, first_z = yi >= ny - s, yi < s, zi >= nz - s, zi < s
        L.cw[e, 0, i] = w[0]
        L.cw[e, 1, i] = w[1]
        L.cw[e, 2, i] = jnp.where(last_y, 0.0, w[2])
        L.cw[e, 3, i] = jnp.where(first_y, 0.0, w[3])
        L.cw[e, 4, i] = jnp.where(last_z, 0.0, w[4])
        L.cw[e, 5, i] = jnp.where(first_z, 0.0, w[5])
        L.st[e, 0, i] = jnp.where(last_y, w[2], jnp.where(first_y, w[3], 0.0))
        L.st[e, 1, i] = jnp.where(last_z, w[4], jnp.where(first_z, w[5], 0.0))
        if i == 0:
            L.xw[e, 0] = w[1]
        if i == n - 1:
            L.xw[e, 1] = w[0]
        if L is L1:
            odd_y, odd_z = yi // s % 2 == 1, zi // s % 2 == 1
            co[e, 1, i] = w[0] if i % 2 == 1 else w[1]
            co[e, 2, i] = jnp.where(odd_y, w[2], w[3])
            co[e, 3, i] = jnp.where(odd_z, w[4], w[5])
            co[e, 0, i] = (
                KEEP + (w[1] if i % 2 == 1 else w[0])
                + jnp.where(odd_y, w[3], w[2]) + jnp.where(odd_z, w[5], w[4])
            )
        return c

    def pack_constants(L):
        L.zs[0] = pack(L, lambda e, i: L.st[e, 1, i])
        L.zs[1] = pack(L, lambda e, i: L.st[e, 0, i])
        L.zs[2] = pack(L, lambda e, i: L.xw[e, 0 if i == 0 else 1], (0, L.n - 1))

    loads[0].wait()
    guess = lambda e, i: g_ref[e, i]
    zpack[0, 0] = pack(L0, guess)
    pl.semaphore_wait(barrier, awaited)
    begin(plans[0]["v"])
    hear = there["gy"][0].astype(jnp.int32) + there["gy"][1].astype(jnp.int32)

    def tell(k):
        for side in range(2):
            @pl.when(there["gy"][side])
            def _():
                pl.semaphore_signal(
                    know.at[k], inc=1, device_id=device(gy=beside["gy"][side]), device_id_type=MESH
                )

    if close:
        tell(0)
    for load in loads[1:]:
        load.wait()
    for e in every:
        for i in range(nx):
            c = scale(L0, lambda e, k, i: w_ref[6 * e + k, i], lambda e, i: d_ref[e, i], e, i)
            L0.cb[e, i] = c * b_ref[e, i]
    pack_constants(L0)
    begin(constants[0])
    for e in every:
        for i in range(nx):
            pfield[0, e, i] = KEEP * guess(e, i) + local(L0, guess, e, i)
    for e in every:
        d1 = coarsen(d_ref[e], 1)
        wsend[6 * EQ + e] = to_rows(coarsen(d1, 2)[None])[0]
        for k in range(6):
            w = 0.25 * coarsen(w_ref[6 * e + k], 1)
            w1[6 * e + k] = w
            wsend[6 * e + k] = to_rows((0.25 * coarsen(w, 2))[None])[0]
        for i in range(half):
            c = scale(L1, lambda e, k, i: w1[6 * e + k, i], lambda e, i: d1[i], e, i)
            w1[6 * EQ + e, i] = c
    own(wsend, wall, l_sem).start()
    start(0)
    if close:
        pl.semaphore_wait(know.at[0], hear)
        tell(1)

    arrive(plans[0]["v"])
    halo = received(L0, 0, hx, hy, hz)
    put(1, L0, planes(lambda e, i: border(L0, pfield[0, e, i], halo, e, i), L0))
    finish = deep(1, L0)
    pack_constants(L1)
    begin(constants[1])
    for m in range(4):
        cos[m] = pack(L1, lambda e, i: co[e, m, i])
    begin(spreads)
    own(wsend, wall, l_sem).wait()
    done(0)
    if close:
        pl.semaphore_wait(know.at[1], hear)
    start(1)
    arrive(constants[0])
    v, outer = finish()
    kept0 = field.at[0]
    for e in every:
        for i in range(nx):
            kept0[e, i] = v[e][i]
    get = lambda e, i: kept0[e, i]
    q = planes(lambda e, i: local(L0, get, e, i), L0)
    halo = outer()
    first = []
    for e in every:
        r = jnp.stack([
            L0.tot[e, i] * (border(L0, q[e][i], halo, e, i) - DAMP * get(e, i)) for i in range(nx)
        ])
        b = coarsen(r, 1)
        first.append([])
        for i in range(half):
            u = w1[6 * EQ + e, i] * b[i]
            L1.cb[e, i] = u
            first[e].append(u)
    put(2, L1, first)
    finish = deep(2, L1)
    done(1)
    start(2)
    arrive(constants[1])
    u, outer = finish()
    kept1 = pfield.at[3]
    for e in every:
        for i in range(half):
            kept1[e, i] = u[e][i]
    get = lambda e, i: kept1[e, i]
    q = planes(lambda e, i: local(L1, get, e, i), L1)
    halo = outer()
    rest = []
    for e in every:
        r = []
        for i in range(half):
            total = border(L1, q[e][i], halo, e, i)
            field[3, e, i] = KEEP * get(e, i) + total
            r.append(L1.tot[e, i] * (total - DAMP * get(e, i)))
        rest.append(coarsen(jnp.stack(r), 2))
    bsend[...] = to_rows(jnp.stack(rest))
    for copy in reversed(everyone()):
        copy.start()
    own(bsend, ball, br_sem).start()
    zpack[3, 0] = pack(L1, lambda e, i: field[3, e, i])
    begin(plans[3]["v"])
    arrive(spreads)
    for m in range(4):
        c = combine(L1, coz[0, m], coz[1, m])
        for e in every:
            for i in range(half):
                zco[e, m, i] = unpack(L1, c, e, i)
    done(2)
    start(3)
    done(3)

    shape = (ngz, rows, nz)
    r_i, l_i = iota(shape, 1), iota(shape, 2)
    g_i = iota(shape, 0)
    zc, yc, xc = l_i % qz, (l_i // qz) % qy, l_i // (qz * qy)
    gyi, gxi = r_i // ngx, r_i % ngx
    inside = [
        ~((xc == qx - 1) & (gxi == ngx - 1)), ~((xc == 0) & (gxi == 0)),
        ~((yc == qy - 1) & (gyi == ngy - 1)), ~((yc == 0) & (gyi == 0)),
        ~((zc == qz - 1) & (g_i == ngz - 1)), ~((zc == 0) & (g_i == 0)),
    ]

    def whole(ref, index):
        return ref[:, :, index].reshape(shape)

    def next_of(v):
        return jnp.concatenate([v[1:], v[:1]], axis=0)

    def prev_of(v):
        return jnp.concatenate([v[-1:], v[:-1]], axis=0)

    def near2(v):
        sy, sx = qz, qz * qy
        return [
            jnp.where(xc == qx - 1, roll(roll(v, (qx - 1) * sx, 2), -1, 1), roll(v, -sx, 2)),
            jnp.where(xc == 0, roll(roll(v, -(qx - 1) * sx, 2), 1, 1), roll(v, sx, 2)),
            jnp.where(yc == qy - 1, roll(roll(v, (qy - 1) * sy, 2), -ngx, 1), roll(v, -sy, 2)),
            jnp.where(yc == 0, roll(roll(v, -(qy - 1) * sy, 2), ngx, 1), roll(v, sy, 2)),
            jnp.where(zc == qz - 1, roll(next_of(v), qz - 1, 2), roll(v, -1, 2)),
            jnp.where(zc == 0, roll(prev_of(v), -(qz - 1), 2), roll(v, 1, 2)),
        ]

    def dot_near(weights, near):
        part = [weights[k] * near[k] for k in range(6)]
        return ((part[0] + part[1]) + (part[2] + part[3])) + (part[4] + part[5])

    def pair(a):
        sy, sx = qz, qz * qy
        a = a + jnp.where(xc % 2 == 0, roll(a, -sx, 2), roll(a, sx, 2))
        a = a + jnp.where(yc % 2 == 0, roll(a, -sy, 2), roll(a, sy, 2))
        a = a + jnp.where(zc % 2 == 0, roll(a, -1, 2), roll(a, 1, 2))
        return a * 0.125

    groups = qx * qy
    tiles = ngz // groups
    shape3 = (tiles, rows, nz)
    r3, l3, t3 = iota(shape3, 1), iota(shape3, 2), iota(shape3, 0)
    inside3 = [
        r3 % ngx < ngx - 1, r3 % ngx > 0, r3 // ngx < ngy - 1, r3 // ngx > 0,
        ~((l3 >= nz - 2) & (t3 == tiles - 1)), ~((l3 < 2) & (t3 == 0)),
    ]

    def join(a):
        a = a.reshape(tiles, groups, rows, nz)
        got = a[:, 0]
        for j in range(1, groups):
            got = jnp.where(l3 // qz == j, a[:, j], got)
        return got

    def part(a):
        parts = []
        for j in range(groups):
            mine = jnp.where(l3 // qz == j, a, 0.0)
            size = qz
            while size < nz:
                mine = mine + roll(mine, size, 2)
                size *= 2
            parts.append(mine)
        return jnp.stack(parts, axis=1).reshape(shape)

    def near3(v):
        if tiles == 1:
            up, down = roll(v, -2, 2), roll(v, 2, 2)
        else:
            up = jnp.where(l3 >= nz - 2, roll(next_of(v), -2, 2), roll(v, -2, 2))
            down = jnp.where(l3 < 2, roll(prev_of(v), 2, 2), roll(v, 2, 2))
        return [roll(v, -1, 1), roll(v, 1, 1), roll(v, -ngx, 1), roll(v, ngx, 1), up, down]

    w2, t2, w3, c2, c3 = [], [], [], [], []
    for e in range(EQ):
        plain = [whole(wall, 6 * e + k) for k in range(6)]
        d2 = whole(wall, 6 * EQ + e)
        total = d2
        for k in range(6):
            total = total + plain[k]
        t2.append((1.0 / DAMP) * total)
        c2.append(DAMP / total)
        w2.append([jnp.where(inside[k], c2[e] * plain[k], 0.0) for k in range(6)])
        plain3 = [0.25 * join(pair(plain[k])) for k in range(6)]
        total = join(pair(d2))
        for k in range(6):
            total = total + plain3[k]
        c3.append(DAMP / total)
        w3.append([jnp.where(inside3[k], c3[e] * plain3[k], 0.0) for k in range(6)])

    arrive(plans[3]["v"])
    pltpu.make_async_copy(ball, ball, br_sem).wait()

    rhs = [c2[e] * whole(ball, e) for e in every]

    def smooth2(v):
        return [(KEEP * v[e] + rhs[e]) + dot_near(w2[e], near2(v[e])) for e in every]

    v2 = list(rhs)
    for step in range(SWEEPS - 1):
        v2 = smooth2(v2)
    rest = [t2[e] * ((rhs[e] - DAMP * v2[e]) + dot_near(w2[e], near2(v2[e]))) for e in every]
    rhs3 = [c3[e] * join(pair(rest[e])) for e in every]
    v3 = list(rhs3)
    for step in range(COARSE_SWEEPS - 1):
        v3 = [(KEEP * v3[e] + rhs3[e]) + dot_near(w3[e], near3(v3[e])) for e in every]
    v2 = [v2[e] + part(v3[e]) for e in every]
    for step in range(SWEEPS):
        v2 = smooth2(v2)
    for e in every:
        e2[e] = v2[e]

    wide = groups * nz
    source = iota((nz, wide), 0)
    target = iota((nz, wide), 1)
    widen = jnp.where(source == (target // nz) * qz + (target % nz) // 4, 1.0, 0.0).astype(jnp.float32)
    here = (gx, gy, gz)
    names = ("gx", "gy", "gz")

    def line(e, *moves):
        at, ok = list(here), None
        for axis, side in moves:
            at[axis] = beside[names[axis]][side]
            ok = there[names[axis]][side] if ok is None else ok & there[names[axis]][side]
        got = e2[e, at[2], pl.ds(at[1] * ngx + at[0], 1), :]
        return got if ok is None else jnp.where(ok, got, 0.0)

    around = ((), ((0, 0),), ((0, 1),), ((1, 0),), ((1, 1),))
    for block in range(3):
        extra = () if block == 0 else ((2, block - 1),)
        for e in every:
            for o, moves in enumerate(around):
                at = 16 * block + 5 * e + o
                lines[at : at + 1, :] = line(e, *moves, *extra)
        lines[16 * block + 15 : 16 * block + 16, :] = jnp.zeros((1, nz), jnp.float32)
    for e in every:
        for sx in range(2):
            for sy in range(2):
                at = 48 + 4 * e + 2 * sx + sy
                lines[at : at + 1, :] = line(e, (0, sx), (1, sy))
    lines[60:64, :] = jnp.zeros((4, nz), jnp.float32)
    broad[...] = jnp.dot(lines[...], widen, precision=HIGH, preferred_element_type=jnp.float32)
    lane16 = iota((16, nz), 1)
    for g in range(groups):
        cols = pl.ds(g * nz, nz)
        c = broad[0:16, cols]
        low, high = roll(broad[16:32, cols], 2, 1), roll(broad[32:48, cols], -2, 1)
        outside[:, cols] = jnp.where(lane16 < nz // 2, low, high)
        beyond[:, cols] = jnp.where(
            lane16 < 2, low,
            jnp.where(lane16 >= nz - 2, high, jnp.where(lane16 % 4 < 2, roll(c, 2, 1), roll(c, -2, 1))),
        )
    ysel, yhalf = yi // 4, yi // 2 % 2

    def strip(ref, at, x, y):
        col = (x * qy + y) * nz
        return jnp.broadcast_to(ref[at : at + 1, col : col + nz], tile)

    def spot(e, o):
        return 5 * e + o

    def corner(e, sx, sy):
        return 48 + 4 * e + 2 * sx + sy

    def plane(ref, at, x):
        got = strip(ref, at, x, 0)
        for y in range(1, qy):
            got = jnp.where(ysel == y, strip(ref, at, x, y), got)
        return got

    def across_y(ref, center, minus, plus, x):
        got = None
        for y in range(qy):
            below = strip(ref, center, x, y - 1) if y > 0 else strip(ref, minus, x, qy - 1)
            above = strip(ref, center, x, y + 1) if y < qy - 1 else strip(ref, plus, x, 0)
            both = jnp.where(yhalf == 0, below, above)
            got = both if got is None else jnp.where(ysel == y, both, got)
        return got

    def across_x(ref, e, i):
        x = i // 2
        to = x + 1 if i % 2 == 1 else x - 1
        if to < 0:
            return plane(ref, spot(e, 1), qx - 1)
        return plane(ref, spot(e, 2), 0) if to == qx else plane(ref, spot(e, 0), to)

    def rows_y(ref, e, x):
        if x < 0:
            low, high, x = corner(e, 0, 0), corner(e, 0, 1), qx - 1
        elif x == qx:
            low, high, x = corner(e, 1, 0), corner(e, 1, 1), 0
        else:
            low, high = spot(e, 3), spot(e, 4)
        return jnp.where(yi < ny // 2, strip(ref, low, x, qy - 1), strip(ref, high, x, 0))

    left, behind, through = received(L1, 3, hx, hy, hz)
    mine = edge_rows(L1.s, *there["gy"])

    def add_x(side, e):
        o, face, near = 1 + side, qx - 1 if side == 0 else 0, 0 if side == 0 else qx - 1
        got = left(side, e) + cox[side, e, 0] * plane(broad, spot(e, o), face)
        got = got + cox[side, e, 1] * plane(broad, spot(e, 0), near)
        got = got + cox[side, e, 2] * across_y(
            broad, spot(e, o), corner(e, side, 0), corner(e, side, 1), face
        )
        got = got + cox[side, e, 3] * plane(beyond, spot(e, o), face)
        return jnp.where(there["gx"][side], got, 0.0)

    def add_y(e, i):
        x = i // 2
        got = behind(e, i) + coy[e, 0, i] * rows_y(broad, e, x)
        got = got + coy[e, 1, i] * rows_y(broad, e, x + 1 if i % 2 == 1 else x - 1)
        got = got + coy[e, 2, i] * plane(broad, spot(e, 0), x)
        got = got + coy[e, 3, i] * rows_y(beyond, e, x)
        return jnp.where(mine, got, 0.0)

    def add_z(e, i):
        x = i // 2
        got = through(e, i) + zco[e, 0, i] * plane(outside, spot(e, 0), x)
        got = got + zco[e, 1, i] * across_x(outside, e, i)
        got = got + zco[e, 2, i] * across_y(outside, spot(e, 0), spot(e, 3), spot(e, 4), x)
        return got + zco[e, 3, i] * plane(broad, spot(e, 0), x)

    swept = pfield.at[3]
    for e in every:
        for i in range(half):
            x = i // 2
            got = field[3, e, i] + co[e, 0, i] * plane(broad, spot(e, 0), x)
            got = got + co[e, 1, i] * across_x(broad, e, i)
            got = got + co[e, 2, i] * across_y(broad, spot(e, 0), spot(e, 3), spot(e, 4), x)
            swept[e, i] = got + co[e, 3, i] * plane(beyond, spot(e, 0), x)
    get = lambda e, i: swept[e, i]
    halo = (add_x, add_y, add_z)
    u = planes(lambda e, i: KEEP * get(e, i) + border(L1, local(L1, get, e, i), halo, e, i), L1)
    put(4, L0, planes(lambda e, i: kept0[e, i] + u[e][i // 2], L0))
    finish = deep(4, L0)
    v, outer = finish()
    last = pfield.at[0]
    for e in every:
        for i in range(nx):
            last[e, i] = v[e][i]
    get = lambda e, i: last[e, i]
    q = planes(lambda e, i: KEEP * get(e, i) + local(L0, get, e, i), L0)
    halo = outer()
    for e in every:
        for i in range(nx):
            out_ref[e, i] = border(L0, q[e][i], halo, e, i)
    await_all(s_sem, [g for p in plans for g in p.values()] + constants + [spreads])
    for number in range(4):
        await_rows(ws_sem.at[number], stage_rows(number))
    await_rows(bs_sem, EQ * (rows * ngz - 1))


def per_device(dims, cores, couplings, diagonal, right_side, guess):
    ngx, ngy, ngz = dims
    brick = guess.shape[1:]
    nx, ny, nz = brick
    half = nx // 2
    qx, qy = nx // 4, ny // 4
    rows = ngx * ngy
    nX = ngz // cores
    rounds = len(DEEP)
    f32 = jnp.float32
    vmem = pltpu.VMEM
    dma = pltpu.SemaphoreType.DMA

    def level(n):
        return [
            vmem((EQ, 6, n, ny, nz), f32),
            vmem((EQ, 2, n, ny, nz), f32),
            vmem((EQ, 2, ny, nz), f32),
            vmem((EQ, n, ny, nz), f32),
            vmem((EQ, n, ny, nz), f32),
            vmem((3, ny, nz), f32),
            vmem((2, EQ, ny, nz), f32),
            vmem((2, EQ, 2, ny, nz), f32),
            vmem((EQ, 2, n, ny, nz), f32),
            vmem((EQ, 2, ny, nz), f32),
            vmem((2, 3, ny, nz), f32),
            dma,
        ]

    faces = [
        vmem((rounds, 2, EQ, ny, nz), f32),
        vmem((rounds, EQ) + brick, f32),
        vmem((rounds, 2, ny, nz), f32),
    ]
    return pl.pallas_call(
        functools.partial(kernel, dims, cores),
        out_shape=vmem(guess.shape, f32),
        in_specs=[pl.BlockSpec(memory_space=pl.ANY)] * 4,
        out_specs=pl.BlockSpec(memory_space=vmem),
        scratch_shapes=[
            vmem(couplings.shape, f32),
            vmem(diagonal.shape, f32),
            vmem(right_side.shape, f32),
            vmem(guess.shape, f32),
            vmem((max(2048, nX * rows * 7 * EQ * (cores - 1) // 8, rows * (nX - 1) * 7 * EQ // 8), 8, nz), f32),
            vmem((rounds, EQ) + brick, f32),
            vmem((rounds, EQ) + brick, f32),
            vmem((rounds, 2, ny, nz), f32),
            *faces,
            *faces,
            vmem((rounds, 2, EQ, ny, nz), f32),
            vmem((rounds, 2, 2, ny, nz), f32),
            vmem((rounds, 2, ny, nz), f32),
            vmem((7 * EQ, half, ny, nz), f32),
            vmem((EQ, 4, half, ny, nz), f32),
            vmem((4, ny, nz), f32),
            vmem((2, EQ, 4, ny, nz), f32),
            vmem((EQ, 4, half, ny, nz), f32),
            vmem((2, 4, ny, nz), f32),
            vmem((EQ, 4, half, ny, nz), f32),
            *level(nx),
            *level(half),
            vmem((7 * EQ, ny, nz), f32),
            vmem((nX, cores, 7 * EQ, rows, nz), f32),
            vmem((EQ, ny, nz), f32),
            vmem((nX, cores, EQ, rows, nz), f32),
            vmem((EQ, ngz, rows, nz), f32),
            vmem((64, nz), f32),
            vmem((64, qx * qy * nz), f32),
            vmem((16, qx * qy * nz), f32),
            vmem((16, qx * qy * nz), f32),
            dma,
            dma((rounds, 3)),
            dma,
            dma((4,)),
            dma((4,)),
            dma,
            dma,
            dma,
            dma((4,)),
            pltpu.SemaphoreType.REGULAR((2,)),
        ],
        compiler_params=pltpu.CompilerParams(
            collective_id=0, has_side_effects=True, vmem_limit_bytes=60 * 1024 * 1024
        ),
    )(couplings, diagonal, right_side, guess)


def solution(mesh):
    dims = (mesh.shape["gx"], mesh.shape["gy"], mesh.shape["gz"])
    cores = 2 if dims[2] % 2 == 0 else 1
    spec = P(None, "gx", "gy", "gz")
    return jax.shard_map(
        functools.partial(per_device, dims, cores),
        mesh=mesh,
        in_specs=(spec,) * 4,
        out_specs=spec,
        check_vma=False,
    )
```

```python
import functools

import jax
import jax.numpy as jnp
from jax import lax
from jax.experimental import pallas as pl
from jax.experimental.pallas import tpu as pltpu
from jax.sharding import PartitionSpec as P

SWEEPS = 2
COARSE_SWEEPS = 8
DAMP = 0.8
KEEP = 1.0 - DAMP
EQ = 3
MESH = pl.DeviceIdType.MESH
HIGH = lax.Precision.HIGHEST
DEEP = (False, True, True, False, True)
FINE = (True, True, False, False, True)


def roll(value, shift, axis):
    size = value.shape[axis]
    shift = shift % size
    return value if shift == 0 else pltpu.roll(value, shift, axis)


def iota(shape, axis):
    return lax.broadcasted_iota(jnp.int32, shape, axis)


class Level:
    def __init__(self, n, s, refs):
        self.n, self.s = n, s
        (self.cw, self.st, self.xw, self.cb, self.tot, self.zs,
         self.xt, self.xst, self.yst, self.yxw, self.zst, self.r_sem) = refs


def kernel(
    dims, cores, w_hbm, d_hbm, b_hbm, g_hbm, out_ref,
    w_ref, d_ref, b_ref, g_ref,
    tally, field, pfield, zpack, hx, hy, hz, px, py, pz, exy, exz, eyz, w1, co, cos, cox, coy, coz, zco, *rest,
):
    level_refs = (rest[:12], rest[12:24])
    (wsend, wall, bsend, ball, e2, lines, broad, widen, mix, mixed,
     s_sem, r_sem, co_sem, ws_sem, wr_sem, bs_sem, br_sem, l_sem, i_sem, know) = rest[24:]
    ngx, ngy, ngz = dims
    nx, ny, nz = g_ref.shape[1:]
    half = nx // 2
    qx, qy, qz = nx // 4, ny // 4, nz // 4
    rows = ngx * ngy
    nX = ngz // cores
    gx, gy, gz = lax.axis_index("gx"), lax.axis_index("gy"), lax.axis_index("gz")
    X, core = gz // cores, gz % cores
    row = gy * ngx + gx
    axes = (("gx", gx, ngx), ("gy", gy, ngy), ("gz", gz, ngz))
    L0 = Level(nx, 1, level_refs[0])
    L1 = Level(half, 2, level_refs[1])
    tile = (ny, nz)
    yi, zi = iota(tile, 0), iota(tile, 1)
    every = range(EQ)

    def device(**change):
        here = {"gx": gx, "gy": gy, "gz": gz}
        here.update(change)
        return (here["gx"], here["gy"], here["gz"])

    barrier = pltpu.get_barrier_semaphore()
    close = ngy <= 4 and ngz <= 4
    awaited = 0

    def greet(ok, where):
        @pl.when(ok)
        def _():
            pl.semaphore_signal(barrier, inc=1, device_id=where, device_id_type=MESH)
        return ok.astype(jnp.int32)

    for name, index, count in axes:
        if close and name != "gx":
            steps = (-1, 1) if name == "gy" or cores == 1 else (-1, 1, -cores, cores)
            for step in steps:
                ok = (index + step >= 0) & (index + step < count)
                awaited = awaited + greet(ok, device(**{name: jnp.clip(index + step, 0, count - 1)}))
        else:
            for step in range(1, count):
                pl.semaphore_signal(
                    barrier, inc=1, device_id=device(**{name: (index + step) % count}),
                    device_id_type=MESH,
                )
            awaited = awaited + (count - 1)

    loads = [
        pltpu.make_async_copy(a, z, i_sem.at[slot])
        for slot, (a, z) in enumerate(
            ((g_hbm, g_ref), (w_hbm, w_ref), (d_hbm, d_ref), (b_hbm, b_ref))
        )
    ]
    for load in loads:
        load.start()

    there = {
        name: (index > 0, index < count - 1) for name, index, count in axes
    }
    beside = {
        name: (jnp.maximum(index - 1, 0), jnp.minimum(index + 1, count - 1))
        for name, index, count in axes
    }

    def edge_rows(s, lo, hi):
        return (yi < jnp.where(lo, s, 0)) | (yi >= jnp.where(hi, ny - s, ny))

    def remote(a, z, ss, rs, where):
        return pltpu.make_async_remote_copy(
            src_ref=a, dst_ref=z, send_sem=ss, recv_sem=rs,
            device_id=where, device_id_type=MESH,
        )

    def rows_of(side, s):
        return pl.ds(0 if side == 0 else ny - s, s)

    counts = [
        [k for k in (0, 1, 2) if (k > 0 or count == 1) and k < count and (k == 2 or count <= 2 or k == 1)]
        for _, _, count in axes
    ]
    found = [
        there[name][0].astype(jnp.int32) + there[name][1].astype(jnp.int32) for name, _, _ in axes
    ]
    cases = []
    for cx in counts[0]:
        for cy in counts[1]:
            for cz in counts[2]:
                cases.append(((cx, cy, cz), (found[0] == cx) & (found[1] == cy) & (found[2] == cz)))

    def await_rows(sem, number):
        if number > 0:
            part = next(k for k in (8, 4, 2, 1) if number % k == 0)
            ref = tally.at[pl.ds(0, number // part), pl.ds(0, part)]
            pltpu.make_async_copy(ref, ref, sem).wait()

    def await_all(sem, groups):
        for (cx, cy, cz), ok in cases:
            many = {"x": cx, "y": cy, "z": cz, "xy": cx * cy, "xz": cx * cz, "yz": cy * cz}
            number = sum(many[kind] * size for g in groups for kind, size in g.sizes.items())
            if len(cases) == 1:
                await_rows(sem, number)
            else:
                @pl.when(ok)
                def _():
                    await_rows(sem, number)

    class Group:
        def __init__(self, sem):
            self.sem, self.copies, self.sizes = sem, [], {}

        def add(self, kind, side, a, z, where, goes):
            self.copies.append((remote(a, z, s_sem, self.sem, where), goes))
            if side == 0:
                size = 1
                for d in z.shape[:-1]:
                    size *= d
                self.sizes[kind] = self.sizes.get(kind, 0) + size

    def plan(r):
        n, s = (nx, 1) if FINE[r] else (half, 2)
        src = g_ref if r == 0 else field.at[r]
        groups = {k: Group(r_sem.at[r, "vdp".index(k)]) for k in "vdp"}
        kinds = [("v", src, 0, hx, hy, hz)]
        if DEEP[r]:
            kinds.append(("p", pfield.at[r], 1, px, py, pz))
        for side in range(2):
            other = 1 - side
            for group, a, which, zx, zy, zz in kinds:
                g = groups[group]
                g.add("x", side, a.at[:, 0 if side == 0 else n - 1], zx.at[r, other],
                      device(gx=beside["gx"][side]), there["gx"][side])
                g.add("y", side, a.at[:, 0:n, rows_of(side, s)], zy.at[r, :, 0:n, rows_of(other, s)],
                      device(gy=beside["gy"][side]), there["gy"][side])
                g.add("z", side, zpack.at[r, which], zz.at[r, other],
                      device(gz=beside["gz"][side]), there["gz"][side])
        if DEEP[r]:
            g = groups["d"]
            for i in range(2):
                for j in range(2):
                    g.add("xy", 2 * i + j, src.at[:, 0 if i == 0 else n - 1, rows_of(j, s)],
                          exy.at[r, 1 - i, :, rows_of(1 - j, s)],
                          device(gx=beside["gx"][i], gy=beside["gy"][j]),
                          there["gx"][i] & there["gy"][j])
                    g.add("xz", 2 * i + j, zpack.at[r, 0], exz.at[r, 1 - i, 1 - j],
                          device(gx=beside["gx"][i], gz=beside["gz"][j]),
                          there["gx"][i] & there["gz"][j])
                    g.add("yz", 2 * i + j, zpack.at[r, 0, rows_of(i, s)], eyz.at[r, 1 - j, rows_of(1 - i, s)],
                          device(gy=beside["gy"][i], gz=beside["gz"][j]),
                          there["gy"][i] & there["gz"][j])
        return groups

    plans = [plan(r) for r in range(len(DEEP))]

    def plan_constants(L):
        g = Group(L.r_sem)
        for side in range(2):
            other = 1 - side
            x_at, x_ok = device(gx=beside["gx"][side]), there["gx"][side]
            y_at, y_ok = device(gy=beside["gy"][side]), there["gy"][side]
            g.add("x", side, L.xw.at[:, side], L.xt.at[other], x_at, x_ok)
            g.add("x", side, L.st.at[:, :, 0 if side == 0 else L.n - 1], L.xst.at[other], x_at, x_ok)
            g.add("y", side, L.st.at[:, :, :, rows_of(side, L.s)],
                  L.yst.at[:, :, :, rows_of(other, L.s)], y_at, y_ok)
            g.add("y", side, L.xw.at[:, :, rows_of(side, L.s)], L.yxw.at[:, :, rows_of(other, L.s)], y_at, y_ok)
            g.add("z", side, L.zs, L.zst.at[other], device(gz=beside["gz"][side]), there["gz"][side])
        return g

    def plan_spreads():
        g = Group(co_sem)
        s = L1.s
        for side in range(2):
            other = 1 - side
            g.add("x", side, co.at[:, :, 0 if side == 0 else half - 1], cox.at[other],
                  device(gx=beside["gx"][side]), there["gx"][side])
            g.add("y", side, co.at[:, :, :, rows_of(side, s)], coy.at[:, :, :, rows_of(other, s)],
                  device(gy=beside["gy"][side]), there["gy"][side])
            g.add("z", side, cos, coz.at[other], device(gz=beside["gz"][side]), there["gz"][side])
        return g

    spreads = plan_spreads()
    constants = [plan_constants(L0), plan_constants(L1)]

    def begin(*groups):
        for g in groups:
            for copy, goes in g.copies:
                @pl.when(goes)
                def _():
                    copy.start()

    def arrive(*groups):
        for g in groups:
            await_all(g.sem, [g])

    def pack(L, get, planes=None):
        got = jnp.zeros(tile, jnp.float32)
        for e in every:
            for i in (range(L.n) if planes is None else planes):
                j = e * L.n + i
                got = jnp.where(zi // (2 * L.s) == j, roll(get(e, i), 2 * L.s * j + L.s, 1), got)
        return got

    def unpack(L, tile_of, e, i):
        return roll(tile_of, -(2 * L.s * (e * L.n + i) + L.s), 1)

    def combine(L, low, high, ok=None):
        s = L.s
        up = zi % (2 * s) < s
        has_low, has_high = there["gz"]
        if ok is not None:
            has_low, has_high = has_low & ok, has_high & ok
        code = jnp.where(up, jnp.where(has_high, 1, 0), jnp.where(has_low, 2, 0))
        return jnp.where(code == 1, roll(high, -s, 1), jnp.where(code == 2, roll(low, s, 1), 0.0))

    def local(L, get, e, i):
        n, s = L.n, L.s
        v = get(e, i)
        q = L.cw[e, 2, i] * roll(v, -s, 0) + L.cw[e, 3, i] * roll(v, s, 0)
        q = q + L.cw[e, 4, i] * roll(v, -s, 1) + L.cw[e, 5, i] * roll(v, s, 1)
        if i < n - 1:
            q = q + L.cw[e, 0, i] * get(e, i + 1)
        if i > 0:
            q = q + L.cw[e, 1, i] * get(e, i - 1)
        return q + L.cb[e, i]

    def border(L, q, halo, e, i):
        gx_of, gy_of, gz_of = halo
        q = q + L.st[e, 0, i] * gy_of(e, i) + L.st[e, 1, i] * gz_of(e, i)
        if i == 0:
            q = q + L.xw[e, 0] * gx_of(0, e)
        if i == L.n - 1:
            q = q + L.xw[e, 1] * gx_of(1, e)
        return q

    def received(L, r, x_ref, y_ref, z_ref):
        my = edge_rows(L.s, *there["gy"])
        c = combine(L, z_ref[r, 0], z_ref[r, 1])
        return (
            lambda side, e: jnp.where(there["gx"][side], x_ref[r, side, e], 0.0),
            lambda e, i: jnp.where(my, y_ref[r, e, i], 0.0),
            lambda e, i: unpack(L, c, e, i),
        )

    def ring(L, r, get, own):
        n, s = L.n, L.s
        my = edge_rows(s, *there["gy"])
        lines_of = []
        columns_of = []
        for side in range(2):
            ok = there["gx"][side]
            mask = edge_rows(s, ok & there["gy"][0], ok & there["gy"][1])
            lines_of.append([jnp.where(mask, exy[r, side, e], 0.0) for e in every])
            columns_of.append(combine(L, exz[r, side, 0], exz[r, side, 1], ok))
        cy = jnp.where(my, combine(L, eyz[r, 0], eyz[r, 1]), 0.0)
        rx = [
            [
                jnp.where(
                    there["gx"][side],
                    px[r, side, e] + L.xt[side, e] * get(e, 0 if side == 0 else n - 1)
                    + L.xst[side, e, 0] * lines_of[side][e]
                    + L.xst[side, e, 1] * unpack(L, columns_of[side], e, n - 1 if side == 0 else 0),
                    0.0,
                )
                for e in every
            ]
            for side in range(2)
        ]

        def ry(e, i):
            got = py[r, e, i] + L.yst[e, 0, i] * get(e, i) + L.yst[e, 1, i] * unpack(L, cy, e, i)
            if i == 0:
                got = got + L.yxw[e, 0] * lines_of[0][e]
            if i == n - 1:
                got = got + L.yxw[e, 1] * lines_of[1][e]
            return jnp.where(my, got, 0.0)

        far = 2 * s * (n - 1)
        sideways = jnp.where(
            zi // (2 * s) % n == 0, roll(columns_of[0], -far, 1), roll(columns_of[1], far, 1)
        )
        toward, along_y, along_x = [combine(L, L.zst[0, k], L.zst[1, k]) for k in range(3)]
        c = combine(L, pz[r, 0], pz[r, 1]) + toward * own + along_y * cy + along_x * sideways
        c = jnp.where(zi < 2 * s * EQ * n, c, 0.0)
        return (
            lambda side, e: rx[side][e],
            ry,
            lambda e, i: unpack(L, c, e, i),
        )

    def put(r, L, v):
        for e in every:
            for i in range(L.n):
                field[r, e, i] = v[e][i]

    def planes(f, L):
        return [[f(e, i) for i in range(L.n)] for e in every]

    def deep(r, L):
        get = lambda e, i: field[r, e, i]
        own = pack(L, get)
        zpack[r, 0] = own
        begin(plans[r]["d"], plans[r]["v"])
        for e in every:
            for i in range(L.n):
                pfield[r, e, i] = KEEP * get(e, i) + local(L, get, e, i)
        zpack[r, 1] = pack(L, lambda e, i: pfield[r, e, i])
        begin(plans[r]["p"])

        def finish():
            arrive(plans[r]["v"])
            halo = received(L, r, hx, hy, hz)
            new = planes(lambda e, i: border(L, pfield[r, e, i], halo, e, i), L)

            def outer():
                arrive(plans[r]["d"], plans[r]["p"])
                return ring(L, r, get, zpack[r, 0])

            return new, outer

        return finish

    def coarsen(a, s):
        n = a.shape[0]
        a = jnp.stack([a[2 * i] + a[2 * i + 1] for i in range(n // 2)])
        y, z = iota(a.shape, 1), iota(a.shape, 2)
        a = a + jnp.where((y // s) % 2 == 0, roll(a, -s, 1), roll(a, s, 1))
        a = a + jnp.where((z // s) % 2 == 0, roll(a, -s, 2), roll(a, s, 2))
        return a * 0.125

    def select(a, onehot):
        parts = []
        for _ in range(3):
            parts.append(a.astype(jnp.bfloat16))
            a = a - parts[-1].astype(jnp.float32)
        got = jnp.dot(jnp.concatenate(parts, axis=0), onehot, preferred_element_type=jnp.float32)
        m = a.shape[0]
        return (got[0:m] + got[m : 2 * m]) + got[2 * m :]

    groups = qx * qy
    source = iota((nz, nz), 0)
    target = iota((nz, nz), 1)
    squeeze = jnp.where(source == 4 * (target % qz), 1.0, 0.0).astype(jnp.bfloat16)

    def to_rows(a):
        m = a.shape[0]
        c = select(a.reshape(m * qx * ny, nz), squeeze).reshape(m, qx, ny, nz)
        place = iota((m, ny, nz), 2) // qz
        got = jnp.zeros((m, ny, nz), jnp.float32)
        for x in range(qx):
            for y in range(qy):
                part = roll(c[:, x], -4 * y, 1)
                got = jnp.where(place == (x * qy + y + gz) % groups, part, got)
        return got

    def own(small, whole, sem):
        return pltpu.make_async_copy(
            small.at[:, pl.ds(0, 1)], whole.at[X, core, :, pl.ds(row, 1)], sem
        )

    def stage(number, small, whole, rs):
        made = []
        if number == 0:
            for step in range(1, ngx):
                made.append((small.at[:, pl.ds(0, 1)], whole.at[X, core, :, pl.ds(row, 1)],
                             step, device(gx=(gx + step) % ngx)))
        elif number == 1:
            block = whole.at[X, core, :, pl.ds(gy * ngx, ngx)]
            for step in range(1, ngy):
                made.append((block, block, step, device(gy=(gy + step) % ngy)))
        elif number == 2:
            block = whole.at[X, core]
            for step in range(1, nX):
                made.append((block, block, step, device(gz=((X + step) % nX) * cores + core)))
        else:
            block = whole.at[:, core]
            for step in range(1, cores):
                made.append((block, block, step, device(gz=X * cores + (core + step) % cores)))
        return [
            remote(a, z, ws_sem.at[number], rs.at[number], where)
            for a, z, _, where in made
        ]

    wargs = (wsend, wall, wr_sem)

    def everyone():
        made = []
        for az in range(ngz):
            for ay in range(ngy):
                for ax in range(ngx):
                    if ax + ay + az == 0:
                        continue
                    made.append(remote(
                        bsend.at[:, pl.ds(0, 1)], ball.at[X, core, :, pl.ds(row, 1)],
                        bs_sem, br_sem,
                        ((gx + ax) % ngx, (gy + ay) % ngy, (gz + az) % ngz),
                    ))
        return made

    def start(number):
        for copy in stage(number, *wargs):
            copy.start()

    def stage_rows(number):
        return 7 * EQ * (
            ngx - 1, ngx * (ngy - 1), rows * (nX - 1), nX * rows * (cores - 1)
        )[number]

    def done(number):
        await_rows(wr_sem.at[number], stage_rows(number))

    def scale(L, get_w, get_d, e, i):
        n, s = L.n, L.s
        raw = [get_w(e, k, i) for k in range(6)]
        total = get_d(e, i)
        for k in range(6):
            total = total + raw[k]
        c = DAMP / total
        w = [c * raw[k] for k in range(6)]
        L.tot[e, i] = (1.0 / DAMP) * total
        last_y, first_y, last_z, first_z = yi >= ny - s, yi < s, zi >= nz - s, zi < s
        L.cw[e, 0, i] = w[0]
        L.cw[e, 1, i] = w[1]
        L.cw[e, 2, i] = jnp.where(last_y, 0.0, w[2])
        L.cw[e, 3, i] = jnp.where(first_y, 0.0, w[3])
        L.cw[e, 4, i] = jnp.where(last_z, 0.0, w[4])
        L.cw[e, 5, i] = jnp.where(first_z, 0.0, w[5])
        L.st[e, 0, i] = jnp.where(last_y, w[2], jnp.where(first_y, w[3], 0.0))
        L.st[e, 1, i] = jnp.where(last_z, w[4], jnp.where(first_z, w[5], 0.0))
        if i == 0:
            L.xw[e, 0] = w[1]
        if i == n - 1:
            L.xw[e, 1] = w[0]
        if L is L1:
            odd_y, odd_z = yi // s % 2 == 1, zi // s % 2 == 1
            co[e, 1, i] = w[0] if i % 2 == 1 else w[1]
            co[e, 2, i] = jnp.where(odd_y, w[2], w[3])
            co[e, 3, i] = jnp.where(odd_z, w[4], w[5])
            co[e, 0, i] = (
                KEEP + (w[1] if i % 2 == 1 else w[0])
                + jnp.where(odd_y, w[3], w[2]) + jnp.where(odd_z, w[5], w[4])
            )
        return c

    def pack_constants(L):
        L.zs[0] = pack(L, lambda e, i: L.st[e, 1, i])
        L.zs[1] = pack(L, lambda e, i: L.st[e, 0, i])
        L.zs[2] = pack(L, lambda e, i: L.xw[e, 0 if i == 0 else 1], (0, L.n - 1))

    loads[0].wait()
    guess = lambda e, i: g_ref[e, i]
    zpack[0, 0] = pack(L0, guess)
    pl.semaphore_wait(barrier, awaited)
    begin(plans[0]["v"])
    hear = there["gy"][0].astype(jnp.int32) + there["gy"][1].astype(jnp.int32)

    def tell(k):
        for side in range(2):
            @pl.when(there["gy"][side])
            def _():
                pl.semaphore_signal(
                    know.at[k], inc=1, device_id=device(gy=beside["gy"][side]), device_id_type=MESH
                )

    if close:
        tell(0)
    for load in loads[1:]:
        load.wait()
    level2 = [None] * (7 * EQ)
    for e in every:
        d1 = coarsen(d_ref[e], 1)
        level2[6 * EQ + e] = coarsen(d1, 2)
        for k in range(6):
            w = 0.25 * coarsen(w_ref[6 * e + k], 1)
            w1[6 * e + k] = w
            level2[6 * e + k] = 0.25 * coarsen(w, 2)
        for i in range(half):
            c = scale(L1, lambda e, k, i: w1[6 * e + k, i], lambda e, i: d1[i], e, i)
            w1[6 * EQ + e, i] = c
    wsend[...] = to_rows(jnp.stack(level2))
    own(wsend, wall, l_sem).start()
    start(0)
    for e in every:
        for i in range(nx):
            c = scale(L0, lambda e, k, i: w_ref[6 * e + k, i], lambda e, i: d_ref[e, i], e, i)
            L0.cb[e, i] = c * b_ref[e, i]
    pack_constants(L0)
    begin(constants[0])
    for e in every:
        for i in range(nx):
            pfield[0, e, i] = KEEP * guess(e, i) + local(L0, guess, e, i)
    if close:
        pl.semaphore_wait(know.at[0], hear)
        tell(1)

    arrive(plans[0]["v"])
    halo = received(L0, 0, hx, hy, hz)
    put(1, L0, planes(lambda e, i: border(L0, pfield[0, e, i], halo, e, i), L0))
    finish = deep(1, L0)
    own(wsend, wall, l_sem).wait()
    done(0)
    if close:
        pl.semaphore_wait(know.at[1], hear)
    start(1)
    pack_constants(L1)
    begin(constants[1])
    v, outer = finish()
    kept0 = field.at[0]
    for e in every:
        for i in range(nx):
            kept0[e, i] = v[e][i]
    get = lambda e, i: kept0[e, i]
    q = planes(lambda e, i: local(L0, get, e, i), L0)
    arrive(constants[0])
    halo = outer()
    first = []
    for e in every:
        r = jnp.stack([
            L0.tot[e, i] * (border(L0, q[e][i], halo, e, i) - DAMP * get(e, i)) for i in range(nx)
        ])
        b = coarsen(r, 1)
        first.append([])
        for i in range(half):
            u = w1[6 * EQ + e, i] * b[i]
            L1.cb[e, i] = u
            first[e].append(u)
    put(2, L1, first)
    finish = deep(2, L1)
    done(1)
    start(2)
    for m in range(4):
        cos[m] = pack(L1, lambda e, i: co[e, m, i])
    begin(spreads)
    u, outer = finish()
    kept1 = pfield.at[3]
    for e in every:
        for i in range(half):
            kept1[e, i] = u[e][i]
    get = lambda e, i: kept1[e, i]
    q = planes(lambda e, i: local(L1, get, e, i), L1)
    arrive(constants[1])
    halo = outer()
    rest = []
    for e in every:
        r = []
        for i in range(half):
            total = border(L1, q[e][i], halo, e, i)
            field[3, e, i] = KEEP * get(e, i) + total
            r.append(L1.tot[e, i] * (total - DAMP * get(e, i)))
        rest.append(coarsen(jnp.stack(r), 2))
    bsend[...] = to_rows(jnp.stack(rest))
    for copy in reversed(everyone()):
        copy.start()
    own(bsend, ball, br_sem).start()
    zpack[3, 0] = pack(L1, lambda e, i: field[3, e, i])
    begin(plans[3]["v"])
    arrive(spreads)
    for m in range(4):
        c = combine(L1, coz[0, m], coz[1, m])
        for e in every:
            for i in range(half):
                zco[e, m, i] = unpack(L1, c, e, i)
    NX, NY, NZ = ngx * qx, ngy * qy, ngz * qz
    shape = (NZ, 3 * nz)
    kind, t = iota(shape, 1) // nz, iota(shape, 1) % nz
    base = gz * qz + t // 4
    wanted = jnp.where(
        kind == 0, base,
        jnp.where(
            kind == 1, base + jnp.where(t % 4 < 2, -1, 1),
            jnp.where(t < nz // 2, gz * qz - 1, gz * qz + qz),
        ),
    )
    widen[...] = jnp.where(iota(shape, 0) == wanted, 1.0, 0.0).astype(jnp.bfloat16)
    for e in every:
        for i in range(NX + 2):
            if i in (0, NX + 1):
                e2[e, i] = jnp.zeros((NY + 16, NZ), jnp.float32)
            else:
                e2[e, i, 0:8] = jnp.zeros((8, NZ), jnp.float32)
                e2[e, i, NY + 8 : NY + 16] = jnp.zeros((8, NZ), jnp.float32)
    done(2)
    start(3)
    done(3)
    def spread(ref, index):
        place, y_of = iota((rows, nz), 1) // qz, iota((NY, nz), 0) % qy
        parts = [[] for _ in range(NX)]
        for t in range(NZ // nz):
            moved = []
            for k in range(groups):
                got = None
                for p in range(groups):
                    g = t * groups + (p - k) % groups
                    a = ref[g // cores, g % cores, index]
                    got = a if got is None else jnp.where(place == p, a, got)
                moved.append(roll(got, -k * qz, 1))
            for x in range(qx):
                if ngx != qy:
                    for y in range(qy):
                        mix[...] = moved[x * qy + y]
                        for g in range(ngx):
                            mixed[g, pl.ds(y, ngy, stride=qy), :] = mix[pl.ds(g, ngy, stride=ngx), :]
                for g in range(ngx):
                    if ngx != qy:
                        got = mixed[g]
                    else:
                        got = roll(moved[x * qy], -g, 0)
                        for y in range(1, qy):
                            got = jnp.where(y_of == y, roll(moved[x * qy + y], y - g, 0), got)
                    parts[g * qx + x].append(got)
        return [p[0] if len(p) == 1 else jnp.concatenate(p, axis=1) for p in parts]

    Y, Z = iota((NY, NZ), 0), iota((NY, NZ), 1)
    even_y, even_z = Y % 2 == 0, Z % 2 == 0
    pairs = NX // 4

    def halve(a):
        made = []
        for p in range(pairs):
            two = []
            for x in (2 * p, 2 * p + 1):
                c = a[2 * x] + a[2 * x + 1]
                two.append(c + jnp.where(even_y, roll(c, -1, 0), roll(c, 1, 0)))
            c = jnp.where(even_y, two[0], two[1])
            made.append(0.125 * (c + jnp.where(even_z, roll(c, -1, 1), roll(c, 1, 1))))
        return made

    def double(a, x):
        c = a[x // 4]
        if x // 2 % 2 == 0:
            return jnp.where(even_y, c, roll(c, 1, 0))
        return jnp.where(even_y, roll(c, -1, 0), c)

    def tree(terms):
        while len(terms) > 1:
            terms = [
                terms[k] + terms[k + 1] if k + 1 < len(terms) else terms[k]
                for k in range(0, len(terms), 2)
            ]
        return terms[0]

    def around2(w, v):
        made = []
        for x in range(NX):
            terms = [
                w[4][x] * roll(v[x], -1, 1), w[5][x] * roll(v[x], 1, 1),
                w[2][x] * roll(v[x], -1, 0), w[3][x] * roll(v[x], 1, 0),
            ]
            if x < NX - 1:
                terms.append(w[0][x] * v[x + 1])
            if x > 0:
                terms.append(w[1][x] * v[x - 1])
            made.append(tree(terms))
        return made

    def around3(w, v):
        made = []
        for p in range(pairs):
            up, down = roll(v[p], -1, 0), roll(v[p], 1, 0)
            if p < pairs - 1:
                up = jnp.where(even_y, up, roll(v[p + 1], 1, 0))
            if p > 0:
                down = jnp.where(even_y, roll(v[p - 1], -1, 0), down)
            made.append(tree([
                w[4][p] * roll(v[p], -2, 1), w[5][p] * roll(v[p], 2, 1),
                w[0][p] * up, w[1][p] * down,
                w[2][p] * roll(v[p], -2, 0), w[3][p] * roll(v[p], 2, 0),
            ]))
        return made

    def inner(w, k, at, last, step):
        if k == 0 and step == 2:
            return jnp.where(even_y, w, 0.0) if at == last else w
        if k == 1 and step == 2:
            return jnp.where(even_y, 0.0, w) if at == 0 else w
        if k < 2:
            return w
        return jnp.where((Y >= NY - step, Y < step, Z >= NZ - step, Z < step)[k - 2], 0.0, w)

    def constants_of(plain, diagonal, count, step):
        scaled, totals, weights = [], [], [[] for _ in range(6)]
        for at in range(count):
            total = diagonal[at] + tree([plain[k][at] for k in range(6)])
            scaled.append(DAMP / total)
            totals.append((1.0 / DAMP) * total)
            for k in range(6):
                weights[k].append(inner(scaled[at] * plain[k][at], k, at, count - 1, step))
        return scaled, totals, weights

    c2, t2, w2, c3, w3 = [], [], [], [], []
    for e in every:
        plain = [spread(wall, 6 * e + k) for k in range(6)]
        diagonal = spread(wall, 6 * EQ + e)
        scaled, totals, weights = constants_of(plain, diagonal, NX, 1)
        c2.append(scaled)
        t2.append(totals)
        w2.append(weights)
        coarse = [[0.25 * c for c in halve(plain[k])] for k in range(6)]
        scaled, _, weights = constants_of(coarse, halve(diagonal), pairs, 2)
        c3.append(scaled)
        w3.append(weights)

    arrive(plans[3]["v"])
    pltpu.make_async_copy(ball, ball, br_sem).wait()
    rhs = []
    for e in every:
        got = spread(ball, e)
        rhs.append([c2[e][x] * got[x] for x in range(NX)])

    def smooth2(v):
        made = []
        for e in every:
            sums = around2(w2[e], v[e])
            made.append([(KEEP * v[e][x] + rhs[e][x]) + sums[x] for x in range(NX)])
        return made

    v2 = rhs
    for step in range(SWEEPS - 1):
        v2 = smooth2(v2)
    rhs3 = []
    for e in every:
        sums = around2(w2[e], v2[e])
        got = halve([t2[e][x] * ((rhs[e][x] - DAMP * v2[e][x]) + sums[x]) for x in range(NX)])
        rhs3.append([c3[e][p] * got[p] for p in range(pairs)])
    v3 = rhs3
    for step in range(COARSE_SWEEPS - 1):
        sums = [around3(w3[e], v3[e]) for e in every]
        v3 = [
            [(KEEP * v3[e][p] + rhs3[e][p]) + sums[e][p] for p in range(pairs)] for e in every
        ]
    v2 = [[v2[e][x] + double(v3[e], x) for x in range(NX)] for e in every]
    for step in range(SWEEPS):
        v2 = smooth2(v2)
    for e in every:
        for x in range(NX):
            e2[e, x + 1, 8 : 8 + NY] = v2[e][x]

    wx, wy = qx + 2, qy + 2
    for e in every:
        for i in range(wx):
            for j in range(wy):
                at = (e * wx + i) * wy + j
                lines[at : at + 1, :] = e2[e, gx * qx + i, pl.ds(7 + gy * qy + j, 1), :]
    broad[...] = select(lines[...], widen[...])
    CENTER, BEYOND_Z, OUTSIDE_Z = range(3)
    ysel, yhalf = yi // 4, yi // 2 % 2

    def strip(kind, e, x, y):
        at = (e * wx + x + 1) * wy + y + 1
        return jnp.broadcast_to(broad[at : at + 1, kind * nz : kind * nz + nz], tile)

    def plane(kind, e, x):
        got = strip(kind, e, x, 0)
        for y in range(1, qy):
            got = jnp.where(ysel == y, strip(kind, e, x, y), got)
        return got

    def across_y(kind, e, x):
        got = None
        for y in range(qy):
            both = jnp.where(yhalf == 0, strip(kind, e, x, y - 1), strip(kind, e, x, y + 1))
            got = both if got is None else jnp.where(ysel == y, both, got)
        return got

    def across_x(kind, e, i):
        return plane(kind, e, i // 2 + (1 if i % 2 == 1 else -1))

    def rows_y(kind, e, x):
        return jnp.where(yi < ny // 2, strip(kind, e, x, -1), strip(kind, e, x, qy))

    left, behind, through = received(L1, 3, hx, hy, hz)
    mine = edge_rows(L1.s, *there["gy"])

    def add_x(side, e):
        face, near = (-1, 0) if side == 0 else (qx, qx - 1)
        got = left(side, e) + cox[side, e, 0] * plane(CENTER, e, face)
        got = got + cox[side, e, 1] * plane(CENTER, e, near)
        got = got + cox[side, e, 2] * across_y(CENTER, e, face)
        got = got + cox[side, e, 3] * plane(BEYOND_Z, e, face)
        return jnp.where(there["gx"][side], got, 0.0)

    def add_y(e, i):
        x = i // 2
        got = behind(e, i) + coy[e, 0, i] * rows_y(CENTER, e, x)
        got = got + coy[e, 1, i] * rows_y(CENTER, e, x + 1 if i % 2 == 1 else x - 1)
        got = got + coy[e, 2, i] * plane(CENTER, e, x)
        got = got + coy[e, 3, i] * rows_y(BEYOND_Z, e, x)
        return jnp.where(mine, got, 0.0)

    def add_z(e, i):
        x = i // 2
        got = through(e, i) + zco[e, 0, i] * plane(OUTSIDE_Z, e, x)
        got = got + zco[e, 1, i] * across_x(OUTSIDE_Z, e, i)
        got = got + zco[e, 2, i] * across_y(OUTSIDE_Z, e, x)
        return got + zco[e, 3, i] * plane(CENTER, e, x)

    swept = pfield.at[3]
    for e in every:
        for i in range(half):
            x = i // 2
            got = field[3, e, i] + co[e, 0, i] * plane(CENTER, e, x)
            got = got + co[e, 1, i] * across_x(CENTER, e, i)
            got = got + co[e, 2, i] * across_y(CENTER, e, x)
            swept[e, i] = got + co[e, 3, i] * plane(BEYOND_Z, e, x)
    get = lambda e, i: swept[e, i]
    halo = (add_x, add_y, add_z)
    u = planes(lambda e, i: KEEP * get(e, i) + border(L1, local(L1, get, e, i), halo, e, i), L1)
    put(4, L0, planes(lambda e, i: kept0[e, i] + u[e][i // 2], L0))
    finish = deep(4, L0)
    v, outer = finish()
    last = pfield.at[0]
    for e in every:
        for i in range(nx):
            last[e, i] = v[e][i]
    get = lambda e, i: last[e, i]
    q = planes(lambda e, i: KEEP * get(e, i) + local(L0, get, e, i), L0)
    halo = outer()
    for e in every:
        for i in range(nx):
            out_ref[e, i] = border(L0, q[e][i], halo, e, i)
    await_all(s_sem, [g for p in plans for g in p.values()] + constants + [spreads])
    for number in range(4):
        await_rows(ws_sem.at[number], stage_rows(number))
    await_rows(bs_sem, EQ * (rows * ngz - 1))


def per_device(dims, cores, couplings, diagonal, right_side, guess):
    ngx, ngy, ngz = dims
    brick = guess.shape[1:]
    nx, ny, nz = brick
    half = nx // 2
    qx, qy, qz = nx // 4, ny // 4, nz // 4
    rows = ngx * ngy
    nX = ngz // cores
    rounds = len(DEEP)
    f32 = jnp.float32
    vmem = pltpu.VMEM
    dma = pltpu.SemaphoreType.DMA

    def level(n):
        return [
            vmem((EQ, 6, n, ny, nz), f32),
            vmem((EQ, 2, n, ny, nz), f32),
            vmem((EQ, 2, ny, nz), f32),
            vmem((EQ, n, ny, nz), f32),
            vmem((EQ, n, ny, nz), f32),
            vmem((3, ny, nz), f32),
            vmem((2, EQ, ny, nz), f32),
            vmem((2, EQ, 2, ny, nz), f32),
            vmem((EQ, 2, n, ny, nz), f32),
            vmem((EQ, 2, ny, nz), f32),
            vmem((2, 3, ny, nz), f32),
            dma,
        ]

    faces = [
        vmem((rounds, 2, EQ, ny, nz), f32),
        vmem((rounds, EQ) + brick, f32),
        vmem((rounds, 2, ny, nz), f32),
    ]
    return pl.pallas_call(
        functools.partial(kernel, dims, cores),
        out_shape=vmem(guess.shape, f32),
        in_specs=[pl.BlockSpec(memory_space=pl.ANY)] * 4,
        out_specs=pl.BlockSpec(memory_space=vmem),
        scratch_shapes=[
            vmem(couplings.shape, f32),
            vmem(diagonal.shape, f32),
            vmem(right_side.shape, f32),
            vmem(guess.shape, f32),
            vmem((max(2048, nX * rows * 7 * EQ * (cores - 1) // 8, rows * (nX - 1) * 7 * EQ // 8), 8, nz), f32),
            vmem((rounds, EQ) + brick, f32),
            vmem((rounds, EQ) + brick, f32),
            vmem((rounds, 2, ny, nz), f32),
            *faces,
            *faces,
            vmem((rounds, 2, EQ, ny, nz), f32),
            vmem((rounds, 2, 2, ny, nz), f32),
            vmem((rounds, 2, ny, nz), f32),
            vmem((7 * EQ, half, ny, nz), f32),
            vmem((EQ, 4, half, ny, nz), f32),
            vmem((4, ny, nz), f32),
            vmem((2, EQ, 4, ny, nz), f32),
            vmem((EQ, 4, half, ny, nz), f32),
            vmem((2, 4, ny, nz), f32),
            vmem((EQ, 4, half, ny, nz), f32),
            *level(nx),
            *level(half),
            vmem((7 * EQ, ny, nz), f32),
            vmem((nX, cores, 7 * EQ, rows, nz), f32),
            vmem((EQ, ny, nz), f32),
            vmem((nX, cores, EQ, rows, nz), f32),
            vmem((EQ, ngx * qx + 2, ngy * qy + 16, ngz * qz), f32),
            vmem((EQ * (qx + 2) * (qy + 2), ngz * qz), f32),
            vmem((EQ * (qx + 2) * (qy + 2), 3 * nz), f32),
            vmem((ngz * qz, 3 * nz), jnp.bfloat16),
            vmem((rows, nz), f32),
            vmem((ngx, ngy * qy, nz), f32),
            dma,
            dma((rounds, 3)),
            dma,
            dma((4,)),
            dma((4,)),
            dma,
            dma,
            dma,
            dma((4,)),
            pltpu.SemaphoreType.REGULAR((2,)),
        ],
        compiler_params=pltpu.CompilerParams(
            collective_id=0, has_side_effects=True, vmem_limit_bytes=60 * 1024 * 1024
        ),
    )(couplings, diagonal, right_side, guess)


def solution(mesh):
    dims = (mesh.shape["gx"], mesh.shape["gy"], mesh.shape["gz"])
    cores = 2 if dims[2] % 2 == 0 else 1
    spec = P(None, "gx", "gy", "gz")
    return jax.shard_map(
        functools.partial(per_device, dims, cores),
        mesh=mesh,
        in_specs=(spec,) * 4,
        out_specs=spec,
        check_vma=False,
    )
```

```python
import functools

import jax
import jax.numpy as jnp
from jax import lax
from jax.experimental import pallas as pl
from jax.experimental.pallas import tpu as pltpu
from jax.sharding import PartitionSpec as P

SWEEPS = 2
COARSE_SWEEPS = 8
DAMP = 0.8
KEEP = 1.0 - DAMP
EQ = 3
MESH = pl.DeviceIdType.MESH
HIGH = lax.Precision.HIGHEST
DEEP = (False, True, True, False, True)
FINE = (True, True, False, False, True)


def roll(value, shift, axis):
    size = value.shape[axis]
    shift = shift % size
    return value if shift == 0 else pltpu.roll(value, shift, axis)


def iota(shape, axis):
    return lax.broadcasted_iota(jnp.int32, shape, axis)


class Level:
    def __init__(self, n, s, refs):
        self.n, self.s = n, s
        (self.cw, self.st, self.xw, self.cb, self.tot, self.zs,
         self.xt, self.xst, self.yst, self.yzs, self.yxw, self.zst, self.r_sem) = refs


def kernel(
    dims, cores, w_hbm, d_hbm, b_hbm, g_hbm, out_ref,
    w_ref, d_ref, b_ref, g_ref,
    tally, field, pfield, zpack, hx, hy, hz, px, py, pz, exy, exz, eyz, w1, co, cos, cox, coy, coz, zco, *rest,
):
    level_refs = (rest[:13], rest[13:26])
    (wsend, wall, bsend, ball, e2, lines, broad, widen, mix, mixed,
     s_sem, r_sem, co_sem, ws_sem, wr_sem, bs_sem, br_sem, i_sem, know) = rest[26:]
    ngx, ngy, ngz = dims
    nx, ny, nz = g_ref.shape[1:]
    half = nx // 2
    qx, qy, qz = nx // 4, ny // 4, nz // 4
    rows = ngx * ngy
    nX = ngz // cores
    gx, gy, gz = lax.axis_index("gx"), lax.axis_index("gy"), lax.axis_index("gz")
    X, core = gz // cores, gz % cores
    row = gy * ngx + gx
    axes = (("gx", gx, ngx), ("gy", gy, ngy), ("gz", gz, ngz))
    L0 = Level(nx, 1, level_refs[0])
    L1 = Level(half, 2, level_refs[1])
    tile = (ny, nz)
    yi, zi = iota(tile, 0), iota(tile, 1)
    every = range(EQ)

    def device(**change):
        here = {"gx": gx, "gy": gy, "gz": gz}
        here.update(change)
        return (here["gx"], here["gy"], here["gz"])

    guess_load = pltpu.make_async_copy(g_hbm, g_ref, i_sem.at[0])
    guess_load.start()
    barrier = pltpu.get_barrier_semaphore()
    close = ngy <= 4 and ngz <= 4
    awaited = 0

    def greet(ok, where):
        @pl.when(ok)
        def _():
            pl.semaphore_signal(barrier, inc=1, device_id=where, device_id_type=MESH)
        return ok.astype(jnp.int32)

    for name, index, count in axes:
        if close and name != "gx":
            steps = (-1, 1) if name == "gy" or cores == 1 else (-1, 1, -cores, cores)
            for step in steps:
                ok = (index + step >= 0) & (index + step < count)
                awaited = awaited + greet(ok, device(**{name: jnp.clip(index + step, 0, count - 1)}))
        else:
            for step in range(1, count):
                pl.semaphore_signal(
                    barrier, inc=1, device_id=device(**{name: (index + step) % count}),
                    device_id_type=MESH,
                )
            awaited = awaited + (count - 1)

    for a, z in ((w_hbm, w_ref), (d_hbm, d_ref), (b_hbm, b_ref)):
        pltpu.make_async_copy(a, z, i_sem.at[1]).start()

    there = {
        name: (index > 0, index < count - 1) for name, index, count in axes
    }
    beside = {
        name: (jnp.maximum(index - 1, 0), jnp.minimum(index + 1, count - 1))
        for name, index, count in axes
    }

    def edge_rows(s, lo, hi):
        return (yi < jnp.where(lo, s, 0)) | (yi >= jnp.where(hi, ny - s, ny))

    def remote(a, z, ss, rs, where):
        return pltpu.make_async_remote_copy(
            src_ref=a, dst_ref=z, send_sem=ss, recv_sem=rs,
            device_id=where, device_id_type=MESH,
        )

    def rows_of(side, s):
        return pl.ds(0 if side == 0 else ny - s, s)

    counts = [
        [k for k in (0, 1, 2) if (k > 0 or count == 1) and k < count and (k == 2 or count <= 2 or k == 1)]
        for _, _, count in axes
    ]
    found = [
        there[name][0].astype(jnp.int32) + there[name][1].astype(jnp.int32) for name, _, _ in axes
    ]
    cases = []
    for cx in counts[0]:
        for cy in counts[1]:
            for cz in counts[2]:
                cases.append(((cx, cy, cz), (found[0] == cx) & (found[1] == cy) & (found[2] == cz)))

    def await_rows(sem, number):
        if number > 0:
            part = next(k for k in (8, 4, 2, 1) if number % k == 0)
            ref = tally.at[pl.ds(0, number // part), pl.ds(0, part)]
            pltpu.make_async_copy(ref, ref, sem).wait()

    def await_all(sem, groups):
        for (cx, cy, cz), ok in cases:
            many = {"x": cx, "y": cy, "z": cz, "xy": cx * cy, "xz": cx * cz, "yz": cy * cz}
            number = sum(many[kind] * size for g in groups for kind, size in g.sizes.items())
            if len(cases) == 1:
                await_rows(sem, number)
            else:
                @pl.when(ok)
                def _():
                    await_rows(sem, number)

    class Group:
        def __init__(self, sem):
            self.sem, self.copies, self.sizes = sem, [], {}

        def add(self, kind, side, a, z, where, goes):
            self.copies.append((kind, remote(a, z, s_sem, self.sem, where), goes))
            if side == 0:
                size = 1
                for d in z.shape[:-1]:
                    size *= d
                self.sizes[kind] = self.sizes.get(kind, 0) + size

    def sides_of_x(n):
        if ngx == 2:
            return [(0, (1 - gx) * (n - 1), 1 - gx, gx, 1 - gx, True)]
        return [
            (side, 0 if side == 0 else n - 1, side, 1 - side, beside["gx"][side], there["gx"][side])
            for side in range(2)
        ]

    def both(a, b):
        return b if a is True else a & b

    def plan(r):
        n, s = (nx, 1) if FINE[r] else (half, 2)
        src = g_ref if r == 0 else field.at[r]
        groups = {k: Group(r_sem.at[r % 2 if k == "v" else 2 + r // 2 % 2]) for k in "vdp"}
        kinds = [("v", src, 0, hx, hy, hz)]
        if DEEP[r]:
            kinds.append(("p", pfield.at[r], 1, px, py, pz))
        for side, plane_at, _, other, to, ok in sides_of_x(n):
            for group, a, which, zx, zy, zz in kinds:
                groups[group].add("x", side, a.at[:, plane_at], zx.at[r, other], device(gx=to), ok)
        for side in range(2):
            other = 1 - side
            for group, a, which, zx, zy, zz in kinds:
                g = groups[group]
                g.add("y", side, a.at[:, 0:n, rows_of(side, s)], zy.at[r, :, 0:n, rows_of(other, s)],
                      device(gy=beside["gy"][side]), there["gy"][side])
                g.add("z", side, zpack.at[r, which], zz.at[r, other],
                      device(gz=beside["gz"][side]), there["gz"][side])
        if DEEP[r]:
            g = groups["d"]
            for i, plane_at, _, other, to, ok in sides_of_x(n):
                for j in range(2):
                    g.add("xy", 2 * i + j, src.at[:, plane_at, rows_of(j, s)],
                          exy.at[r, other, :, rows_of(1 - j, s)],
                          device(gx=to, gy=beside["gy"][j]), both(ok, there["gy"][j]))
                    g.add("xz", 2 * i + j, zpack.at[r, 0], exz.at[r, other, 1 - j],
                          device(gx=to, gz=beside["gz"][j]), both(ok, there["gz"][j]))
            for i in range(2):
                for j in range(2):
                    g.add("yz", 2 * i + j, zpack.at[r, 0, rows_of(i, s)], eyz.at[r, 1 - j, rows_of(1 - i, s)],
                          device(gy=beside["gy"][i], gz=beside["gz"][j]),
                          there["gy"][i] & there["gz"][j])
        return groups

    plans = [plan(r) for r in range(len(DEEP))]

    def plan_constants(L):
        g = Group(L.r_sem)
        for side, plane_at, mine, other, to, ok in sides_of_x(L.n):
            g.add("x", side, L.xw.at[:, mine], L.xt.at[other], device(gx=to), ok)
            g.add("x", side, L.st.at[:, :, plane_at], L.xst.at[other], device(gx=to), ok)
        for side in range(2):
            other = 1 - side
            y_at, y_ok = device(gy=beside["gy"][side]), there["gy"][side]
            g.add("y", side, L.st.at[:, 0, :, rows_of(side, L.s)],
                  L.yst.at[:, :, rows_of(other, L.s)], y_at, y_ok)
            g.add("y", side, L.zs.at[0, rows_of(side, L.s)], L.yzs.at[rows_of(other, L.s)], y_at, y_ok)
            g.add("y", side, L.xw.at[:, :, rows_of(side, L.s)], L.yxw.at[:, :, rows_of(other, L.s)], y_at, y_ok)
            g.add("z", side, L.zs, L.zst.at[other], device(gz=beside["gz"][side]), there["gz"][side])
        return g

    def plan_spreads():
        g = Group(co_sem)
        s = L1.s
        for side, plane_at, _, other, to, ok in sides_of_x(half):
            g.add("x", side, co.at[:, :, plane_at], cox.at[other], device(gx=to), ok)
        for side in range(2):
            other = 1 - side
            g.add("y", side, co.at[:, :, :, rows_of(side, s)], coy.at[:, :, :, rows_of(other, s)],
                  device(gy=beside["gy"][side]), there["gy"][side])
            g.add("z", side, cos, coz.at[other], device(gz=beside["gz"][side]), there["gz"][side])
        return g

    spreads = plan_spreads()
    constants = [plan_constants(L0), plan_constants(L1)]

    def begin(*groups, only=None):
        for g in groups:
            for kind, copy, goes in g.copies:
                if only is not None and kind not in only:
                    continue
                if goes is True:
                    copy.start()
                    continue

                @pl.when(goes)
                def _():
                    copy.start()

    def arrive(*groups):
        await_all(groups[0].sem, groups)

    def pack(L, get, planes=None):
        got = jnp.zeros(tile, jnp.float32)
        for e in every:
            for i in (range(L.n) if planes is None else planes):
                j = e * L.n + i
                got = jnp.where(zi // (2 * L.s) == j, roll(get(e, i), 2 * L.s * j + L.s, 1), got)
        return got

    def unpack(L, tile_of, e, i):
        return roll(tile_of, -(2 * L.s * (e * L.n + i) + L.s), 1)

    def combine(L, low, high, ok=None):
        s = L.s
        up = zi % (2 * s) < s
        has_low, has_high = there["gz"]
        if ok is not None:
            has_low, has_high = has_low & ok, has_high & ok
        code = jnp.where(up, jnp.where(has_high, 1, 0), jnp.where(has_low, 2, 0))
        return jnp.where(code == 1, roll(high, -s, 1), jnp.where(code == 2, roll(low, s, 1), 0.0))

    def local(L, get, e, i):
        n, s = L.n, L.s
        v = get(e, i)
        q = L.cw[e, 2, i] * roll(v, -s, 0) + L.cw[e, 3, i] * roll(v, s, 0)
        q = q + L.cw[e, 4, i] * roll(v, -s, 1) + L.cw[e, 5, i] * roll(v, s, 1)
        if i < n - 1:
            q = q + L.cw[e, 0, i] * get(e, i + 1)
        if i > 0:
            q = q + L.cw[e, 1, i] * get(e, i - 1)
        return q + L.cb[e, i]

    def border(L, q, halo, e, i):
        gx_of, gy_of, term_z = halo
        q = q + L.st[e, 0, i] * gy_of(e, i) + term_z(e, i)
        if i == 0:
            q = q + L.xw[e, 0] * gx_of(0, e)
        if i == L.n - 1:
            q = q + L.xw[e, 1] * gx_of(1, e)
        return q

    def ends(L, packed):
        at = (zi < L.s) | (zi >= nz - L.s)
        return lambda e, i: jnp.where(at, unpack(L, packed, e, i), 0.0)

    def received(L, r, x_ref, y_ref, z_ref):
        my = edge_rows(L.s, *there["gy"])
        c = combine(L, z_ref[r, 0], z_ref[r, 1])
        return (
            lambda side, e: jnp.where(there["gx"][side], x_ref[r, side, e], 0.0),
            lambda e, i: jnp.where(my, y_ref[r, e, i], 0.0),
            ends(L, L.zs[0] * c),
            c,
        )

    def ring(L, r, get, own):
        n, s = L.n, L.s
        my = edge_rows(s, *there["gy"])
        lines_of = []
        columns_of = []
        for side in range(2):
            ok = there["gx"][side]
            mask = edge_rows(s, ok & there["gy"][0], ok & there["gy"][1])
            lines_of.append([jnp.where(mask, exy[r, side, e], 0.0) for e in every])
            columns_of.append(combine(L, exz[r, side, 0], exz[r, side, 1], ok))
        cy = jnp.where(my, combine(L, eyz[r, 0], eyz[r, 1]), 0.0)
        rx = [
            [
                jnp.where(
                    there["gx"][side],
                    px[r, side, e] + L.xt[side, e] * get(e, 0 if side == 0 else n - 1)
                    + L.xst[side, e, 0] * lines_of[side][e]
                    + L.xst[side, e, 1] * unpack(L, columns_of[side], e, n - 1 if side == 0 else 0),
                    0.0,
                )
                for e in every
            ]
            for side in range(2)
        ]

        def ry(e, i):
            got = py[r, e, i] + L.yst[e, i] * get(e, i)
            if i == 0:
                got = got + L.yxw[e, 0] * lines_of[0][e]
            if i == n - 1:
                got = got + L.yxw[e, 1] * lines_of[1][e]
            return jnp.where(my, got, 0.0)

        far = 2 * s * (n - 1)
        sideways = jnp.where(
            zi // (2 * s) % n == 0, roll(columns_of[0], -far, 1), roll(columns_of[1], far, 1)
        )
        toward, along_y, along_x = [combine(L, L.zst[0, k], L.zst[1, k]) for k in range(3)]
        c = combine(L, pz[r, 0], pz[r, 1]) + toward * own + along_y * cy + along_x * sideways
        c = jnp.where(zi < 2 * s * EQ * n, c, 0.0)
        y_ends = L.zs[1] * jnp.where(my, L.yzs[...] * cy, 0.0)
        return (
            lambda side, e: rx[side][e],
            ry,
            ends(L, L.zs[0] * c + y_ends),
        )

    def put(r, L, v):
        for e in every:
            for i in range(L.n):
                field[r, e, i] = v[e][i]

    def planes(f, L):
        return [[f(e, i) for i in range(L.n)] for e in every]

    def deep(r, L):
        get = lambda e, i: field[r, e, i]
        begin(plans[r]["d"], only=("xy",))
        zpack[r, 0] = pack(L, get)
        begin(plans[r]["d"], only=("xz", "yz"))
        begin(plans[r]["v"])
        for e in every:
            for i in range(L.n):
                pfield[r, e, i] = KEEP * get(e, i) + local(L, get, e, i)
        zpack[r, 1] = pack(L, lambda e, i: pfield[r, e, i])
        begin(plans[r]["p"])

        def finish():
            arrive(plans[r]["v"])
            halo = received(L, r, hx, hy, hz)[:3]
            new = planes(lambda e, i: border(L, pfield[r, e, i], halo, e, i), L)

            def outer():
                arrive(plans[r]["d"], plans[r]["p"])
                return ring(L, r, get, zpack[r, 0])

            return new, outer

        return finish

    def coarsen(a, s):
        n = a.shape[0]
        a = jnp.stack([a[2 * i] + a[2 * i + 1] for i in range(n // 2)])
        y, z = iota(a.shape, 1), iota(a.shape, 2)
        a = a + jnp.where((y // s) % 2 == 0, roll(a, -s, 1), roll(a, s, 1))
        a = a + jnp.where((z // s) % 2 == 0, roll(a, -s, 2), roll(a, s, 2))
        return a * 0.125

    def select(a, onehot):
        parts = []
        for _ in range(3):
            parts.append(a.astype(jnp.bfloat16))
            a = a - parts[-1].astype(jnp.float32)
        got = jnp.dot(jnp.concatenate(parts, axis=0), onehot, preferred_element_type=jnp.float32)
        m = a.shape[0]
        return (got[0:m] + got[m : 2 * m]) + got[2 * m :]

    groups = qx * qy
    source = iota((nz, nz), 0)
    target = iota((nz, nz), 1)
    squeeze = jnp.where(source == 4 * (target % qz), 1.0, 0.0).astype(jnp.bfloat16)

    def to_rows(a):
        m = a.shape[0]
        c = select(a.reshape(m * qx * ny, nz), squeeze).reshape(m, qx, ny, nz)
        place = iota((m, ny, nz), 2) // qz
        got = jnp.zeros((m, ny, nz), jnp.float32)
        for x in range(qx):
            for y in range(qy):
                part = roll(c[:, x], -4 * y, 1)
                got = jnp.where(place == (x * qy + y + gz) % groups, part, got)
        return got

    def own(small, whole, sem):
        return pltpu.make_async_copy(
            small.at[:, pl.ds(0, 1)], whole.at[X, core, :, pl.ds(row, 1)], sem
        )

    def stage(number, small, whole, rs):
        made = []
        if number == 0:
            for step in range(1, ngx):
                made.append((small.at[:, pl.ds(0, 1)], whole.at[X, core, :, pl.ds(row, 1)],
                             step, device(gx=(gx + step) % ngx)))
        elif number == 1:
            block = whole.at[X, core, :, pl.ds(gy * ngx, ngx)]
            for step in range(1, ngy):
                made.append((block, block, step, device(gy=(gy + step) % ngy)))
        elif number == 2:
            block = whole.at[X, core]
            for step in range(1, nX):
                made.append((block, block, step, device(gz=((X + step) % nX) * cores + core)))
        else:
            block = whole.at[:, core]
            for step in range(1, cores):
                made.append((block, block, step, device(gz=X * cores + (core + step) % cores)))
        return [
            remote(a, z, ws_sem.at[number], rs.at[number], where)
            for a, z, _, where in made
        ]

    wargs = (wsend, wall, wr_sem)

    def everyone():
        mirrored = all(count & (count - 1) == 0 for count in dims)

        def other(index, step, count):
            return index ^ step if mirrored else (index + step) % count

        made = []
        for ay in reversed(range(ngy)):
            for az in reversed(range(ngz)):
                for ax in reversed(range(ngx)):
                    if ax + ay + az == 0:
                        continue
                    made.append(remote(
                        bsend.at[:, pl.ds(0, 1)], ball.at[X, core, :, pl.ds(row, 1)],
                        bs_sem, br_sem,
                        (other(gx, ax, ngx), other(gy, ay, ngy), other(gz, az, ngz)),
                    ))
        return made

    def start(number):
        for copy in stage(number, *wargs):
            copy.start()

    def stage_rows(number):
        return 7 * EQ * (
            ngx - 1, ngx * (ngy - 1), rows * (nX - 1), nX * rows * (cores - 1)
        )[number]

    def done(number):
        await_rows(wr_sem.at[number], stage_rows(number))

    def scale(L, get_w, get_d, e, i):
        n, s = L.n, L.s
        raw = [get_w(e, k, i) for k in range(6)]
        total = get_d(e, i)
        for k in range(6):
            total = total + raw[k]
        c = DAMP / total
        w = [c * raw[k] for k in range(6)]
        L.tot[e, i] = (1.0 / DAMP) * total
        last_y, first_y, last_z, first_z = yi >= ny - s, yi < s, zi >= nz - s, zi < s
        L.cw[e, 0, i] = w[0]
        L.cw[e, 1, i] = w[1]
        L.cw[e, 2, i] = jnp.where(last_y, 0.0, w[2])
        L.cw[e, 3, i] = jnp.where(first_y, 0.0, w[3])
        L.cw[e, 4, i] = jnp.where(last_z, 0.0, w[4])
        L.cw[e, 5, i] = jnp.where(first_z, 0.0, w[5])
        L.st[e, 0, i] = jnp.where(last_y, w[2], jnp.where(first_y, w[3], 0.0))
        L.st[e, 1, i] = jnp.where(last_z, w[4], jnp.where(first_z, w[5], 0.0))
        if i == 0:
            L.xw[e, 0] = w[1]
        if i == n - 1:
            L.xw[e, 1] = w[0]
        if L is L1:
            odd_y, odd_z = yi // s % 2 == 1, zi // s % 2 == 1
            co[e, 1, i] = w[0] if i % 2 == 1 else w[1]
            co[e, 2, i] = jnp.where(odd_y, w[2], w[3])
            co[e, 3, i] = jnp.where(odd_z, w[4], w[5])
            co[e, 0, i] = (
                KEEP + (w[1] if i % 2 == 1 else w[0])
                + jnp.where(odd_y, w[3], w[2]) + jnp.where(odd_z, w[5], w[4])
            )
        return c

    def pack_constants(L):
        L.zs[0] = pack(L, lambda e, i: L.st[e, 1, i])
        L.zs[1] = pack(L, lambda e, i: L.st[e, 0, i])
        L.zs[2] = pack(L, lambda e, i: L.xw[e, 0 if i == 0 else 1], (0, L.n - 1))

    guess_load.wait()
    guess = lambda e, i: g_ref[e, i]
    zpack[0, 0] = pack(L0, guess)
    pl.semaphore_wait(barrier, awaited)
    begin(plans[0]["v"])
    hear = there["gy"][0].astype(jnp.int32) + there["gy"][1].astype(jnp.int32)

    def tell(k):
        for side in range(2):
            @pl.when(there["gy"][side])
            def _():
                pl.semaphore_signal(
                    know.at[k], inc=1, device_id=device(gy=beside["gy"][side]), device_id_type=MESH
                )

    if close:
        tell(0)
    await_rows(i_sem.at[1], 8 * EQ * nx * ny)
    level2 = [None] * (7 * EQ)
    for e in every:
        d1 = coarsen(d_ref[e], 1)
        level2[6 * EQ + e] = coarsen(d1, 2)
        for k in range(6):
            w = 0.25 * coarsen(w_ref[6 * e + k], 1)
            w1[6 * e + k] = w
            level2[6 * e + k] = 0.25 * coarsen(w, 2)
        for i in range(half):
            c = scale(L1, lambda e, k, i: w1[6 * e + k, i], lambda e, i: d1[i], e, i)
            w1[6 * EQ + e, i] = c
    wsend[...] = to_rows(jnp.stack(level2))
    own(wsend, wall, i_sem.at[0]).start()
    start(0)
    for e in every:
        for i in range(nx):
            c = scale(L0, lambda e, k, i: w_ref[6 * e + k, i], lambda e, i: d_ref[e, i], e, i)
            L0.cb[e, i] = c * b_ref[e, i]
    pack_constants(L0)
    begin(constants[0])
    for e in every:
        for i in range(nx):
            pfield[0, e, i] = KEEP * guess(e, i) + local(L0, guess, e, i)
    if close:
        pl.semaphore_wait(know.at[0], hear)
        tell(1)

    arrive(plans[0]["v"])
    halo = received(L0, 0, hx, hy, hz)[:3]
    put(1, L0, planes(lambda e, i: border(L0, pfield[0, e, i], halo, e, i), L0))
    finish = deep(1, L0)
    own(wsend, wall, i_sem.at[0]).wait()
    done(0)
    if close:
        pl.semaphore_wait(know.at[1], hear)
    start(1)
    pack_constants(L1)
    begin(constants[1])
    v, outer = finish()
    kept0 = field.at[0]
    for e in every:
        for i in range(nx):
            kept0[e, i] = v[e][i]
    get = lambda e, i: kept0[e, i]
    q = planes(lambda e, i: local(L0, get, e, i), L0)
    arrive(constants[0])
    halo = outer()
    first = []
    for e in every:
        r = jnp.stack([
            L0.tot[e, i] * (border(L0, q[e][i], halo, e, i) - DAMP * get(e, i)) for i in range(nx)
        ])
        b = coarsen(r, 1)
        first.append([])
        for i in range(half):
            u = w1[6 * EQ + e, i] * b[i]
            L1.cb[e, i] = u
            first[e].append(u)
    put(2, L1, first)
    finish = deep(2, L1)
    done(1)
    start(2)
    for m in range(4):
        cos[m] = pack(L1, lambda e, i: co[e, m, i])
    begin(spreads)
    u, outer = finish()
    kept1 = pfield.at[3]
    for e in every:
        for i in range(half):
            kept1[e, i] = u[e][i]
    get = lambda e, i: kept1[e, i]
    q = planes(lambda e, i: local(L1, get, e, i), L1)
    arrive(constants[1])
    halo = outer()
    rest = []
    for e in every:
        r = []
        for i in range(half):
            total = border(L1, q[e][i], halo, e, i)
            field[3, e, i] = KEEP * get(e, i) + total
            r.append(L1.tot[e, i] * (total - DAMP * get(e, i)))
        rest.append(coarsen(jnp.stack(r), 2))
    bsend[...] = to_rows(jnp.stack(rest))
    for copy in everyone():
        copy.start()
    own(bsend, ball, br_sem).start()
    zpack[3, 0] = pack(L1, lambda e, i: field[3, e, i])
    begin(plans[3]["v"])
    arrive(spreads)
    for m in range(4):
        c = combine(L1, coz[0, m], coz[1, m])
        for e in every:
            for i in range(half):
                zco[e, m, i] = unpack(L1, c, e, i)
    NX, NY, NZ = ngx * qx, ngy * qy, ngz * qz
    shape = (NZ, 3 * nz)
    kind, t = iota(shape, 1) // nz, iota(shape, 1) % nz
    base = gz * qz + t // 4
    wanted = jnp.where(
        kind == 0, base,
        jnp.where(
            kind == 1, base + jnp.where(t % 4 < 2, -1, 1),
            jnp.where(t < nz // 2, gz * qz - 1, gz * qz + qz),
        ),
    )
    widen[...] = jnp.where(iota(shape, 0) == wanted, 1.0, 0.0).astype(jnp.bfloat16)
    for e in every:
        for i in range(NX + 2):
            if i in (0, NX + 1):
                e2[e, i] = jnp.zeros((NY + 16, NZ), jnp.float32)
            else:
                e2[e, i, 0:8] = jnp.zeros((8, NZ), jnp.float32)
                e2[e, i, NY + 8 : NY + 16] = jnp.zeros((8, NZ), jnp.float32)
    done(2)
    start(3)
    done(3)
    def spread(ref, index):
        place, y_of = iota((rows, nz), 1) // qz, iota((NY, nz), 0) % qy
        parts = [[] for _ in range(NX)]
        for t in range(NZ // nz):
            moved = []
            for k in range(groups):
                got = None
                for p in range(groups):
                    g = t * groups + (p - k) % groups
                    a = ref[g // cores, g % cores, index]
                    got = a if got is None else jnp.where(place == p, a, got)
                moved.append(roll(got, -k * qz, 1))
            for x in range(qx):
                if ngx != qy:
                    for y in range(qy):
                        mix[...] = moved[x * qy + y]
                        for g in range(ngx):
                            mixed[g, pl.ds(y, ngy, stride=qy), :] = mix[pl.ds(g, ngy, stride=ngx), :]
                for g in range(ngx):
                    if ngx != qy:
                        got = mixed[g]
                    else:
                        got = roll(moved[x * qy], -g, 0)
                        for y in range(1, qy):
                            got = jnp.where(y_of == y, roll(moved[x * qy + y], y - g, 0), got)
                    parts[g * qx + x].append(got)
        return [p[0] if len(p) == 1 else jnp.concatenate(p, axis=1) for p in parts]

    Y, Z = iota((NY, NZ), 0), iota((NY, NZ), 1)
    even_y, even_z = Y % 2 == 0, Z % 2 == 0
    pairs = NX // 4

    def halve(a):
        made = []
        for p in range(pairs):
            two = []
            for x in (2 * p, 2 * p + 1):
                c = a[2 * x] + a[2 * x + 1]
                two.append(c + jnp.where(even_y, roll(c, -1, 0), roll(c, 1, 0)))
            c = jnp.where(even_y, two[0], two[1])
            made.append(0.125 * (c + jnp.where(even_z, roll(c, -1, 1), roll(c, 1, 1))))
        return made

    def double(a, x):
        c = a[x // 4]
        if x // 2 % 2 == 0:
            return jnp.where(even_y, c, roll(c, 1, 0))
        return jnp.where(even_y, roll(c, -1, 0), c)

    def tree(terms):
        while len(terms) > 1:
            terms = [
                terms[k] + terms[k + 1] if k + 1 < len(terms) else terms[k]
                for k in range(0, len(terms), 2)
            ]
        return terms[0]

    def around2(w, v):
        made = []
        for x in range(NX):
            terms = [
                w[4][x] * roll(v[x], -1, 1), w[5][x] * roll(v[x], 1, 1),
                w[2][x] * roll(v[x], -1, 0), w[3][x] * roll(v[x], 1, 0),
            ]
            if x < NX - 1:
                terms.append(w[0][x] * v[x + 1])
            if x > 0:
                terms.append(w[1][x] * v[x - 1])
            made.append(tree(terms))
        return made

    def around3(w, v):
        made = []
        for p in range(pairs):
            up, down = roll(v[p], -1, 0), roll(v[p], 1, 0)
            if p < pairs - 1:
                up = jnp.where(even_y, up, roll(v[p + 1], 1, 0))
            if p > 0:
                down = jnp.where(even_y, roll(v[p - 1], -1, 0), down)
            made.append(tree([
                w[4][p] * roll(v[p], -2, 1), w[5][p] * roll(v[p], 2, 1),
                w[0][p] * up, w[1][p] * down,
                w[2][p] * roll(v[p], -2, 0), w[3][p] * roll(v[p], 2, 0),
            ]))
        return made

    steps3 = ((-1, 0), (1, 0), (-2, 0), (2, 0), (0, -2), (0, 2))

    def shifted(v, dr, dl):
        return roll(roll(v, dl, 1), dr, 0)

    def twice(w):
        got = {(0, 0): KEEP * KEEP}

        def add(at, value):
            at = (at[0] % NY, at[1] % NZ)
            got[at] = got[at] + value if at in got else value

        for k, (dr, dl) in enumerate(steps3):
            add((dr, dl), 2.0 * KEEP * w[k])
            for m, (er, el) in enumerate(steps3):
                if k == m and k < 2:
                    continue
                add((dr + er, dl + el), w[k] * shifted(w[m], dr, dl))
        return got

    def apply_twice(w, v):
        turned = {dl: roll(v, dl, 1) for dl in sorted({at[1] for at in w})}
        return tree([c * roll(turned[dl], dr, 0) for (dr, dl), c in w.items()])

    def inner(w, k, at, last, step):
        if k == 0 and step == 2:
            return jnp.where(even_y, w, 0.0) if at == last else w
        if k == 1 and step == 2:
            return jnp.where(even_y, 0.0, w) if at == 0 else w
        if k < 2:
            return w
        return jnp.where((Y >= NY - step, Y < step, Z >= NZ - step, Z < step)[k - 2], 0.0, w)

    def constants_of(plain, diagonal, count, step):
        scaled, totals, weights = [], [], [[] for _ in range(6)]
        for at in range(count):
            total = diagonal[at] + tree([plain[k][at] for k in range(6)])
            scaled.append(DAMP / total)
            totals.append((1.0 / DAMP) * total)
            for k in range(6):
                weights[k].append(inner(scaled[at] * plain[k][at], k, at, count - 1, step))
        return scaled, totals, weights

    c2, t2, w2, c3, w3, ww3 = [], [], [], [], [], []
    by_two = pairs == 1 and NY >= 8 and COARSE_SWEEPS % 2 == 0
    for e in every:
        plain = [spread(wall, 6 * e + k) for k in range(6)]
        diagonal = spread(wall, 6 * EQ + e)
        scaled, totals, weights = constants_of(plain, diagonal, NX, 1)
        c2.append(scaled)
        t2.append(totals)
        w2.append(weights)
        coarse = [[0.25 * c for c in halve(plain[k])] for k in range(6)]
        scaled, _, weights = constants_of(coarse, halve(diagonal), pairs, 2)
        c3.append(scaled)
        w3.append(weights)
        if by_two:
            ww3.append(twice([weights[k][0] for k in range(6)]))

    arrive(plans[3]["v"])
    pltpu.make_async_copy(ball, ball, br_sem).wait()
    rhs = []
    for e in every:
        got = spread(ball, e)
        rhs.append([c2[e][x] * got[x] for x in range(NX)])

    def smooth2(v):
        made = []
        for e in every:
            sums = around2(w2[e], v[e])
            made.append([(KEEP * v[e][x] + rhs[e][x]) + sums[x] for x in range(NX)])
        return made

    v2 = rhs
    for step in range(SWEEPS - 1):
        v2 = smooth2(v2)
    rhs3 = []
    for e in every:
        sums = around2(w2[e], v2[e])
        got = halve([t2[e][x] * ((rhs[e][x] - DAMP * v2[e][x]) + sums[x]) for x in range(NX)])
        rhs3.append([c3[e][p] * got[p] for p in range(pairs)])
    v3 = rhs3
    for step in range(1 if by_two else COARSE_SWEEPS - 1):
        sums = [around3(w3[e], v3[e]) for e in every]
        v3 = [
            [(KEEP * v3[e][p] + rhs3[e][p]) + sums[e][p] for p in range(pairs)] for e in every
        ]
    if by_two:
        once = v3
        for step in range(COARSE_SWEEPS // 2 - 1):
            v3 = [[apply_twice(ww3[e], v3[e][0]) + once[e][0]] for e in every]
    v2 = [[v2[e][x] + double(v3[e], x) for x in range(NX)] for e in every]
    for step in range(SWEEPS):
        v2 = smooth2(v2)
    for e in every:
        for x in range(NX):
            e2[e, x + 1, 8 : 8 + NY] = v2[e][x]

    wx, wy = qx + 2, qy + 2
    for e in every:
        for i in range(wx):
            for j in range(wy):
                at = (e * wx + i) * wy + j
                lines[at : at + 1, :] = e2[e, gx * qx + i, pl.ds(7 + gy * qy + j, 1), :]
    broad[...] = select(lines[...], widen[...])
    CENTER, BEYOND_Z, OUTSIDE_Z = range(3)
    ysel, yhalf = yi // 4, yi // 2 % 2

    def strip(kind, e, x, y):
        at = (e * wx + x + 1) * wy + y + 1
        return jnp.broadcast_to(broad[at : at + 1, kind * nz : kind * nz + nz], tile)

    def plane(kind, e, x):
        got = strip(kind, e, x, 0)
        for y in range(1, qy):
            got = jnp.where(ysel == y, strip(kind, e, x, y), got)
        return got

    def across_y(kind, e, x):
        got = None
        for y in range(qy):
            both = jnp.where(yhalf == 0, strip(kind, e, x, y - 1), strip(kind, e, x, y + 1))
            got = both if got is None else jnp.where(ysel == y, both, got)
        return got

    def across_x(kind, e, i):
        return plane(kind, e, i // 2 + (1 if i % 2 == 1 else -1))

    def rows_y(kind, e, x):
        return jnp.where(yi < ny // 2, strip(kind, e, x, -1), strip(kind, e, x, qy))

    left, behind, _, columns = received(L1, 3, hx, hy, hz)
    mine = edge_rows(L1.s, *there["gy"])

    def add_x(side, e):
        face, near = (-1, 0) if side == 0 else (qx, qx - 1)
        got = left(side, e) + cox[side, e, 0] * plane(CENTER, e, face)
        got = got + cox[side, e, 1] * plane(CENTER, e, near)
        got = got + cox[side, e, 2] * across_y(CENTER, e, face)
        got = got + cox[side, e, 3] * plane(BEYOND_Z, e, face)
        return jnp.where(there["gx"][side], got, 0.0)

    def add_y(e, i):
        x = i // 2
        got = behind(e, i) + coy[e, 0, i] * rows_y(CENTER, e, x)
        got = got + coy[e, 1, i] * rows_y(CENTER, e, x + 1 if i % 2 == 1 else x - 1)
        got = got + coy[e, 2, i] * plane(CENTER, e, x)
        got = got + coy[e, 3, i] * rows_y(BEYOND_Z, e, x)
        return jnp.where(mine, got, 0.0)

    def add_z(e, i):
        x = i // 2
        got = unpack(L1, columns, e, i) + zco[e, 0, i] * plane(OUTSIDE_Z, e, x)
        got = got + zco[e, 1, i] * across_x(OUTSIDE_Z, e, i)
        got = got + zco[e, 2, i] * across_y(OUTSIDE_Z, e, x)
        return L1.st[e, 1, i] * (got + zco[e, 3, i] * plane(CENTER, e, x))

    swept = pfield.at[3]
    for e in every:
        for i in range(half):
            x = i // 2
            got = field[3, e, i] + co[e, 0, i] * plane(CENTER, e, x)
            got = got + co[e, 1, i] * across_x(CENTER, e, i)
            got = got + co[e, 2, i] * across_y(CENTER, e, x)
            swept[e, i] = got + co[e, 3, i] * plane(BEYOND_Z, e, x)
    get = lambda e, i: swept[e, i]
    halo = (add_x, add_y, add_z)
    u = planes(lambda e, i: KEEP * get(e, i) + border(L1, local(L1, get, e, i), halo, e, i), L1)
    put(4, L0, planes(lambda e, i: kept0[e, i] + u[e][i // 2], L0))
    finish = deep(4, L0)
    v, outer = finish()
    last = pfield.at[0]
    for e in every:
        for i in range(nx):
            last[e, i] = v[e][i]
    get = lambda e, i: last[e, i]
    q = planes(lambda e, i: KEEP * get(e, i) + local(L0, get, e, i), L0)
    halo = outer()
    for e in every:
        for i in range(nx):
            out_ref[e, i] = border(L0, q[e][i], halo, e, i)
    await_all(s_sem, [g for p in plans for g in p.values()] + constants + [spreads])
    for number in range(4):
        await_rows(ws_sem.at[number], stage_rows(number))
    await_rows(bs_sem, EQ * (rows * ngz - 1))


def per_device(dims, cores, couplings, diagonal, right_side, guess):
    ngx, ngy, ngz = dims
    brick = guess.shape[1:]
    nx, ny, nz = brick
    half = nx // 2
    qx, qy, qz = nx // 4, ny // 4, nz // 4
    rows = ngx * ngy
    nX = ngz // cores
    rounds = len(DEEP)
    f32 = jnp.float32
    vmem = pltpu.VMEM
    dma = pltpu.SemaphoreType.DMA

    def level(n):
        return [
            vmem((EQ, 6, n, ny, nz), f32),
            vmem((EQ, 2, n, ny, nz), f32),
            vmem((EQ, 2, ny, nz), f32),
            vmem((EQ, n, ny, nz), f32),
            vmem((EQ, n, ny, nz), f32),
            vmem((3, ny, nz), f32),
            vmem((2, EQ, ny, nz), f32),
            vmem((2, EQ, 2, ny, nz), f32),
            vmem((EQ, n, ny, nz), f32),
            vmem((ny, nz), f32),
            vmem((EQ, 2, ny, nz), f32),
            vmem((2, 3, ny, nz), f32),
            dma,
        ]

    faces = [
        vmem((rounds, 2, EQ, ny, nz), f32),
        vmem((rounds, EQ) + brick, f32),
        vmem((rounds, 2, ny, nz), f32),
    ]
    return pl.pallas_call(
        functools.partial(kernel, dims, cores),
        out_shape=vmem(guess.shape, f32),
        in_specs=[pl.BlockSpec(memory_space=pl.ANY)] * 4,
        out_specs=pl.BlockSpec(memory_space=vmem),
        scratch_shapes=[
            vmem(couplings.shape, f32),
            vmem(diagonal.shape, f32),
            vmem(right_side.shape, f32),
            vmem(guess.shape, f32),
            vmem((max(2048, nX * rows * 7 * EQ * (cores - 1) // 8, rows * (nX - 1) * 7 * EQ // 8), 8, nz), f32),
            vmem((rounds, EQ) + brick, f32),
            vmem((rounds, EQ) + brick, f32),
            vmem((rounds, 2, ny, nz), f32),
            *faces,
            *faces,
            vmem((rounds, 2, EQ, ny, nz), f32),
            vmem((rounds, 2, 2, ny, nz), f32),
            vmem((rounds, 2, ny, nz), f32),
            vmem((7 * EQ, half, ny, nz), f32),
            vmem((EQ, 4, half, ny, nz), f32),
            vmem((4, ny, nz), f32),
            vmem((2, EQ, 4, ny, nz), f32),
            vmem((EQ, 4, half, ny, nz), f32),
            vmem((2, 4, ny, nz), f32),
            vmem((EQ, 4, half, ny, nz), f32),
            *level(nx),
            *level(half),
            vmem((7 * EQ, ny, nz), f32),
            vmem((nX, cores, 7 * EQ, rows, nz), f32),
            vmem((EQ, ny, nz), f32),
            vmem((nX, cores, EQ, rows, nz), f32),
            vmem((EQ, ngx * qx + 2, ngy * qy + 16, ngz * qz), f32),
            vmem((EQ * (qx + 2) * (qy + 2), ngz * qz), f32),
            vmem((EQ * (qx + 2) * (qy + 2), 3 * nz), f32),
            vmem((ngz * qz, 3 * nz), jnp.bfloat16),
            vmem((rows, nz), f32),
            vmem((ngx, ngy * qy, nz), f32),
            dma,
            dma((4,)),
            dma,
            dma((4,)),
            dma((4,)),
            dma,
            dma,
            dma((2,)),
            pltpu.SemaphoreType.REGULAR((2,)),
        ],
        compiler_params=pltpu.CompilerParams(
            collective_id=0, has_side_effects=True, vmem_limit_bytes=60 * 1024 * 1024
        ),
    )(couplings, diagonal, right_side, guess)


def solution(mesh):
    dims = (mesh.shape["gx"], mesh.shape["gy"], mesh.shape["gz"])
    cores = 2 if dims[2] % 2 == 0 else 1
    spec = P(None, "gx", "gy", "gz")
    return jax.shard_map(
        functools.partial(per_device, dims, cores),
        mesh=mesh,
        in_specs=(spec,) * 4,
        out_specs=spec,
        check_vma=False,
    )
```

```python
import functools

import jax
import jax.numpy as jnp
from jax import lax
from jax.experimental import pallas as pl
from jax.experimental.pallas import tpu as pltpu
from jax.sharding import PartitionSpec as P

SWEEPS = 2
COARSE_SWEEPS = 8
DAMP = 0.8
KEEP = 1.0 - DAMP
EQ = 3
MESH = pl.DeviceIdType.MESH
HIGH = lax.Precision.HIGHEST
DEEP = (False, True, True, False, True)
FINE = (True, True, False, False, True)


def roll(value, shift, axis):
    size = value.shape[axis]
    shift = shift % size
    return value if shift == 0 else pltpu.roll(value, shift, axis)


def iota(shape, axis):
    return lax.broadcasted_iota(jnp.int32, shape, axis)


class Level:
    def __init__(self, n, s, refs):
        self.n, self.s = n, s
        (self.cw, self.st, self.xw, self.cb, self.tot, self.zs,
         self.xt, self.xst, self.yst, self.yzs, self.yxw, self.zst, self.r_sem) = refs


def kernel(
    dims, cores, w_hbm, d_hbm, b_hbm, g_hbm, out_ref,
    w_ref, d_ref, b_ref, g_ref,
    tally, field, pfield, zpack, hx, hy, hz, px, py, pz, exy, exz, eyz, w1, co, cos, cox, coy, coz, zco, *rest,
):
    level_refs = (rest[:13], rest[13:26])
    (wsend, wall, bsend, ball, e2, lines, broad, widen, mix, mixed,
     s_sem, r_sem, co_sem, ws_sem, wr_sem, bs_sem, br_sem, i_sem, g_sem, know) = rest[26:]
    ngx, ngy, ngz = dims
    nx, ny, nz = g_ref.shape[1:]
    half = nx // 2
    qx, qy, qz = nx // 4, ny // 4, nz // 4
    rows = ngx * ngy
    nX = ngz // cores
    gx, gy, gz = lax.axis_index("gx"), lax.axis_index("gy"), lax.axis_index("gz")
    X, core = gz // cores, gz % cores
    row = gy * ngx + gx
    axes = (("gx", gx, ngx), ("gy", gy, ngy), ("gz", gz, ngz))
    L0 = Level(nx, 1, level_refs[0])
    L1 = Level(half, 2, level_refs[1])
    tile = (ny, nz)
    yi, zi = iota(tile, 0), iota(tile, 1)
    every = range(EQ)

    def device(**change):
        here = {"gx": gx, "gy": gy, "gz": gz}
        here.update(change)
        return (here["gx"], here["gy"], here["gz"])

    guess_loads = [pltpu.make_async_copy(g_hbm.at[e], g_ref.at[e], g_sem.at[e]) for e in range(EQ)]
    for load in guess_loads:
        load.start()
    barrier = pltpu.get_barrier_semaphore()
    close = ngy <= 4 and ngz <= 4
    awaited = 0

    def greet(ok, where):
        @pl.when(ok)
        def _():
            pl.semaphore_signal(barrier, inc=1, device_id=where, device_id_type=MESH)
        return ok.astype(jnp.int32)

    for name, index, count in axes:
        if close and name != "gx":
            steps = (-1, 1) if name == "gy" or cores == 1 else (-1, 1, -cores, cores)
            for step in steps:
                ok = (index + step >= 0) & (index + step < count)
                awaited = awaited + greet(ok, device(**{name: jnp.clip(index + step, 0, count - 1)}))
        else:
            for step in range(1, count):
                pl.semaphore_signal(
                    barrier, inc=1, device_id=device(**{name: (index + step) % count}),
                    device_id_type=MESH,
                )
            awaited = awaited + (count - 1)

    for a, z in ((w_hbm, w_ref), (d_hbm, d_ref), (b_hbm, b_ref)):
        pltpu.make_async_copy(a, z, i_sem.at[1]).start()

    there = {
        name: (index > 0, index < count - 1) for name, index, count in axes
    }
    beside = {
        name: (jnp.maximum(index - 1, 0), jnp.minimum(index + 1, count - 1))
        for name, index, count in axes
    }

    def edge_rows(s, lo, hi):
        return (yi < jnp.where(lo, s, 0)) | (yi >= jnp.where(hi, ny - s, ny))

    def remote(a, z, ss, rs, where):
        return pltpu.make_async_remote_copy(
            src_ref=a, dst_ref=z, send_sem=ss, recv_sem=rs,
            device_id=where, device_id_type=MESH,
        )

    def rows_of(side, s):
        return pl.ds(0 if side == 0 else ny - s, s)

    counts = [
        [k for k in (0, 1, 2) if (k > 0 or count == 1) and k < count and (k == 2 or count <= 2 or k == 1)]
        for _, _, count in axes
    ]
    found = [
        there[name][0].astype(jnp.int32) + there[name][1].astype(jnp.int32) for name, _, _ in axes
    ]
    cases = []
    for cx in counts[0]:
        for cy in counts[1]:
            for cz in counts[2]:
                cases.append(((cx, cy, cz), (found[0] == cx) & (found[1] == cy) & (found[2] == cz)))

    def await_rows(sem, number):
        if number > 0:
            part = next(k for k in (8, 4, 2, 1) if number % k == 0)
            ref = tally.at[pl.ds(0, number // part), pl.ds(0, part)]
            pltpu.make_async_copy(ref, ref, sem).wait()

    def await_all(sem, groups):
        for (cx, cy, cz), ok in cases:
            many = {"x": cx, "y": cy, "z": cz, "xy": cx * cy, "xz": cx * cz, "yz": cy * cz}
            number = sum(many[kind] * size for g in groups for kind, size in g.sizes.items())
            if len(cases) == 1:
                await_rows(sem, number)
            else:
                @pl.when(ok)
                def _():
                    await_rows(sem, number)

    class Group:
        def __init__(self, sem):
            self.sem, self.copies, self.sizes = sem, [], {}

        def add(self, kind, side, a, z, where, goes):
            self.copies.append((kind, remote(a, z, s_sem, self.sem, where), goes))
            if side == 0:
                size = 1
                for d in z.shape[:-1]:
                    size *= d
                self.sizes[kind] = self.sizes.get(kind, 0) + size

    def sides_of_x(n):
        if ngx == 2:
            return [(0, (1 - gx) * (n - 1), 1 - gx, gx, 1 - gx, True)]
        return [
            (side, 0 if side == 0 else n - 1, side, 1 - side, beside["gx"][side], there["gx"][side])
            for side in range(2)
        ]

    def both(a, b):
        return b if a is True else a & b

    def plan(r):
        n, s = (nx, 1) if FINE[r] else (half, 2)
        src = g_ref if r == 0 else field.at[r]
        groups = {k: Group(r_sem.at[r % 2 if k == "v" else 2 + r // 2 % 2]) for k in "vdp"}
        kinds = [("v", src, 0, hx, hy, hz)]
        if DEEP[r]:
            kinds.append(("p", pfield.at[r], 1, px, py, pz))
        for side, plane_at, _, other, to, ok in sides_of_x(n):
            for group, a, which, zx, zy, zz in kinds:
                groups[group].add("x", side, a.at[:, plane_at], zx.at[r, other], device(gx=to), ok)
        for side in range(2):
            other = 1 - side
            for group, a, which, zx, zy, zz in kinds:
                g = groups[group]
                g.add("y", side, a.at[:, 0:n, rows_of(side, s)], zy.at[r, :, 0:n, rows_of(other, s)],
                      device(gy=beside["gy"][side]), there["gy"][side])
                g.add("z", side, zpack.at[r, which], zz.at[r, other],
                      device(gz=beside["gz"][side]), there["gz"][side])
        if DEEP[r]:
            g = groups["d"]
            for i, plane_at, _, other, to, ok in sides_of_x(n):
                for j in range(2):
                    g.add("xy", 2 * i + j, src.at[:, plane_at, rows_of(j, s)],
                          exy.at[r, other, :, rows_of(1 - j, s)],
                          device(gx=to, gy=beside["gy"][j]), both(ok, there["gy"][j]))
                    g.add("xz", 2 * i + j, zpack.at[r, 0], exz.at[r, other, 1 - j],
                          device(gx=to, gz=beside["gz"][j]), both(ok, there["gz"][j]))
            for i in range(2):
                for j in range(2):
                    g.add("yz", 2 * i + j, zpack.at[r, 0, rows_of(i, s)], eyz.at[r, 1 - j, rows_of(1 - i, s)],
                          device(gy=beside["gy"][i], gz=beside["gz"][j]),
                          there["gy"][i] & there["gz"][j])
        return groups

    plans = [plan(r) for r in range(len(DEEP))]

    def plan_constants(L):
        g = Group(L.r_sem)
        for side, plane_at, mine, other, to, ok in sides_of_x(L.n):
            g.add("x", side, L.xw.at[:, mine], L.xt.at[other], device(gx=to), ok)
            g.add("x", side, L.st.at[:, :, plane_at], L.xst.at[other], device(gx=to), ok)
        for side in range(2):
            other = 1 - side
            y_at, y_ok = device(gy=beside["gy"][side]), there["gy"][side]
            g.add("y", side, L.st.at[:, 0, :, rows_of(side, L.s)],
                  L.yst.at[:, :, rows_of(other, L.s)], y_at, y_ok)
            g.add("y", side, L.zs.at[0, rows_of(side, L.s)], L.yzs.at[rows_of(other, L.s)], y_at, y_ok)
            g.add("y", side, L.xw.at[:, :, rows_of(side, L.s)], L.yxw.at[:, :, rows_of(other, L.s)], y_at, y_ok)
            g.add("z", side, L.zs, L.zst.at[other], device(gz=beside["gz"][side]), there["gz"][side])
        return g

    def plan_spreads():
        g = Group(co_sem)
        s = L1.s
        for side, plane_at, _, other, to, ok in sides_of_x(half):
            g.add("x", side, co.at[:, :, plane_at], cox.at[other], device(gx=to), ok)
        for side in range(2):
            other = 1 - side
            g.add("y", side, co.at[:, :, :, rows_of(side, s)], coy.at[:, :, :, rows_of(other, s)],
                  device(gy=beside["gy"][side]), there["gy"][side])
            g.add("z", side, cos, coz.at[other], device(gz=beside["gz"][side]), there["gz"][side])
        return g

    spreads = plan_spreads()
    constants = [plan_constants(L0), plan_constants(L1)]

    def begin(*groups, only=None):
        for g in groups:
            for kind, copy, goes in g.copies:
                if only is not None and kind not in only:
                    continue
                if goes is True:
                    copy.start()
                    continue

                @pl.when(goes)
                def _():
                    copy.start()

    def arrive(*groups):
        await_all(groups[0].sem, groups)

    def pack(L, get, planes=None):
        got = jnp.zeros(tile, jnp.float32)
        for e in every:
            for i in (range(L.n) if planes is None else planes):
                j = e * L.n + i
                got = jnp.where(zi // (2 * L.s) == j, roll(get(e, i), 2 * L.s * j + L.s, 1), got)
        return got

    def unpack(L, tile_of, e, i):
        return roll(tile_of, -(2 * L.s * (e * L.n + i) + L.s), 1)

    def combine(L, low, high, ok=None):
        s = L.s
        up = zi % (2 * s) < s
        has_low, has_high = there["gz"]
        if ok is not None:
            has_low, has_high = has_low & ok, has_high & ok
        code = jnp.where(up, jnp.where(has_high, 1, 0), jnp.where(has_low, 2, 0))
        return jnp.where(code == 1, roll(high, -s, 1), jnp.where(code == 2, roll(low, s, 1), 0.0))

    def local(L, get, e, i):
        n, s = L.n, L.s
        v = get(e, i)
        q = L.cw[e, 2, i] * roll(v, -s, 0) + L.cw[e, 3, i] * roll(v, s, 0)
        q = q + L.cw[e, 4, i] * roll(v, -s, 1) + L.cw[e, 5, i] * roll(v, s, 1)
        if i < n - 1:
            q = q + L.cw[e, 0, i] * get(e, i + 1)
        if i > 0:
            q = q + L.cw[e, 1, i] * get(e, i - 1)
        return q + L.cb[e, i]

    def border(L, q, halo, e, i):
        gx_of, gy_of, term_z = halo
        q = q + L.st[e, 0, i] * gy_of(e, i) + term_z(e, i)
        if i == 0:
            q = q + L.xw[e, 0] * gx_of(0, e)
        if i == L.n - 1:
            q = q + L.xw[e, 1] * gx_of(1, e)
        return q

    def ends(L, packed):
        at = (zi < L.s) | (zi >= nz - L.s)
        return lambda e, i: jnp.where(at, unpack(L, packed, e, i), 0.0)

    def received(L, r, x_ref, y_ref, z_ref):
        my = edge_rows(L.s, *there["gy"])
        c = combine(L, z_ref[r, 0], z_ref[r, 1])
        return (
            lambda side, e: jnp.where(there["gx"][side], x_ref[r, side, e], 0.0),
            lambda e, i: jnp.where(my, y_ref[r, e, i], 0.0),
            ends(L, L.zs[0] * c),
            c,
        )

    def ring(L, r, get, own):
        n, s = L.n, L.s
        my = edge_rows(s, *there["gy"])
        lines_of = []
        columns_of = []
        for side in range(2):
            ok = there["gx"][side]
            mask = edge_rows(s, ok & there["gy"][0], ok & there["gy"][1])
            lines_of.append([jnp.where(mask, exy[r, side, e], 0.0) for e in every])
            columns_of.append(combine(L, exz[r, side, 0], exz[r, side, 1], ok))
        cy = jnp.where(my, combine(L, eyz[r, 0], eyz[r, 1]), 0.0)
        rx = [
            [
                jnp.where(
                    there["gx"][side],
                    px[r, side, e] + L.xt[side, e] * get(e, 0 if side == 0 else n - 1)
                    + L.xst[side, e, 0] * lines_of[side][e]
                    + L.xst[side, e, 1] * unpack(L, columns_of[side], e, n - 1 if side == 0 else 0),
                    0.0,
                )
                for e in every
            ]
            for side in range(2)
        ]

        def ry(e, i):
            got = py[r, e, i] + L.yst[e, i] * get(e, i)
            if i == 0:
                got = got + L.yxw[e, 0] * lines_of[0][e]
            if i == n - 1:
                got = got + L.yxw[e, 1] * lines_of[1][e]
            return jnp.where(my, got, 0.0)

        far = 2 * s * (n - 1)
        sideways = jnp.where(
            zi // (2 * s) % n == 0, roll(columns_of[0], -far, 1), roll(columns_of[1], far, 1)
        )
        toward, along_y, along_x = [combine(L, L.zst[0, k], L.zst[1, k]) for k in range(3)]
        c = combine(L, pz[r, 0], pz[r, 1]) + toward * own + along_y * cy + along_x * sideways
        c = jnp.where(zi < 2 * s * EQ * n, c, 0.0)
        y_ends = L.zs[1] * jnp.where(my, L.yzs[...] * cy, 0.0)
        return (
            lambda side, e: rx[side][e],
            ry,
            ends(L, L.zs[0] * c + y_ends),
        )

    def put(r, L, v):
        for e in every:
            for i in range(L.n):
                field[r, e, i] = v[e][i]

    def planes(f, L):
        return [[f(e, i) for i in range(L.n)] for e in every]

    def deep(r, L):
        get = lambda e, i: field[r, e, i]
        begin(plans[r]["d"], only=("xy",))
        zpack[r, 0] = pack(L, get)
        begin(plans[r]["d"], only=("xz", "yz"))
        begin(plans[r]["v"])
        for e in every:
            for i in range(L.n):
                pfield[r, e, i] = KEEP * get(e, i) + local(L, get, e, i)
        zpack[r, 1] = pack(L, lambda e, i: pfield[r, e, i])
        begin(plans[r]["p"])

        def finish():
            arrive(plans[r]["v"])
            halo = received(L, r, hx, hy, hz)[:3]
            new = planes(lambda e, i: border(L, pfield[r, e, i], halo, e, i), L)

            def outer():
                arrive(plans[r]["d"], plans[r]["p"])
                return ring(L, r, get, zpack[r, 0])

            return new, outer

        return finish

    def coarsen(a, s):
        n = a.shape[0]
        a = jnp.stack([a[2 * i] + a[2 * i + 1] for i in range(n // 2)])
        y, z = iota(a.shape, 1), iota(a.shape, 2)
        a = a + jnp.where((y // s) % 2 == 0, roll(a, -s, 1), roll(a, s, 1))
        a = a + jnp.where((z // s) % 2 == 0, roll(a, -s, 2), roll(a, s, 2))
        return a * 0.125

    def select(a, onehot):
        parts = []
        for _ in range(3):
            parts.append(a.astype(jnp.bfloat16))
            a = a - parts[-1].astype(jnp.float32)
        got = jnp.dot(jnp.concatenate(parts, axis=0), onehot, preferred_element_type=jnp.float32)
        m = a.shape[0]
        return (got[0:m] + got[m : 2 * m]) + got[2 * m :]

    groups = qx * qy
    source = iota((nz, nz), 0)
    target = iota((nz, nz), 1)
    squeeze = jnp.where(source == 4 * (target % qz), 1.0, 0.0).astype(jnp.bfloat16)
    squeeze_pairs = jnp.where(
        (source == 4 * (target % qz)) | (source == 4 * (target % qz) + 2), 1.0, 0.0
    ).astype(jnp.bfloat16)

    def to_rows(a, lanes):
        m = a.shape[0]
        c = select(a.reshape(m * qx * ny, nz), lanes).reshape(m, qx, ny, nz)
        place = iota((m, ny, nz), 2) // qz
        got = jnp.zeros((m, ny, nz), jnp.float32)
        for x in range(qx):
            for y in range(qy):
                part = roll(c[:, x], -4 * y, 1)
                got = jnp.where(place == (x * qy + y + gz) % groups, part, got)
        return got

    def own(small, whole, sem):
        return pltpu.make_async_copy(
            small.at[:, pl.ds(0, 1)], whole.at[X, core, :, pl.ds(row, 1)], sem
        )

    def stage(number, small, whole, rs):
        made = []
        if number == 0:
            for step in range(1, ngx):
                made.append((small.at[:, pl.ds(0, 1)], whole.at[X, core, :, pl.ds(row, 1)],
                             step, device(gx=(gx + step) % ngx)))
        elif number == 1:
            block = whole.at[X, core, :, pl.ds(gy * ngx, ngx)]
            for step in range(1, ngy):
                made.append((block, block, step, device(gy=(gy + step) % ngy)))
        elif number == 2:
            block = whole.at[X, core]
            for step in range(1, nX):
                made.append((block, block, step, device(gz=((X + step) % nX) * cores + core)))
        else:
            block = whole.at[:, core]
            for step in range(1, cores):
                made.append((block, block, step, device(gz=X * cores + (core + step) % cores)))
        return [
            remote(a, z, ws_sem.at[number], rs.at[number], where)
            for a, z, _, where in made
        ]

    wargs = (wsend, wall, wr_sem)

    def everyone():
        mirrored = all(count & (count - 1) == 0 for count in dims)

        def other(index, step, count):
            return index ^ step if mirrored else (index + step) % count

        made = []
        for ay in reversed(range(ngy)):
            for az in reversed(range(ngz)):
                for ax in reversed(range(ngx)):
                    if ax + ay + az == 0:
                        continue
                    made.append(remote(
                        bsend.at[:, pl.ds(0, 1)], ball.at[X, core, :, pl.ds(row, 1)],
                        bs_sem, br_sem,
                        (other(gx, ax, ngx), other(gy, ay, ngy), other(gz, az, ngz)),
                    ))
        return made

    def start(number):
        for copy in stage(number, *wargs):
            copy.start()

    def stage_rows(number):
        return 7 * EQ * (
            ngx - 1, ngx * (ngy - 1), rows * (nX - 1), nX * rows * (cores - 1)
        )[number]

    def done(number):
        await_rows(wr_sem.at[number], stage_rows(number))

    def scale(L, get_w, get_d, e, i):
        n, s = L.n, L.s
        raw = [get_w(e, k, i) for k in range(6)]
        total = get_d(e, i)
        for k in range(6):
            total = total + raw[k]
        c = DAMP / total
        w = [c * raw[k] for k in range(6)]
        L.tot[e, i] = (1.0 / DAMP) * total
        last_y, first_y, last_z, first_z = yi >= ny - s, yi < s, zi >= nz - s, zi < s
        L.cw[e, 0, i] = w[0]
        L.cw[e, 1, i] = w[1]
        L.cw[e, 2, i] = jnp.where(last_y, 0.0, w[2])
        L.cw[e, 3, i] = jnp.where(first_y, 0.0, w[3])
        L.cw[e, 4, i] = jnp.where(last_z, 0.0, w[4])
        L.cw[e, 5, i] = jnp.where(first_z, 0.0, w[5])
        L.st[e, 0, i] = jnp.where(last_y, w[2], jnp.where(first_y, w[3], 0.0))
        L.st[e, 1, i] = jnp.where(last_z, w[4], jnp.where(first_z, w[5], 0.0))
        if i == 0:
            L.xw[e, 0] = w[1]
        if i == n - 1:
            L.xw[e, 1] = w[0]
        if L is L1:
            odd_y, odd_z = yi // s % 2 == 1, zi // s % 2 == 1
            co[e, 1, i] = w[0] if i % 2 == 1 else w[1]
            co[e, 2, i] = jnp.where(odd_y, w[2], w[3])
            co[e, 3, i] = jnp.where(odd_z, w[4], w[5])
            co[e, 0, i] = (
                KEEP + (w[1] if i % 2 == 1 else w[0])
                + jnp.where(odd_y, w[3], w[2]) + jnp.where(odd_z, w[5], w[4])
            )
        return c

    def pack_constants(L):
        L.zs[0] = pack(L, lambda e, i: L.st[e, 1, i])
        L.zs[1] = pack(L, lambda e, i: L.st[e, 0, i])
        L.zs[2] = pack(L, lambda e, i: L.xw[e, 0 if i == 0 else 1], (0, L.n - 1))

    for load in guess_loads:
        load.wait()
    guess = lambda e, i: g_ref[e, i]
    zpack[0, 0] = pack(L0, guess)
    pl.semaphore_wait(barrier, awaited)
    begin(plans[0]["v"])
    hear = there["gy"][0].astype(jnp.int32) + there["gy"][1].astype(jnp.int32)

    def tell(k):
        for side in range(2):
            @pl.when(there["gy"][side])
            def _():
                pl.semaphore_signal(
                    know.at[k], inc=1, device_id=device(gy=beside["gy"][side]), device_id_type=MESH
                )

    if close:
        tell(0)
    await_rows(i_sem.at[1], 8 * EQ * nx * ny)
    level2 = [None] * (7 * EQ)
    for e in every:
        d1 = coarsen(d_ref[e], 1)
        level2[6 * EQ + e] = coarsen(d1, 2)
        for k in range(6):
            w = 0.25 * coarsen(w_ref[6 * e + k], 1)
            w1[6 * e + k] = w
            level2[6 * e + k] = 0.25 * coarsen(w, 2)
        for i in range(half):
            c = scale(L1, lambda e, k, i: w1[6 * e + k, i], lambda e, i: d1[i], e, i)
            w1[6 * EQ + e, i] = c
    wsend[...] = to_rows(jnp.stack(level2), squeeze)
    own(wsend, wall, i_sem.at[0]).start()
    start(0)
    for e in every:
        for i in range(nx):
            c = scale(L0, lambda e, k, i: w_ref[6 * e + k, i], lambda e, i: d_ref[e, i], e, i)
            L0.cb[e, i] = c * b_ref[e, i]
    pack_constants(L0)
    begin(constants[0])
    for e in every:
        for i in range(nx):
            pfield[0, e, i] = KEEP * guess(e, i) + local(L0, guess, e, i)
    if close:
        pl.semaphore_wait(know.at[0], hear)
        tell(1)

    arrive(plans[0]["v"])
    halo = received(L0, 0, hx, hy, hz)[:3]
    put(1, L0, planes(lambda e, i: border(L0, pfield[0, e, i], halo, e, i), L0))
    finish = deep(1, L0)
    own(wsend, wall, i_sem.at[0]).wait()
    done(0)
    if close:
        pl.semaphore_wait(know.at[1], hear)
    start(1)
    pack_constants(L1)
    begin(constants[1])
    v, outer = finish()
    kept0 = field.at[0]
    for e in every:
        for i in range(nx):
            kept0[e, i] = v[e][i]
    get = lambda e, i: kept0[e, i]
    q = planes(lambda e, i: local(L0, get, e, i), L0)
    arrive(constants[0])
    halo = outer()
    first = []
    for e in every:
        r = jnp.stack([
            L0.tot[e, i] * (border(L0, q[e][i], halo, e, i) - DAMP * get(e, i)) for i in range(nx)
        ])
        b = coarsen(r, 1)
        first.append([])
        for i in range(half):
            u = w1[6 * EQ + e, i] * b[i]
            L1.cb[e, i] = u
            first[e].append(u)
    put(2, L1, first)
    finish = deep(2, L1)
    done(1)
    start(2)
    for m in range(4):
        cos[m] = pack(L1, lambda e, i: co[e, m, i])
    begin(spreads)
    u, outer = finish()
    kept1 = pfield.at[3]
    for e in every:
        for i in range(half):
            kept1[e, i] = u[e][i]
    get = lambda e, i: kept1[e, i]
    q = planes(lambda e, i: local(L1, get, e, i), L1)
    arrive(constants[1])
    halo = outer()
    rest = []
    for e in every:
        r = []
        for i in range(half):
            total = border(L1, q[e][i], halo, e, i)
            field[3, e, i] = KEEP * get(e, i) + total
            r.append(L1.tot[e, i] * (total - DAMP * get(e, i)))
        r = [r[2 * x] + r[2 * x + 1] for x in range(qx)]
        rest.append(jnp.stack([c + roll(c, -2, 0) for c in r]))
    bsend[...] = 0.125 * to_rows(jnp.stack(rest), squeeze_pairs)
    for copy in everyone():
        copy.start()
    own(bsend, ball, br_sem).start()
    zpack[3, 0] = pack(L1, lambda e, i: field[3, e, i])
    begin(plans[3]["v"])
    arrive(spreads)
    for m in range(4):
        c = combine(L1, coz[0, m], coz[1, m])
        for e in every:
            for i in range(half):
                zco[e, m, i] = unpack(L1, c, e, i)
    NX, NY, NZ = ngx * qx, ngy * qy, ngz * qz
    shape = (NZ, 3 * nz)
    kind, t = iota(shape, 1) // nz, iota(shape, 1) % nz
    base = gz * qz + t // 4
    wanted = jnp.where(
        kind == 0, base,
        jnp.where(
            kind == 1, base + jnp.where(t % 4 < 2, -1, 1),
            jnp.where(t < nz // 2, gz * qz - 1, gz * qz + qz),
        ),
    )
    widen[...] = jnp.where(iota(shape, 0) == wanted, 1.0, 0.0).astype(jnp.bfloat16)
    for e in every:
        for i in range(NX + 2):
            if i in (0, NX + 1):
                e2[e, i] = jnp.zeros((NY + 16, NZ), jnp.float32)
            else:
                e2[e, i, 0:8] = jnp.zeros((8, NZ), jnp.float32)
                e2[e, i, NY + 8 : NY + 16] = jnp.zeros((8, NZ), jnp.float32)
    done(2)
    start(3)
    done(3)
    def spread(ref, index):
        place, y_of = iota((rows, nz), 1) // qz, iota((NY, nz), 0) % qy
        parts = [[] for _ in range(NX)]
        for t in range(NZ // nz):
            moved = []
            for k in range(groups):
                got = None
                for p in range(groups):
                    g = t * groups + (p - k) % groups
                    a = ref[g // cores, g % cores, index]
                    got = a if got is None else jnp.where(place == p, a, got)
                moved.append(roll(got, -k * qz, 1))
            for x in range(qx):
                if ngx != qy:
                    for y in range(qy):
                        mix[...] = moved[x * qy + y]
                        for g in range(ngx):
                            mixed[g, pl.ds(y, ngy, stride=qy), :] = mix[pl.ds(g, ngy, stride=ngx), :]
                for g in range(ngx):
                    if ngx != qy:
                        got = mixed[g]
                    else:
                        got = roll(moved[x * qy], -g, 0)
                        for y in range(1, qy):
                            got = jnp.where(y_of == y, roll(moved[x * qy + y], y - g, 0), got)
                    parts[g * qx + x].append(got)
        return [p[0] if len(p) == 1 else jnp.concatenate(p, axis=1) for p in parts]

    Y, Z = iota((NY, NZ), 0), iota((NY, NZ), 1)
    even_y, even_z = Y % 2 == 0, Z % 2 == 0
    pairs = NX // 4

    def halve(a):
        made = []
        for p in range(pairs):
            two = []
            for x in (2 * p, 2 * p + 1):
                c = a[2 * x] + a[2 * x + 1]
                two.append(c + jnp.where(even_y, roll(c, -1, 0), roll(c, 1, 0)))
            c = jnp.where(even_y, two[0], two[1])
            made.append(0.125 * (c + jnp.where(even_z, roll(c, -1, 1), roll(c, 1, 1))))
        return made

    def double(a, x):
        c = a[x // 4]
        if x // 2 % 2 == 0:
            return jnp.where(even_y, c, roll(c, 1, 0))
        return jnp.where(even_y, roll(c, -1, 0), c)

    def tree(terms):
        while len(terms) > 1:
            terms = [
                terms[k] + terms[k + 1] if k + 1 < len(terms) else terms[k]
                for k in range(0, len(terms), 2)
            ]
        return terms[0]

    def around2(w, v):
        made = []
        for x in range(NX):
            terms = [
                w[4][x] * roll(v[x], -1, 1), w[5][x] * roll(v[x], 1, 1),
                w[2][x] * roll(v[x], -1, 0), w[3][x] * roll(v[x], 1, 0),
            ]
            if x < NX - 1:
                terms.append(w[0][x] * v[x + 1])
            if x > 0:
                terms.append(w[1][x] * v[x - 1])
            made.append(tree(terms))
        return made

    def around3(w, v):
        made = []
        for p in range(pairs):
            up, down = roll(v[p], -1, 0), roll(v[p], 1, 0)
            if p < pairs - 1:
                up = jnp.where(even_y, up, roll(v[p + 1], 1, 0))
            if p > 0:
                down = jnp.where(even_y, roll(v[p - 1], -1, 0), down)
            made.append(tree([
                w[4][p] * roll(v[p], -2, 1), w[5][p] * roll(v[p], 2, 1),
                w[0][p] * up, w[1][p] * down,
                w[2][p] * roll(v[p], -2, 0), w[3][p] * roll(v[p], 2, 0),
            ]))
        return made

    steps3 = ((-1, 0), (1, 0), (-2, 0), (2, 0), (0, -2), (0, 2))

    def shifted(v, dr, dl):
        return roll(roll(v, dl, 1), dr, 0)

    def twice(w):
        got = {(0, 0): KEEP * KEEP}

        def add(at, value):
            at = (at[0] % NY, at[1] % NZ)
            got[at] = got[at] + value if at in got else value

        for k, (dr, dl) in enumerate(steps3):
            add((dr, dl), 2.0 * KEEP * w[k])
            for m, (er, el) in enumerate(steps3):
                if k == m and k < 2:
                    continue
                add((dr + er, dl + el), w[k] * shifted(w[m], dr, dl))
        return got

    def apply_twice(w, v):
        turned = {dl: roll(v, dl, 1) for dl in sorted({at[1] for at in w})}
        return tree([c * roll(turned[dl], dr, 0) for (dr, dl), c in w.items()])

    def inner(w, k, at, last, step):
        if k == 0 and step == 2:
            return jnp.where(even_y, w, 0.0) if at == last else w
        if k == 1 and step == 2:
            return jnp.where(even_y, 0.0, w) if at == 0 else w
        if k < 2:
            return w
        return jnp.where((Y >= NY - step, Y < step, Z >= NZ - step, Z < step)[k - 2], 0.0, w)

    def constants_of(plain, diagonal, count, step):
        scaled, totals, weights = [], [], [[] for _ in range(6)]
        for at in range(count):
            total = diagonal[at] + tree([plain[k][at] for k in range(6)])
            scaled.append(DAMP / total)
            totals.append((1.0 / DAMP) * total)
            for k in range(6):
                weights[k].append(inner(scaled[at] * plain[k][at], k, at, count - 1, step))
        return scaled, totals, weights

    c2, t2, w2, c3, w3, ww3 = [], [], [], [], [], []
    by_two = pairs == 1 and NY >= 8 and COARSE_SWEEPS % 2 == 0
    for e in every:
        plain = [spread(wall, 6 * e + k) for k in range(6)]
        diagonal = spread(wall, 6 * EQ + e)
        scaled, totals, weights = constants_of(plain, diagonal, NX, 1)
        c2.append(scaled)
        t2.append(totals)
        w2.append(weights)
        coarse = [[0.25 * c for c in halve(plain[k])] for k in range(6)]
        scaled, _, weights = constants_of(coarse, halve(diagonal), pairs, 2)
        c3.append(scaled)
        w3.append(weights)
        if by_two:
            ww3.append(twice([weights[k][0] for k in range(6)]))

    arrive(plans[3]["v"])
    pltpu.make_async_copy(ball, ball, br_sem).wait()
    rhs = []
    for e in every:
        got = spread(ball, e)
        rhs.append([c2[e][x] * got[x] for x in range(NX)])

    def smooth2(v):
        made = []
        for e in every:
            sums = around2(w2[e], v[e])
            made.append([(KEEP * v[e][x] + rhs[e][x]) + sums[x] for x in range(NX)])
        return made

    v2 = rhs
    for step in range(SWEEPS - 1):
        v2 = smooth2(v2)
    rhs3 = []
    for e in every:
        sums = around2(w2[e], v2[e])
        got = halve([t2[e][x] * ((rhs[e][x] - DAMP * v2[e][x]) + sums[x]) for x in range(NX)])
        rhs3.append([c3[e][p] * got[p] for p in range(pairs)])
    v3 = rhs3
    for step in range(1 if by_two else COARSE_SWEEPS - 1):
        sums = [around3(w3[e], v3[e]) for e in every]
        v3 = [
            [(KEEP * v3[e][p] + rhs3[e][p]) + sums[e][p] for p in range(pairs)] for e in every
        ]
    if by_two:
        once = v3
        for step in range(COARSE_SWEEPS // 2 - 1):
            v3 = [[apply_twice(ww3[e], v3[e][0]) + once[e][0]] for e in every]
    v2 = [[v2[e][x] + double(v3[e], x) for x in range(NX)] for e in every]
    for step in range(SWEEPS):
        v2 = smooth2(v2)
    for e in every:
        for x in range(NX):
            e2[e, x + 1, 8 : 8 + NY] = v2[e][x]

    wx, wy = qx + 2, qy + 2
    for e in every:
        for i in range(wx):
            for j in range(wy):
                at = (e * wx + i) * wy + j
                lines[at : at + 1, :] = e2[e, gx * qx + i, pl.ds(7 + gy * qy + j, 1), :]
    broad[...] = select(lines[...], widen[...])
    CENTER, BEYOND_Z, OUTSIDE_Z = range(3)
    ysel, yhalf = yi // 4, yi // 2 % 2

    def strip(kind, e, x, y):
        at = (e * wx + x + 1) * wy + y + 1
        return jnp.broadcast_to(broad[at : at + 1, kind * nz : kind * nz + nz], tile)

    def plane(kind, e, x):
        got = strip(kind, e, x, 0)
        for y in range(1, qy):
            got = jnp.where(ysel == y, strip(kind, e, x, y), got)
        return got

    def across_y(kind, e, x):
        got = None
        for y in range(qy):
            both = jnp.where(yhalf == 0, strip(kind, e, x, y - 1), strip(kind, e, x, y + 1))
            got = both if got is None else jnp.where(ysel == y, both, got)
        return got

    def across_x(kind, e, i):
        return plane(kind, e, i // 2 + (1 if i % 2 == 1 else -1))

    def rows_y(kind, e, x):
        return jnp.where(yi < ny // 2, strip(kind, e, x, -1), strip(kind, e, x, qy))

    left, behind, _, columns = received(L1, 3, hx, hy, hz)
    mine = edge_rows(L1.s, *there["gy"])

    def add_x(side, e):
        face, near = (-1, 0) if side == 0 else (qx, qx - 1)
        got = left(side, e) + cox[side, e, 0] * plane(CENTER, e, face)
        got = got + cox[side, e, 1] * plane(CENTER, e, near)
        got = got + cox[side, e, 2] * across_y(CENTER, e, face)
        got = got + cox[side, e, 3] * plane(BEYOND_Z, e, face)
        return jnp.where(there["gx"][side], got, 0.0)

    def add_y(e, i):
        x = i // 2
        got = behind(e, i) + coy[e, 0, i] * rows_y(CENTER, e, x)
        got = got + coy[e, 1, i] * rows_y(CENTER, e, x + 1 if i % 2 == 1 else x - 1)
        got = got + coy[e, 2, i] * plane(CENTER, e, x)
        got = got + coy[e, 3, i] * rows_y(BEYOND_Z, e, x)
        return jnp.where(mine, got, 0.0)

    def add_z(e, i):
        x = i // 2
        got = unpack(L1, columns, e, i) + zco[e, 0, i] * plane(OUTSIDE_Z, e, x)
        got = got + zco[e, 1, i] * across_x(OUTSIDE_Z, e, i)
        got = got + zco[e, 2, i] * across_y(OUTSIDE_Z, e, x)
        return L1.st[e, 1, i] * (got + zco[e, 3, i] * plane(CENTER, e, x))

    swept = pfield.at[3]
    for e in every:
        for i in range(half):
            x = i // 2
            got = field[3, e, i] + co[e, 0, i] * plane(CENTER, e, x)
            got = got + co[e, 1, i] * across_x(CENTER, e, i)
            got = got + co[e, 2, i] * across_y(CENTER, e, x)
            swept[e, i] = got + co[e, 3, i] * plane(BEYOND_Z, e, x)
    get = lambda e, i: swept[e, i]
    halo = (add_x, add_y, add_z)
    u = planes(lambda e, i: KEEP * get(e, i) + border(L1, local(L1, get, e, i), halo, e, i), L1)
    put(4, L0, planes(lambda e, i: kept0[e, i] + u[e][i // 2], L0))
    finish = deep(4, L0)
    v, outer = finish()
    last = pfield.at[0]
    for e in every:
        for i in range(nx):
            last[e, i] = v[e][i]
    get = lambda e, i: last[e, i]
    q = planes(lambda e, i: KEEP * get(e, i) + local(L0, get, e, i), L0)
    halo = outer()
    for e in every:
        for i in range(nx):
            out_ref[e, i] = border(L0, q[e][i], halo, e, i)
    await_all(s_sem, [g for p in plans for g in p.values()] + constants + [spreads])
    for number in range(4):
        await_rows(ws_sem.at[number], stage_rows(number))
    await_rows(bs_sem, EQ * (rows * ngz - 1))


def per_device(dims, cores, couplings, diagonal, right_side, guess):
    ngx, ngy, ngz = dims
    brick = guess.shape[1:]
    nx, ny, nz = brick
    half = nx // 2
    qx, qy, qz = nx // 4, ny // 4, nz // 4
    rows = ngx * ngy
    nX = ngz // cores
    rounds = len(DEEP)
    f32 = jnp.float32
    vmem = pltpu.VMEM
    dma = pltpu.SemaphoreType.DMA

    def level(n):
        return [
            vmem((EQ, 6, n, ny, nz), f32),
            vmem((EQ, 2, n, ny, nz), f32),
            vmem((EQ, 2, ny, nz), f32),
            vmem((EQ, n, ny, nz), f32),
            vmem((EQ, n, ny, nz), f32),
            vmem((3, ny, nz), f32),
            vmem((2, EQ, ny, nz), f32),
            vmem((2, EQ, 2, ny, nz), f32),
            vmem((EQ, n, ny, nz), f32),
            vmem((ny, nz), f32),
            vmem((EQ, 2, ny, nz), f32),
            vmem((2, 3, ny, nz), f32),
            dma,
        ]

    faces = [
        vmem((rounds, 2, EQ, ny, nz), f32),
        vmem((rounds, EQ) + brick, f32),
        vmem((rounds, 2, ny, nz), f32),
    ]
    return pl.pallas_call(
        functools.partial(kernel, dims, cores),
        out_shape=vmem(guess.shape, f32),
        in_specs=[pl.BlockSpec(memory_space=pl.ANY)] * 4,
        out_specs=pl.BlockSpec(memory_space=vmem),
        scratch_shapes=[
            vmem(couplings.shape, f32),
            vmem(diagonal.shape, f32),
            vmem(right_side.shape, f32),
            vmem(guess.shape, f32),
            vmem((max(2048, nX * rows * 7 * EQ * (cores - 1) // 8, rows * (nX - 1) * 7 * EQ // 8), 8, nz), f32),
            vmem((rounds, EQ) + brick, f32),
            vmem((rounds, EQ) + brick, f32),
            vmem((rounds, 2, ny, nz), f32),
            *faces,
            *faces,
            vmem((rounds, 2, EQ, ny, nz), f32),
            vmem((rounds, 2, 2, ny, nz), f32),
            vmem((rounds, 2, ny, nz), f32),
            vmem((7 * EQ, half, ny, nz), f32),
            vmem((EQ, 4, half, ny, nz), f32),
            vmem((4, ny, nz), f32),
            vmem((2, EQ, 4, ny, nz), f32),
            vmem((EQ, 4, half, ny, nz), f32),
            vmem((2, 4, ny, nz), f32),
            vmem((EQ, 4, half, ny, nz), f32),
            *level(nx),
            *level(half),
            vmem((7 * EQ, ny, nz), f32),
            vmem((nX, cores, 7 * EQ, rows, nz), f32),
            vmem((EQ, ny, nz), f32),
            vmem((nX, cores, EQ, rows, nz), f32),
            vmem((EQ, ngx * qx + 2, ngy * qy + 16, ngz * qz), f32),
            vmem((EQ * (qx + 2) * (qy + 2), ngz * qz), f32),
            vmem((EQ * (qx + 2) * (qy + 2), 3 * nz), f32),
            vmem((ngz * qz, 3 * nz), jnp.bfloat16),
            vmem((rows, nz), f32),
            vmem((ngx, ngy * qy, nz), f32),
            dma,
            dma((4,)),
            dma,
            dma((4,)),
            dma((4,)),
            dma,
            dma,
            dma((2,)),
            dma((3,)),
            pltpu.SemaphoreType.REGULAR((2,)),
        ],
        compiler_params=pltpu.CompilerParams(
            collective_id=0, has_side_effects=True, vmem_limit_bytes=60 * 1024 * 1024
        ),
    )(couplings, diagonal, right_side, guess)


def solution(mesh):
    dims = (mesh.shape["gx"], mesh.shape["gy"], mesh.shape["gz"])
    cores = 2 if dims[2] % 2 == 0 else 1
    spec = P(None, "gx", "gy", "gz")
    return jax.shard_map(
        functools.partial(per_device, dims, cores),
        mesh=mesh,
        in_specs=(spec,) * 4,
        out_specs=spec,
        check_vma=False,
    )
```

```python
import functools

import jax
import jax.numpy as jnp
from jax import lax
from jax.experimental import pallas as pl
from jax.experimental.pallas import tpu as pltpu
from jax.sharding import PartitionSpec as P

SWEEPS = 2
COARSE_SWEEPS = 8
DAMP = 0.8
KEEP = 1.0 - DAMP
EQ = 3
MESH = pl.DeviceIdType.MESH
HIGH = lax.Precision.HIGHEST
DEEP = (False, True, True, False, True)
FINE = (True, True, False, False, True)


def roll(value, shift, axis):
    size = value.shape[axis]
    shift = shift % size
    return value if shift == 0 else pltpu.roll(value, shift, axis)


def iota(shape, axis):
    return lax.broadcasted_iota(jnp.int32, shape, axis)


class Level:
    def __init__(self, n, s, refs):
        self.n, self.s = n, s
        (self.cw, self.st, self.xw, self.cb, self.tot, self.zs,
         self.xt, self.xst, self.yst, self.yzs, self.yxw, self.zst, self.r_sem) = refs


def kernel(
    dims, cores, w_hbm, d_hbm, b_hbm, g_hbm, out_ref,
    w_ref, d_ref, b_ref, g_ref,
    tally, field, pfield, zpack, hx, hy, hz, px, py, pz, exy, exz, eyz, w1, co, cos, cox, coy, coz, zco, *rest,
):
    level_refs = (rest[:13], rest[13:26])
    (wsend, wall, bsend, ball, e2, lines, broad, widen, mix, mixed,
     s_sem, r_sem, co_sem, ws_sem, wr_sem, bs_sem, br_sem, i_sem, g_sem, know) = rest[26:]
    ngx, ngy, ngz = dims
    nx, ny, nz = g_ref.shape[1:]
    half = nx // 2
    qx, qy, qz = nx // 4, ny // 4, nz // 4
    rows = ngx * ngy
    nX = ngz // cores
    gx, gy, gz = lax.axis_index("gx"), lax.axis_index("gy"), lax.axis_index("gz")
    X, core = gz // cores, gz % cores
    row = gy * ngx + gx
    axes = (("gx", gx, ngx), ("gy", gy, ngy), ("gz", gz, ngz))
    L0 = Level(nx, 1, level_refs[0])
    L1 = Level(half, 2, level_refs[1])
    tile = (ny, nz)
    yi, zi = iota(tile, 0), iota(tile, 1)
    every = range(EQ)

    def device(**change):
        here = {"gx": gx, "gy": gy, "gz": gz}
        here.update(change)
        return (here["gx"], here["gy"], here["gz"])

    guess_loads = [pltpu.make_async_copy(g_hbm.at[e], g_ref.at[e], g_sem.at[e]) for e in range(EQ)]
    for load in guess_loads:
        load.start()
    barrier = pltpu.get_barrier_semaphore()
    close = ngy <= 4 and ngz <= 4
    awaited = 0

    def greet(ok, where):
        @pl.when(ok)
        def _():
            pl.semaphore_signal(barrier, inc=1, device_id=where, device_id_type=MESH)
        return ok.astype(jnp.int32)

    for name, index, count in axes:
        if close and name != "gx":
            steps = (-1, 1)
            for step in steps:
                ok = (index + step >= 0) & (index + step < count)
                awaited = awaited + greet(ok, device(**{name: jnp.clip(index + step, 0, count - 1)}))
        else:
            for step in range(1, count):
                pl.semaphore_signal(
                    barrier, inc=1, device_id=device(**{name: (index + step) % count}),
                    device_id_type=MESH,
                )
            awaited = awaited + (count - 1)

    for a, z in ((w_hbm, w_ref), (d_hbm, d_ref), (b_hbm, b_ref)):
        pltpu.make_async_copy(a, z, i_sem.at[1]).start()

    there = {
        name: (index > 0, index < count - 1) for name, index, count in axes
    }
    beside = {
        name: (jnp.maximum(index - 1, 0), jnp.minimum(index + 1, count - 1))
        for name, index, count in axes
    }

    def edge_rows(s, lo, hi):
        return (yi < jnp.where(lo, s, 0)) | (yi >= jnp.where(hi, ny - s, ny))

    def remote(a, z, ss, rs, where):
        return pltpu.make_async_remote_copy(
            src_ref=a, dst_ref=z, send_sem=ss, recv_sem=rs,
            device_id=where, device_id_type=MESH,
        )

    def rows_of(side, s):
        return pl.ds(0 if side == 0 else ny - s, s)

    counts = [
        [k for k in (0, 1, 2) if (k > 0 or count == 1) and k < count and (k == 2 or count <= 2 or k == 1)]
        for _, _, count in axes
    ]
    found = [
        there[name][0].astype(jnp.int32) + there[name][1].astype(jnp.int32) for name, _, _ in axes
    ]
    cases = []
    for cx in counts[0]:
        for cy in counts[1]:
            for cz in counts[2]:
                cases.append(((cx, cy, cz), (found[0] == cx) & (found[1] == cy) & (found[2] == cz)))

    def await_rows(sem, number):
        if number > 0:
            part = next(k for k in (8, 4, 2, 1) if number % k == 0)
            ref = tally.at[pl.ds(0, number // part), pl.ds(0, part)]
            pltpu.make_async_copy(ref, ref, sem).wait()

    def await_all(sem, groups):
        for (cx, cy, cz), ok in cases:
            many = {"x": cx, "y": cy, "z": cz, "xy": cx * cy, "xz": cx * cz, "yz": cy * cz}
            number = sum(many[kind] * size for g in groups for kind, size in g.sizes.items())
            if len(cases) == 1:
                await_rows(sem, number)
            else:
                @pl.when(ok)
                def _():
                    await_rows(sem, number)

    class Group:
        def __init__(self, sem):
            self.sem, self.copies, self.sizes = sem, [], {}

        def add(self, kind, side, a, z, where, goes):
            self.copies.append((kind, remote(a, z, s_sem, self.sem, where), goes))
            if side == 0:
                size = 1
                for d in z.shape[:-1]:
                    size *= d
                self.sizes[kind] = self.sizes.get(kind, 0) + size

    def sides_of_x(n):
        if ngx == 2:
            return [(0, (1 - gx) * (n - 1), 1 - gx, gx, 1 - gx, True)]
        return [
            (side, 0 if side == 0 else n - 1, side, 1 - side, beside["gx"][side], there["gx"][side])
            for side in range(2)
        ]

    def both(a, b):
        return b if a is True else a & b

    def plan(r):
        n, s = (nx, 1) if FINE[r] else (half, 2)
        src = g_ref if r == 0 else field.at[r]
        groups = {k: Group(r_sem.at[r % 2 if k == "v" else 2 + r // 2 % 2]) for k in "vdp"}
        kinds = [("v", src, 0, hx, hy, hz)]
        if DEEP[r]:
            kinds.append(("p", pfield.at[r], 1, px, py, pz))
        for side, plane_at, _, other, to, ok in sides_of_x(n):
            for group, a, which, zx, zy, zz in kinds:
                groups[group].add("x", side, a.at[:, plane_at], zx.at[r, other], device(gx=to), ok)
        for side in range(2):
            other = 1 - side
            for group, a, which, zx, zy, zz in kinds:
                g = groups[group]
                g.add("y", side, a.at[:, 0:n, rows_of(side, s)], zy.at[r, :, 0:n, rows_of(other, s)],
                      device(gy=beside["gy"][side]), there["gy"][side])
                g.add("z", side, zpack.at[r, which], zz.at[r, other],
                      device(gz=beside["gz"][side]), there["gz"][side])
        if DEEP[r]:
            g = groups["d"]
            for i, plane_at, _, other, to, ok in sides_of_x(n):
                for j in range(2):
                    g.add("xy", 2 * i + j, src.at[:, plane_at, rows_of(j, s)],
                          exy.at[r, other, :, rows_of(1 - j, s)],
                          device(gx=to, gy=beside["gy"][j]), both(ok, there["gy"][j]))
                    g.add("xz", 2 * i + j, zpack.at[r, 0], exz.at[r, other, 1 - j],
                          device(gx=to, gz=beside["gz"][j]), both(ok, there["gz"][j]))
            for i in range(2):
                for j in range(2):
                    g.add("yz", 2 * i + j, zpack.at[r, 0, rows_of(i, s)], eyz.at[r, 1 - j, rows_of(1 - i, s)],
                          device(gy=beside["gy"][i], gz=beside["gz"][j]),
                          there["gy"][i] & there["gz"][j])
        return groups

    plans = [plan(r) for r in range(len(DEEP))]

    def plan_constants(L):
        g = Group(L.r_sem)
        for side, plane_at, mine, other, to, ok in sides_of_x(L.n):
            g.add("x", side, L.xw.at[:, mine], L.xt.at[other], device(gx=to), ok)
            g.add("x", side, L.st.at[:, :, plane_at], L.xst.at[other], device(gx=to), ok)
        for side in range(2):
            other = 1 - side
            y_at, y_ok = device(gy=beside["gy"][side]), there["gy"][side]
            g.add("y", side, L.st.at[:, 0, :, rows_of(side, L.s)],
                  L.yst.at[:, :, rows_of(other, L.s)], y_at, y_ok)
            g.add("y", side, L.zs.at[0, rows_of(side, L.s)], L.yzs.at[rows_of(other, L.s)], y_at, y_ok)
            g.add("y", side, L.xw.at[:, :, rows_of(side, L.s)], L.yxw.at[:, :, rows_of(other, L.s)], y_at, y_ok)
            g.add("z", side, L.zs, L.zst.at[other], device(gz=beside["gz"][side]), there["gz"][side])
        return g

    def plan_spreads():
        g = Group(co_sem)
        s = L1.s
        for side, plane_at, _, other, to, ok in sides_of_x(half):
            g.add("x", side, co.at[:, :, plane_at], cox.at[other], device(gx=to), ok)
        for side in range(2):
            other = 1 - side
            g.add("y", side, co.at[:, :, :, rows_of(side, s)], coy.at[:, :, :, rows_of(other, s)],
                  device(gy=beside["gy"][side]), there["gy"][side])
            g.add("z", side, cos, coz.at[other], device(gz=beside["gz"][side]), there["gz"][side])
        return g

    spreads = plan_spreads()
    constants = [plan_constants(L0), plan_constants(L1)]

    def begin(*groups, only=None):
        for g in groups:
            for kind, copy, goes in g.copies:
                if only is not None and kind not in only:
                    continue
                if goes is True:
                    copy.start()
                    continue

                @pl.when(goes)
                def _():
                    copy.start()

    def arrive(*groups):
        await_all(groups[0].sem, groups)

    def pack(L, get, planes=None):
        got = jnp.zeros(tile, jnp.float32)
        for e in every:
            for i in (range(L.n) if planes is None else planes):
                j = e * L.n + i
                got = jnp.where(zi // (2 * L.s) == j, roll(get(e, i), 2 * L.s * j + L.s, 1), got)
        return got

    def unpack(L, tile_of, e, i):
        return roll(tile_of, -(2 * L.s * (e * L.n + i) + L.s), 1)

    def combine(L, low, high, ok=None):
        s = L.s
        up = zi % (2 * s) < s
        has_low, has_high = there["gz"]
        if ok is not None:
            has_low, has_high = has_low & ok, has_high & ok
        code = jnp.where(up, jnp.where(has_high, 1, 0), jnp.where(has_low, 2, 0))
        return jnp.where(code == 1, roll(high, -s, 1), jnp.where(code == 2, roll(low, s, 1), 0.0))

    def local(L, get, e, i):
        n, s = L.n, L.s
        v = get(e, i)
        q = L.cw[e, 2, i] * roll(v, -s, 0) + L.cw[e, 3, i] * roll(v, s, 0)
        q = q + L.cw[e, 4, i] * roll(v, -s, 1) + L.cw[e, 5, i] * roll(v, s, 1)
        if i < n - 1:
            q = q + L.cw[e, 0, i] * get(e, i + 1)
        if i > 0:
            q = q + L.cw[e, 1, i] * get(e, i - 1)
        return q + L.cb[e, i]

    def border(L, q, halo, e, i):
        gx_of, gy_of, term_z = halo
        q = q + L.st[e, 0, i] * gy_of(e, i) + term_z(e, i)
        if i == 0:
            q = q + L.xw[e, 0] * gx_of(0, e)
        if i == L.n - 1:
            q = q + L.xw[e, 1] * gx_of(1, e)
        return q

    def ends(L, packed):
        at = (zi < L.s) | (zi >= nz - L.s)
        return lambda e, i: jnp.where(at, unpack(L, packed, e, i), 0.0)

    def received(L, r, x_ref, y_ref, z_ref):
        my = edge_rows(L.s, *there["gy"])
        c = combine(L, z_ref[r, 0], z_ref[r, 1])
        return (
            lambda side, e: jnp.where(there["gx"][side], x_ref[r, side, e], 0.0),
            lambda e, i: jnp.where(my, y_ref[r, e, i], 0.0),
            ends(L, L.zs[0] * c),
            c,
        )

    def ring(L, r, get, own):
        n, s = L.n, L.s
        my = edge_rows(s, *there["gy"])
        lines_of = []
        columns_of = []
        for side in range(2):
            ok = there["gx"][side]
            mask = edge_rows(s, ok & there["gy"][0], ok & there["gy"][1])
            lines_of.append([jnp.where(mask, exy[r, side, e], 0.0) for e in every])
            columns_of.append(combine(L, exz[r, side, 0], exz[r, side, 1], ok))
        cy = jnp.where(my, combine(L, eyz[r, 0], eyz[r, 1]), 0.0)
        rx = [
            [
                jnp.where(
                    there["gx"][side],
                    px[r, side, e] + L.xt[side, e] * get(e, 0 if side == 0 else n - 1)
                    + L.xst[side, e, 0] * lines_of[side][e]
                    + L.xst[side, e, 1] * unpack(L, columns_of[side], e, n - 1 if side == 0 else 0),
                    0.0,
                )
                for e in every
            ]
            for side in range(2)
        ]

        def ry(e, i):
            got = py[r, e, i] + L.yst[e, i] * get(e, i)
            if i == 0:
                got = got + L.yxw[e, 0] * lines_of[0][e]
            if i == n - 1:
                got = got + L.yxw[e, 1] * lines_of[1][e]
            return jnp.where(my, got, 0.0)

        far = 2 * s * (n - 1)
        sideways = jnp.where(
            zi // (2 * s) % n == 0, roll(columns_of[0], -far, 1), roll(columns_of[1], far, 1)
        )
        toward, along_y, along_x = [combine(L, L.zst[0, k], L.zst[1, k]) for k in range(3)]
        c = combine(L, pz[r, 0], pz[r, 1]) + toward * own + along_y * cy + along_x * sideways
        c = jnp.where(zi < 2 * s * EQ * n, c, 0.0)
        y_ends = L.zs[1] * jnp.where(my, L.yzs[...] * cy, 0.0)
        return (
            lambda side, e: rx[side][e],
            ry,
            ends(L, L.zs[0] * c + y_ends),
        )

    def put(r, L, v):
        for e in every:
            for i in range(L.n):
                field[r, e, i] = v[e][i]

    def planes(f, L):
        return [[f(e, i) for i in range(L.n)] for e in every]

    def deep(r, L):
        get = lambda e, i: field[r, e, i]
        begin(plans[r]["d"], only=("xy",))
        zpack[r, 0] = pack(L, get)
        begin(plans[r]["d"], only=("xz", "yz"))
        begin(plans[r]["v"])
        for e in every:
            for i in range(L.n):
                pfield[r, e, i] = KEEP * get(e, i) + local(L, get, e, i)
        zpack[r, 1] = pack(L, lambda e, i: pfield[r, e, i])
        begin(plans[r]["p"])

        def finish():
            arrive(plans[r]["v"])
            halo = received(L, r, hx, hy, hz)[:3]
            new = planes(lambda e, i: border(L, pfield[r, e, i], halo, e, i), L)

            def outer():
                arrive(plans[r]["d"], plans[r]["p"])
                return ring(L, r, get, zpack[r, 0])

            return new, outer

        return finish

    def coarsen(a, s):
        n = a.shape[0]
        a = jnp.stack([a[2 * i] + a[2 * i + 1] for i in range(n // 2)])
        y, z = iota(a.shape, 1), iota(a.shape, 2)
        a = a + jnp.where((y // s) % 2 == 0, roll(a, -s, 1), roll(a, s, 1))
        a = a + jnp.where((z // s) % 2 == 0, roll(a, -s, 2), roll(a, s, 2))
        return a * 0.125

    def select(a, onehot):
        parts = []
        for _ in range(3):
            parts.append(a.astype(jnp.bfloat16))
            a = a - parts[-1].astype(jnp.float32)
        got = jnp.dot(jnp.concatenate(parts, axis=0), onehot, preferred_element_type=jnp.float32)
        m = a.shape[0]
        return (got[0:m] + got[m : 2 * m]) + got[2 * m :]

    groups = qx * qy
    source = iota((nz, nz), 0)
    target = iota((nz, nz), 1)
    squeeze = jnp.where(source == 4 * (target % qz), 1.0, 0.0).astype(jnp.bfloat16)
    squeeze_pairs = jnp.where(
        (source == 4 * (target % qz)) | (source == 4 * (target % qz) + 2), 1.0, 0.0
    ).astype(jnp.bfloat16)

    def to_rows(a, lanes):
        m = a.shape[0]
        c = select(a.reshape(m * qx * ny, nz), lanes).reshape(m, qx, ny, nz)
        place = iota((m, ny, nz), 2) // qz
        got = jnp.zeros((m, ny, nz), jnp.float32)
        for x in range(qx):
            for y in range(qy):
                part = roll(c[:, x], -4 * y, 1)
                got = jnp.where(place == (x * qy + y + gz) % groups, part, got)
        return got

    def own(small, whole, sem):
        return pltpu.make_async_copy(
            small.at[:, pl.ds(0, 1)], whole.at[X, core, :, pl.ds(row, 1)], sem
        )

    def stage(number, small, whole, rs):
        made = []
        if number == 0:
            for step in range(1, ngx):
                made.append((small.at[:, pl.ds(0, 1)], whole.at[X, core, :, pl.ds(row, 1)],
                             step, device(gx=(gx + step) % ngx)))
        elif number == 1:
            block = whole.at[X, core, :, pl.ds(gy * ngx, ngx)]
            for step in range(1, ngy):
                made.append((block, block, step, device(gy=(gy + step) % ngy)))
        elif number == 2:
            block = whole.at[X, core]
            for step in range(1, nX):
                made.append((block, block, step, device(gz=((X + step) % nX) * cores + core)))
        else:
            block = whole.at[:, core]
            for step in range(1, cores):
                made.append((block, block, step, device(gz=X * cores + (core + step) % cores)))
        return [
            remote(a, z, ws_sem.at[number], rs.at[number], where)
            for a, z, _, where in made
        ]

    wargs = (wsend, wall, wr_sem)

    def everyone():
        mirrored = all(count & (count - 1) == 0 for count in dims)

        def other(index, step, count):
            return index ^ step if mirrored else (index + step) % count

        made = []
        for ay in reversed(range(ngy)):
            for az in reversed(range(ngz)):
                for ax in reversed(range(ngx)):
                    if ax + ay + az == 0:
                        continue
                    made.append(remote(
                        bsend.at[:, pl.ds(0, 1)], ball.at[X, core, :, pl.ds(row, 1)],
                        bs_sem, br_sem,
                        (other(gx, ax, ngx), other(gy, ay, ngy), other(gz, az, ngz)),
                    ))
        return made

    def start(number):
        for copy in stage(number, *wargs):
            copy.start()

    def stage_rows(number):
        return 7 * EQ * (
            ngx - 1, ngx * (ngy - 1), rows * (nX - 1), nX * rows * (cores - 1)
        )[number]

    def done(number):
        await_rows(wr_sem.at[number], stage_rows(number))

    def scale(L, get_w, get_d, e, i):
        n, s = L.n, L.s
        raw = [get_w(e, k, i) for k in range(6)]
        total = get_d(e, i)
        for k in range(6):
            total = total + raw[k]
        c = DAMP / total
        w = [c * raw[k] for k in range(6)]
        L.tot[e, i] = (1.0 / DAMP) * total
        last_y, first_y, last_z, first_z = yi >= ny - s, yi < s, zi >= nz - s, zi < s
        L.cw[e, 0, i] = w[0]
        L.cw[e, 1, i] = w[1]
        L.cw[e, 2, i] = jnp.where(last_y, 0.0, w[2])
        L.cw[e, 3, i] = jnp.where(first_y, 0.0, w[3])
        L.cw[e, 4, i] = jnp.where(last_z, 0.0, w[4])
        L.cw[e, 5, i] = jnp.where(first_z, 0.0, w[5])
        L.st[e, 0, i] = jnp.where(last_y, w[2], jnp.where(first_y, w[3], 0.0))
        L.st[e, 1, i] = jnp.where(last_z, w[4], jnp.where(first_z, w[5], 0.0))
        if i == 0:
            L.xw[e, 0] = w[1]
        if i == n - 1:
            L.xw[e, 1] = w[0]
        if L is L1:
            odd_y, odd_z = yi // s % 2 == 1, zi // s % 2 == 1
            co[e, 1, i] = w[0] if i % 2 == 1 else w[1]
            co[e, 2, i] = jnp.where(odd_y, w[2], w[3])
            co[e, 3, i] = jnp.where(odd_z, w[4], w[5])
            co[e, 0, i] = (
                KEEP + (w[1] if i % 2 == 1 else w[0])
                + jnp.where(odd_y, w[3], w[2]) + jnp.where(odd_z, w[5], w[4])
            )
        return c

    def pack_constants(L):
        L.zs[0] = pack(L, lambda e, i: L.st[e, 1, i])
        L.zs[1] = pack(L, lambda e, i: L.st[e, 0, i])
        L.zs[2] = pack(L, lambda e, i: L.xw[e, 0 if i == 0 else 1], (0, L.n - 1))

    for load in guess_loads:
        load.wait()
    guess = lambda e, i: g_ref[e, i]
    zpack[0, 0] = pack(L0, guess)
    pl.semaphore_wait(barrier, awaited)
    begin(plans[0]["v"])
    hear = found[0] + found[1] + found[2]

    def tell(k):
        for name, _, _ in axes:
            for side in range(2):
                @pl.when(there[name][side])
                def _():
                    pl.semaphore_signal(
                        know.at[k], inc=1, device_id=device(**{name: beside[name][side]}),
                        device_id_type=MESH,
                    )

    if close:
        tell(0)
    await_rows(i_sem.at[1], 8 * EQ * nx * ny)
    level2 = [None] * (7 * EQ)
    for e in every:
        d1 = coarsen(d_ref[e], 1)
        level2[6 * EQ + e] = coarsen(d1, 2)
        for k in range(6):
            w = 0.25 * coarsen(w_ref[6 * e + k], 1)
            w1[6 * e + k] = w
            level2[6 * e + k] = 0.25 * coarsen(w, 2)
        for i in range(half):
            c = scale(L1, lambda e, k, i: w1[6 * e + k, i], lambda e, i: d1[i], e, i)
            w1[6 * EQ + e, i] = c
    wsend[...] = to_rows(jnp.stack(level2), squeeze)
    own(wsend, wall, i_sem.at[0]).start()
    start(0)
    for e in every:
        for i in range(nx):
            c = scale(L0, lambda e, k, i: w_ref[6 * e + k, i], lambda e, i: d_ref[e, i], e, i)
            L0.cb[e, i] = c * b_ref[e, i]
    pack_constants(L0)
    begin(constants[0])
    for e in every:
        for i in range(nx):
            pfield[0, e, i] = KEEP * guess(e, i) + local(L0, guess, e, i)
    if close:
        pl.semaphore_wait(know.at[0], hear)
        tell(1)

    arrive(plans[0]["v"])
    halo = received(L0, 0, hx, hy, hz)[:3]
    put(1, L0, planes(lambda e, i: border(L0, pfield[0, e, i], halo, e, i), L0))
    if close:
        pl.semaphore_wait(know.at[1], hear)
    finish = deep(1, L0)
    own(wsend, wall, i_sem.at[0]).wait()
    done(0)
    start(1)
    pack_constants(L1)
    begin(constants[1])
    v, outer = finish()
    kept0 = field.at[0]
    for e in every:
        for i in range(nx):
            kept0[e, i] = v[e][i]
    get = lambda e, i: kept0[e, i]
    q = planes(lambda e, i: local(L0, get, e, i), L0)
    arrive(constants[0])
    halo = outer()
    first = []
    for e in every:
        r = jnp.stack([
            L0.tot[e, i] * (border(L0, q[e][i], halo, e, i) - DAMP * get(e, i)) for i in range(nx)
        ])
        b = coarsen(r, 1)
        first.append([])
        for i in range(half):
            u = w1[6 * EQ + e, i] * b[i]
            L1.cb[e, i] = u
            first[e].append(u)
    put(2, L1, first)
    finish = deep(2, L1)
    done(1)
    start(2)
    for m in range(4):
        cos[m] = pack(L1, lambda e, i: co[e, m, i])
    begin(spreads)
    u, outer = finish()
    kept1 = pfield.at[3]
    for e in every:
        for i in range(half):
            kept1[e, i] = u[e][i]
    get = lambda e, i: kept1[e, i]
    q = planes(lambda e, i: local(L1, get, e, i), L1)
    arrive(constants[1])
    halo = outer()
    rest = []
    for e in every:
        r = []
        for i in range(half):
            total = border(L1, q[e][i], halo, e, i)
            field[3, e, i] = KEEP * get(e, i) + total
            r.append(L1.tot[e, i] * (total - DAMP * get(e, i)))
        r = [r[2 * x] + r[2 * x + 1] for x in range(qx)]
        rest.append(jnp.stack([c + roll(c, -2, 0) for c in r]))
    bsend[...] = 0.125 * to_rows(jnp.stack(rest), squeeze_pairs)
    for copy in everyone():
        copy.start()
    own(bsend, ball, br_sem).start()
    zpack[3, 0] = pack(L1, lambda e, i: field[3, e, i])
    begin(plans[3]["v"])
    arrive(spreads)
    for m in range(4):
        c = combine(L1, coz[0, m], coz[1, m])
        for e in every:
            for i in range(half):
                zco[e, m, i] = unpack(L1, c, e, i)
    NX, NY, NZ = ngx * qx, ngy * qy, ngz * qz
    shape = (NZ, 3 * nz)
    kind, t = iota(shape, 1) // nz, iota(shape, 1) % nz
    base = gz * qz + t // 4
    wanted = jnp.where(
        kind == 0, base,
        jnp.where(
            kind == 1, base + jnp.where(t % 4 < 2, -1, 1),
            jnp.where(t < nz // 2, gz * qz - 1, gz * qz + qz),
        ),
    )
    widen[...] = jnp.where(iota(shape, 0) == wanted, 1.0, 0.0).astype(jnp.bfloat16)
    for e in every:
        for i in range(NX + 2):
            if i in (0, NX + 1):
                e2[e, i] = jnp.zeros((NY + 16, NZ), jnp.float32)
            else:
                e2[e, i, 0:8] = jnp.zeros((8, NZ), jnp.float32)
                e2[e, i, NY + 8 : NY + 16] = jnp.zeros((8, NZ), jnp.float32)
    done(2)
    start(3)
    done(3)
    def spread(ref, index):
        place, y_of = iota((rows, nz), 1) // qz, iota((NY, nz), 0) % qy
        parts = [[] for _ in range(NX)]
        for t in range(NZ // nz):
            moved = []
            for k in range(groups):
                got = None
                for p in range(groups):
                    g = t * groups + (p - k) % groups
                    a = ref[g // cores, g % cores, index]
                    got = a if got is None else jnp.where(place == p, a, got)
                moved.append(roll(got, -k * qz, 1))
            for x in range(qx):
                if ngx != qy:
                    for y in range(qy):
                        mix[...] = moved[x * qy + y]
                        for g in range(ngx):
                            mixed[g, pl.ds(y, ngy, stride=qy), :] = mix[pl.ds(g, ngy, stride=ngx), :]
                for g in range(ngx):
                    if ngx != qy:
                        got = mixed[g]
                    else:
                        got = roll(moved[x * qy], -g, 0)
                        for y in range(1, qy):
                            got = jnp.where(y_of == y, roll(moved[x * qy + y], y - g, 0), got)
                    parts[g * qx + x].append(got)
        return [p[0] if len(p) == 1 else jnp.concatenate(p, axis=1) for p in parts]

    Y, Z = iota((NY, NZ), 0), iota((NY, NZ), 1)
    even_y, even_z = Y % 2 == 0, Z % 2 == 0
    pairs = NX // 4

    def halve(a):
        made = []
        for p in range(pairs):
            two = []
            for x in (2 * p, 2 * p + 1):
                c = a[2 * x] + a[2 * x + 1]
                two.append(c + jnp.where(even_y, roll(c, -1, 0), roll(c, 1, 0)))
            c = jnp.where(even_y, two[0], two[1])
            made.append(0.125 * (c + jnp.where(even_z, roll(c, -1, 1), roll(c, 1, 1))))
        return made

    def double(a, x):
        c = a[x // 4]
        if x // 2 % 2 == 0:
            return jnp.where(even_y, c, roll(c, 1, 0))
        return jnp.where(even_y, roll(c, -1, 0), c)

    def tree(terms):
        while len(terms) > 1:
            terms = [
                terms[k] + terms[k + 1] if k + 1 < len(terms) else terms[k]
                for k in range(0, len(terms), 2)
            ]
        return terms[0]

    def around2(w, v):
        made = []
        for x in range(NX):
            terms = [
                w[4][x] * roll(v[x], -1, 1), w[5][x] * roll(v[x], 1, 1),
                w[2][x] * roll(v[x], -1, 0), w[3][x] * roll(v[x], 1, 0),
            ]
            if x < NX - 1:
                terms.append(w[0][x] * v[x + 1])
            if x > 0:
                terms.append(w[1][x] * v[x - 1])
            made.append(tree(terms))
        return made

    def around3(w, v):
        made = []
        for p in range(pairs):
            up, down = roll(v[p], -1, 0), roll(v[p], 1, 0)
            if p < pairs - 1:
                up = jnp.where(even_y, up, roll(v[p + 1], 1, 0))
            if p > 0:
                down = jnp.where(even_y, roll(v[p - 1], -1, 0), down)
            made.append(tree([
                w[4][p] * roll(v[p], -2, 1), w[5][p] * roll(v[p], 2, 1),
                w[0][p] * up, w[1][p] * down,
                w[2][p] * roll(v[p], -2, 0), w[3][p] * roll(v[p], 2, 0),
            ]))
        return made

    steps3 = ((-1, 0), (1, 0), (-2, 0), (2, 0), (0, -2), (0, 2))

    def shifted(v, dr, dl):
        return roll(roll(v, dl, 1), dr, 0)

    def twice(w):
        got = {(0, 0): KEEP * KEEP}

        def add(at, value):
            at = (at[0] % NY, at[1] % NZ)
            got[at] = got[at] + value if at in got else value

        for k, (dr, dl) in enumerate(steps3):
            add((dr, dl), 2.0 * KEEP * w[k])
            for m, (er, el) in enumerate(steps3):
                if k == m and k < 2:
                    continue
                add((dr + er, dl + el), w[k] * shifted(w[m], dr, dl))
        return got

    def apply_twice(w, v):
        turned = {dl: roll(v, dl, 1) for dl in sorted({at[1] for at in w})}
        return tree([c * roll(turned[dl], dr, 0) for (dr, dl), c in w.items()])

    def inner(w, k, at, last, step):
        if k == 0 and step == 2:
            return jnp.where(even_y, w, 0.0) if at == last else w
        if k == 1 and step == 2:
            return jnp.where(even_y, 0.0, w) if at == 0 else w
        if k < 2:
            return w
        return jnp.where((Y >= NY - step, Y < step, Z >= NZ - step, Z < step)[k - 2], 0.0, w)

    def constants_of(plain, diagonal, count, step):
        scaled, totals, weights = [], [], [[] for _ in range(6)]
        for at in range(count):
            total = diagonal[at] + tree([plain[k][at] for k in range(6)])
            scaled.append(DAMP / total)
            totals.append((1.0 / DAMP) * total)
            for k in range(6):
                weights[k].append(inner(scaled[at] * plain[k][at], k, at, count - 1, step))
        return scaled, totals, weights

    c2, t2, w2, c3, w3, ww3 = [], [], [], [], [], []
    by_two = pairs == 1 and NY >= 8 and COARSE_SWEEPS % 2 == 0
    for e in every:
        plain = [spread(wall, 6 * e + k) for k in range(6)]
        diagonal = spread(wall, 6 * EQ + e)
        scaled, totals, weights = constants_of(plain, diagonal, NX, 1)
        c2.append(scaled)
        t2.append(totals)
        w2.append(weights)
        coarse = [[0.25 * c for c in halve(plain[k])] for k in range(6)]
        scaled, _, weights = constants_of(coarse, halve(diagonal), pairs, 2)
        c3.append(scaled)
        w3.append(weights)
        if by_two:
            ww3.append(twice([weights[k][0] for k in range(6)]))

    arrive(plans[3]["v"])
    pltpu.make_async_copy(ball, ball, br_sem).wait()
    rhs = []
    for e in every:
        got = spread(ball, e)
        rhs.append([c2[e][x] * got[x] for x in range(NX)])

    def smooth2(v):
        made = []
        for e in every:
            sums = around2(w2[e], v[e])
            made.append([(KEEP * v[e][x] + rhs[e][x]) + sums[x] for x in range(NX)])
        return made

    v2 = rhs
    for step in range(SWEEPS - 1):
        v2 = smooth2(v2)
    rhs3 = []
    for e in every:
        sums = around2(w2[e], v2[e])
        got = halve([t2[e][x] * ((rhs[e][x] - DAMP * v2[e][x]) + sums[x]) for x in range(NX)])
        rhs3.append([c3[e][p] * got[p] for p in range(pairs)])
    v3 = rhs3
    for step in range(1 if by_two else COARSE_SWEEPS - 1):
        sums = [around3(w3[e], v3[e]) for e in every]
        v3 = [
            [(KEEP * v3[e][p] + rhs3[e][p]) + sums[e][p] for p in range(pairs)] for e in every
        ]
    if by_two:
        once = v3
        for step in range(COARSE_SWEEPS // 2 - 1):
            v3 = [[apply_twice(ww3[e], v3[e][0]) + once[e][0]] for e in every]
    v2 = [[v2[e][x] + double(v3[e], x) for x in range(NX)] for e in every]
    for step in range(SWEEPS):
        v2 = smooth2(v2)
    for e in every:
        for x in range(NX):
            e2[e, x + 1, 8 : 8 + NY] = v2[e][x]

    wx, wy = qx + 2, qy + 2
    for e in every:
        for i in range(wx):
            for j in range(wy):
                at = (e * wx + i) * wy + j
                lines[at : at + 1, :] = e2[e, gx * qx + i, pl.ds(7 + gy * qy + j, 1), :]
    broad[...] = select(lines[...], widen[...])
    CENTER, BEYOND_Z, OUTSIDE_Z = range(3)
    ysel, yhalf = yi // 4, yi // 2 % 2

    def strip(kind, e, x, y):
        at = (e * wx + x + 1) * wy + y + 1
        return jnp.broadcast_to(broad[at : at + 1, kind * nz : kind * nz + nz], tile)

    def plane(kind, e, x):
        got = strip(kind, e, x, 0)
        for y in range(1, qy):
            got = jnp.where(ysel == y, strip(kind, e, x, y), got)
        return got

    def across_y(kind, e, x):
        got = None
        for y in range(qy):
            both = jnp.where(yhalf == 0, strip(kind, e, x, y - 1), strip(kind, e, x, y + 1))
            got = both if got is None else jnp.where(ysel == y, both, got)
        return got

    def across_x(kind, e, i):
        return plane(kind, e, i // 2 + (1 if i % 2 == 1 else -1))

    def rows_y(kind, e, x):
        return jnp.where(yi < ny // 2, strip(kind, e, x, -1), strip(kind, e, x, qy))

    left, behind, _, columns = received(L1, 3, hx, hy, hz)
    mine = edge_rows(L1.s, *there["gy"])

    def add_x(side, e):
        face, near = (-1, 0) if side == 0 else (qx, qx - 1)
        got = left(side, e) + cox[side, e, 0] * plane(CENTER, e, face)
        got = got + cox[side, e, 1] * plane(CENTER, e, near)
        got = got + cox[side, e, 2] * across_y(CENTER, e, face)
        got = got + cox[side, e, 3] * plane(BEYOND_Z, e, face)
        return jnp.where(there["gx"][side], got, 0.0)

    def add_y(e, i):
        x = i // 2
        got = behind(e, i) + coy[e, 0, i] * rows_y(CENTER, e, x)
        got = got + coy[e, 1, i] * rows_y(CENTER, e, x + 1 if i % 2 == 1 else x - 1)
        got = got + coy[e, 2, i] * plane(CENTER, e, x)
        got = got + coy[e, 3, i] * rows_y(BEYOND_Z, e, x)
        return jnp.where(mine, got, 0.0)

    def add_z(e, i):
        x = i // 2
        got = unpack(L1, columns, e, i) + zco[e, 0, i] * plane(OUTSIDE_Z, e, x)
        got = got + zco[e, 1, i] * across_x(OUTSIDE_Z, e, i)
        got = got + zco[e, 2, i] * across_y(OUTSIDE_Z, e, x)
        return L1.st[e, 1, i] * (got + zco[e, 3, i] * plane(CENTER, e, x))

    swept = pfield.at[3]
    for e in every:
        for i in range(half):
            x = i // 2
            got = field[3, e, i] + co[e, 0, i] * plane(CENTER, e, x)
            got = got + co[e, 1, i] * across_x(CENTER, e, i)
            got = got + co[e, 2, i] * across_y(CENTER, e, x)
            swept[e, i] = got + co[e, 3, i] * plane(BEYOND_Z, e, x)
    get = lambda e, i: swept[e, i]
    halo = (add_x, add_y, add_z)
    u = planes(lambda e, i: KEEP * get(e, i) + border(L1, local(L1, get, e, i), halo, e, i), L1)
    put(4, L0, planes(lambda e, i: kept0[e, i] + u[e][i // 2], L0))
    finish = deep(4, L0)
    v, outer = finish()
    last = pfield.at[0]
    for e in every:
        for i in range(nx):
            last[e, i] = v[e][i]
    get = lambda e, i: last[e, i]
    q = planes(lambda e, i: KEEP * get(e, i) + local(L0, get, e, i), L0)
    halo = outer()
    for e in every:
        for i in range(nx):
            out_ref[e, i] = border(L0, q[e][i], halo, e, i)
    await_all(s_sem, [g for p in plans for g in p.values()] + constants + [spreads])
    for number in range(4):
        await_rows(ws_sem.at[number], stage_rows(number))
    await_rows(bs_sem, EQ * (rows * ngz - 1))


def per_device(dims, cores, couplings, diagonal, right_side, guess):
    ngx, ngy, ngz = dims
    brick = guess.shape[1:]
    nx, ny, nz = brick
    half = nx // 2
    qx, qy, qz = nx // 4, ny // 4, nz // 4
    rows = ngx * ngy
    nX = ngz // cores
    rounds = len(DEEP)
    f32 = jnp.float32
    vmem = pltpu.VMEM
    dma = pltpu.SemaphoreType.DMA

    def level(n):
        return [
            vmem((EQ, 6, n, ny, nz), f32),
            vmem((EQ, 2, n, ny, nz), f32),
            vmem((EQ, 2, ny, nz), f32),
            vmem((EQ, n, ny, nz), f32),
            vmem((EQ, n, ny, nz), f32),
            vmem((3, ny, nz), f32),
            vmem((2, EQ, ny, nz), f32),
            vmem((2, EQ, 2, ny, nz), f32),
            vmem((EQ, n, ny, nz), f32),
            vmem((ny, nz), f32),
            vmem((EQ, 2, ny, nz), f32),
            vmem((2, 3, ny, nz), f32),
            dma,
        ]

    faces = [
        vmem((rounds, 2, EQ, ny, nz), f32),
        vmem((rounds, EQ) + brick, f32),
        vmem((rounds, 2, ny, nz), f32),
    ]
    return pl.pallas_call(
        functools.partial(kernel, dims, cores),
        out_shape=vmem(guess.shape, f32),
        in_specs=[pl.BlockSpec(memory_space=pl.ANY)] * 4,
        out_specs=pl.BlockSpec(memory_space=vmem),
        scratch_shapes=[
            vmem(couplings.shape, f32),
            vmem(diagonal.shape, f32),
            vmem(right_side.shape, f32),
            vmem(guess.shape, f32),
            vmem((max(2048, nX * rows * 7 * EQ * (cores - 1) // 8, rows * (nX - 1) * 7 * EQ // 8), 8, nz), f32),
            vmem((rounds, EQ) + brick, f32),
            vmem((rounds, EQ) + brick, f32),
            vmem((rounds, 2, ny, nz), f32),
            *faces,
            *faces,
            vmem((rounds, 2, EQ, ny, nz), f32),
            vmem((rounds, 2, 2, ny, nz), f32),
            vmem((rounds, 2, ny, nz), f32),
            vmem((7 * EQ, half, ny, nz), f32),
            vmem((EQ, 4, half, ny, nz), f32),
            vmem((4, ny, nz), f32),
            vmem((2, EQ, 4, ny, nz), f32),
            vmem((EQ, 4, half, ny, nz), f32),
            vmem((2, 4, ny, nz), f32),
            vmem((EQ, 4, half, ny, nz), f32),
            *level(nx),
            *level(half),
            vmem((7 * EQ, ny, nz), f32),
            vmem((nX, cores, 7 * EQ, rows, nz), f32),
            vmem((EQ, ny, nz), f32),
            vmem((nX, cores, EQ, rows, nz), f32),
            vmem((EQ, ngx * qx + 2, ngy * qy + 16, ngz * qz), f32),
            vmem((EQ * (qx + 2) * (qy + 2), ngz * qz), f32),
            vmem((EQ * (qx + 2) * (qy + 2), 3 * nz), f32),
            vmem((ngz * qz, 3 * nz), jnp.bfloat16),
            vmem((rows, nz), f32),
            vmem((ngx, ngy * qy, nz), f32),
            dma,
            dma((4,)),
            dma,
            dma((4,)),
            dma((4,)),
            dma,
            dma,
            dma((2,)),
            dma((3,)),
            pltpu.SemaphoreType.REGULAR((2,)),
        ],
        compiler_params=pltpu.CompilerParams(
            collective_id=0, has_side_effects=True, vmem_limit_bytes=60 * 1024 * 1024
        ),
    )(couplings, diagonal, right_side, guess)


def solution(mesh):
    dims = (mesh.shape["gx"], mesh.shape["gy"], mesh.shape["gz"])
    cores = 2 if dims[2] % 2 == 0 else 1
    spec = P(None, "gx", "gy", "gz")
    return jax.shard_map(
        functools.partial(per_device, dims, cores),
        mesh=mesh,
        in_specs=(spec,) * 4,
        out_specs=spec,
        check_vma=False,
    )
```

```python
import functools

import jax
import jax.numpy as jnp
from jax import lax
from jax.experimental import pallas as pl
from jax.experimental.pallas import tpu as pltpu
from jax.sharding import PartitionSpec as P

SWEEPS = 2
COARSE_SWEEPS = 8
DAMP = 0.8
KEEP = 1.0 - DAMP
EQ = 3
MESH = pl.DeviceIdType.MESH
HIGH = lax.Precision.HIGHEST
DEEP = (False, True, True, False, True)
FINE = (True, True, False, False, True)


def roll(value, shift, axis):
    size = value.shape[axis]
    shift = shift % size
    return value if shift == 0 else pltpu.roll(value, shift, axis)


def iota(shape, axis):
    return lax.broadcasted_iota(jnp.int32, shape, axis)


class Level:
    def __init__(self, n, s, refs):
        self.n, self.s = n, s
        (self.cw, self.st, self.xw, self.cb, self.tot, self.zs,
         self.xt, self.xst, self.yst, self.yzs, self.yxw, self.zst, self.r_sem) = refs


def kernel(
    dims, cores, w_hbm, d_hbm, b_hbm, g_hbm, out_ref,
    w_ref, d_ref, b_ref, g_ref,
    tally, field, pfield, zpack, hx, hy, hz, px, py, pz, exy, exz, eyz, w1, co, cos, cox, coy, coz, zco, *rest,
):
    level_refs = (rest[:13], rest[13:26])
    (wsend, wall, bsend, ball, e2, lines, broad, widen, mix, mixed,
     s_sem, r_sem, co_sem, ws_sem, wr_sem, bs_sem, br_sem, i_sem, g_sem, know) = rest[26:]
    ngx, ngy, ngz = dims
    nx, ny, nz = g_ref.shape[1:]
    half = nx // 2
    qx, qy, qz = nx // 4, ny // 4, nz // 4
    rows = ngx * ngy
    nX = ngz // cores
    gx, gy, gz = lax.axis_index("gx"), lax.axis_index("gy"), lax.axis_index("gz")
    X, core = gz // cores, gz % cores
    row = gy * ngx + gx
    axes = (("gx", gx, ngx), ("gy", gy, ngy), ("gz", gz, ngz))
    L0 = Level(nx, 1, level_refs[0])
    L1 = Level(half, 2, level_refs[1])
    tile = (ny, nz)
    yi, zi = iota(tile, 0), iota(tile, 1)
    every = range(EQ)

    def device(**change):
        here = {"gx": gx, "gy": gy, "gz": gz}
        here.update(change)
        return (here["gx"], here["gy"], here["gz"])

    guess_loads = [pltpu.make_async_copy(g_hbm.at[e], g_ref.at[e], g_sem.at[e]) for e in range(EQ)]
    for load in guess_loads:
        load.start()
    barrier = pltpu.get_barrier_semaphore()
    close = ngy <= 4 and ngz <= 4
    awaited = 0

    def greet(ok, where):
        @pl.when(ok)
        def _():
            pl.semaphore_signal(barrier, inc=1, device_id=where, device_id_type=MESH)
        return ok.astype(jnp.int32)

    for name, index, count in axes:
        if close and name != "gx":
            steps = (-1, 1)
            for step in steps:
                ok = (index + step >= 0) & (index + step < count)
                awaited = awaited + greet(ok, device(**{name: jnp.clip(index + step, 0, count - 1)}))
        else:
            for step in range(1, count):
                pl.semaphore_signal(
                    barrier, inc=1, device_id=device(**{name: (index + step) % count}),
                    device_id_type=MESH,
                )
            awaited = awaited + (count - 1)

    for a, z in ((w_hbm, w_ref), (d_hbm, d_ref), (b_hbm, b_ref)):
        pltpu.make_async_copy(a, z, i_sem.at[1]).start()

    there = {
        name: (index > 0, index < count - 1) for name, index, count in axes
    }
    beside = {
        name: (jnp.maximum(index - 1, 0), jnp.minimum(index + 1, count - 1))
        for name, index, count in axes
    }

    def edge_rows(s, lo, hi):
        return (yi < jnp.where(lo, s, 0)) | (yi >= jnp.where(hi, ny - s, ny))

    def remote(a, z, ss, rs, where):
        return pltpu.make_async_remote_copy(
            src_ref=a, dst_ref=z, send_sem=ss, recv_sem=rs,
            device_id=where, device_id_type=MESH,
        )

    def rows_of(side, s):
        return pl.ds(0 if side == 0 else ny - s, s)

    counts = [
        [k for k in (0, 1, 2) if (k > 0 or count == 1) and k < count and (k == 2 or count <= 2 or k == 1)]
        for _, _, count in axes
    ]
    found = [
        there[name][0].astype(jnp.int32) + there[name][1].astype(jnp.int32) for name, _, _ in axes
    ]
    cases = []
    for cx in counts[0]:
        for cy in counts[1]:
            for cz in counts[2]:
                cases.append(((cx, cy, cz), (found[0] == cx) & (found[1] == cy) & (found[2] == cz)))

    def await_rows(sem, number):
        if number > 0:
            part = next(k for k in (8, 4, 2, 1) if number % k == 0)
            ref = tally.at[pl.ds(0, number // part), pl.ds(0, part)]
            pltpu.make_async_copy(ref, ref, sem).wait()

    def await_all(sem, groups):
        for (cx, cy, cz), ok in cases:
            many = {"x": cx, "y": cy, "z": cz, "xy": cx * cy, "xz": cx * cz, "yz": cy * cz}
            number = sum(many[kind] * size for g in groups for kind, size in g.sizes.items())
            if len(cases) == 1:
                await_rows(sem, number)
            else:
                @pl.when(ok)
                def _():
                    await_rows(sem, number)

    class Group:
        def __init__(self, sem):
            self.sem, self.copies, self.sizes = sem, [], {}

        def add(self, kind, side, a, z, where, goes):
            self.copies.append((kind, remote(a, z, s_sem, self.sem, where), goes))
            if side == 0:
                size = 1
                for d in z.shape[:-1]:
                    size *= d
                self.sizes[kind] = self.sizes.get(kind, 0) + size

    def sides_of_x(n):
        if ngx == 2:
            return [(0, (1 - gx) * (n - 1), 1 - gx, gx, 1 - gx, True)]
        return [
            (side, 0 if side == 0 else n - 1, side, 1 - side, beside["gx"][side], there["gx"][side])
            for side in range(2)
        ]

    def both(a, b):
        return b if a is True else a & b

    def plan(r):
        n, s = (nx, 1) if FINE[r] else (half, 2)
        src = g_ref if r == 0 else field.at[r]
        groups = {k: Group(r_sem.at[r % 2 if k == "v" else 2 + r // 2 % 2]) for k in "vdp"}
        kinds = [("v", src, 0, hx, hy, hz)]
        if DEEP[r]:
            kinds.append(("p", pfield.at[r], 1, px, py, pz))
        for side, plane_at, _, other, to, ok in sides_of_x(n):
            for group, a, which, zx, zy, zz in kinds:
                groups[group].add("x", side, a.at[:, plane_at], zx.at[r, other], device(gx=to), ok)
        for side in range(2):
            other = 1 - side
            for group, a, which, zx, zy, zz in kinds:
                g = groups[group]
                g.add("y", side, a.at[:, 0:n, rows_of(side, s)], zy.at[r, :, 0:n, rows_of(other, s)],
                      device(gy=beside["gy"][side]), there["gy"][side])
                g.add("z", side, zpack.at[r, which], zz.at[r, other],
                      device(gz=beside["gz"][side]), there["gz"][side])
        if DEEP[r]:
            g = groups["d"]
            for i, plane_at, _, other, to, ok in sides_of_x(n):
                for j in range(2):
                    g.add("xy", 2 * i + j, src.at[:, plane_at, rows_of(j, s)],
                          exy.at[r, other, :, rows_of(1 - j, s)],
                          device(gx=to, gy=beside["gy"][j]), both(ok, there["gy"][j]))
                    g.add("xz", 2 * i + j, zpack.at[r, 0], exz.at[r, other, 1 - j],
                          device(gx=to, gz=beside["gz"][j]), both(ok, there["gz"][j]))
            for i in range(2):
                for j in range(2):
                    g.add("yz", 2 * i + j, zpack.at[r, 0, rows_of(i, s)], eyz.at[r, 1 - j, rows_of(1 - i, s)],
                          device(gy=beside["gy"][i], gz=beside["gz"][j]),
                          there["gy"][i] & there["gz"][j])
        return groups

    plans = [plan(r) for r in range(len(DEEP))]

    def plan_constants(L):
        g = Group(L.r_sem)
        for side, plane_at, mine, other, to, ok in sides_of_x(L.n):
            g.add("x", side, L.xw.at[:, mine], L.xt.at[other], device(gx=to), ok)
            g.add("x", side, L.st.at[:, :, plane_at], L.xst.at[other], device(gx=to), ok)
        for side in range(2):
            other = 1 - side
            y_at, y_ok = device(gy=beside["gy"][side]), there["gy"][side]
            g.add("y", side, L.st.at[:, 0, :, rows_of(side, L.s)],
                  L.yst.at[:, :, rows_of(other, L.s)], y_at, y_ok)
            g.add("y", side, L.zs.at[0, rows_of(side, L.s)], L.yzs.at[rows_of(other, L.s)], y_at, y_ok)
            g.add("y", side, L.xw.at[:, :, rows_of(side, L.s)], L.yxw.at[:, :, rows_of(other, L.s)], y_at, y_ok)
            g.add("z", side, L.zs, L.zst.at[other], device(gz=beside["gz"][side]), there["gz"][side])
        return g

    def plan_spreads():
        g = Group(co_sem)
        s = L1.s
        for side, plane_at, _, other, to, ok in sides_of_x(half):
            g.add("x", side, co.at[:, :, plane_at], cox.at[other], device(gx=to), ok)
        for side in range(2):
            other = 1 - side
            g.add("y", side, co.at[:, :, :, rows_of(side, s)], coy.at[:, :, :, rows_of(other, s)],
                  device(gy=beside["gy"][side]), there["gy"][side])
            g.add("z", side, cos, coz.at[other], device(gz=beside["gz"][side]), there["gz"][side])
        return g

    spreads = plan_spreads()
    constants = [plan_constants(L0), plan_constants(L1)]

    def begin(*groups, only=None):
        for g in groups:
            for kind, copy, goes in g.copies:
                if only is not None and kind not in only:
                    continue
                if goes is True:
                    copy.start()
                    continue

                @pl.when(goes)
                def _():
                    copy.start()

    def arrive(*groups):
        await_all(groups[0].sem, groups)

    def pack(L, get, planes=None):
        got = jnp.zeros(tile, jnp.float32)
        for e in every:
            for i in (range(L.n) if planes is None else planes):
                j = e * L.n + i
                got = jnp.where(zi // (2 * L.s) == j, roll(get(e, i), 2 * L.s * j + L.s, 1), got)
        return got

    def unpack(L, tile_of, e, i):
        return roll(tile_of, -(2 * L.s * (e * L.n + i) + L.s), 1)

    def combine(L, low, high, ok=None):
        s = L.s
        up = zi % (2 * s) < s
        has_low, has_high = there["gz"]
        if ok is not None:
            has_low, has_high = has_low & ok, has_high & ok
        code = jnp.where(up, jnp.where(has_high, 1, 0), jnp.where(has_low, 2, 0))
        return jnp.where(code == 1, roll(high, -s, 1), jnp.where(code == 2, roll(low, s, 1), 0.0))

    def local(L, get, e, i):
        n, s = L.n, L.s
        v = get(e, i)
        q = L.cw[e, 2, i] * roll(v, -s, 0) + L.cw[e, 3, i] * roll(v, s, 0)
        q = q + L.cw[e, 4, i] * roll(v, -s, 1) + L.cw[e, 5, i] * roll(v, s, 1)
        if i < n - 1:
            q = q + L.cw[e, 0, i] * get(e, i + 1)
        if i > 0:
            q = q + L.cw[e, 1, i] * get(e, i - 1)
        return q + L.cb[e, i]

    def border(L, q, halo, e, i):
        gx_of, gy_of, term_z = halo
        q = q + L.st[e, 0, i] * gy_of(e, i) + term_z(e, i)
        if i == 0:
            q = q + L.xw[e, 0] * gx_of(0, e)
        if i == L.n - 1:
            q = q + L.xw[e, 1] * gx_of(1, e)
        return q

    def ends(L, packed):
        at = (zi < L.s) | (zi >= nz - L.s)
        return lambda e, i: jnp.where(at, unpack(L, packed, e, i), 0.0)

    def received(L, r, x_ref, y_ref, z_ref):
        my = edge_rows(L.s, *there["gy"])
        c = combine(L, z_ref[r, 0], z_ref[r, 1])
        return (
            lambda side, e: jnp.where(there["gx"][side], x_ref[r, side, e], 0.0),
            lambda e, i: jnp.where(my, y_ref[r, e, i], 0.0),
            ends(L, L.zs[0] * c),
            c,
        )

    def ring(L, r, get, own):
        n, s = L.n, L.s
        my = edge_rows(s, *there["gy"])
        lines_of = []
        columns_of = []
        for side in range(2):
            ok = there["gx"][side]
            mask = edge_rows(s, ok & there["gy"][0], ok & there["gy"][1])
            lines_of.append([jnp.where(mask, exy[r, side, e], 0.0) for e in every])
            columns_of.append(combine(L, exz[r, side, 0], exz[r, side, 1], ok))
        cy = jnp.where(my, combine(L, eyz[r, 0], eyz[r, 1]), 0.0)
        rx = [
            [
                jnp.where(
                    there["gx"][side],
                    px[r, side, e] + L.xt[side, e] * get(e, 0 if side == 0 else n - 1)
                    + L.xst[side, e, 0] * lines_of[side][e]
                    + L.xst[side, e, 1] * unpack(L, columns_of[side], e, n - 1 if side == 0 else 0),
                    0.0,
                )
                for e in every
            ]
            for side in range(2)
        ]

        def ry(e, i):
            got = py[r, e, i] + L.yst[e, i] * get(e, i)
            if i == 0:
                got = got + L.yxw[e, 0] * lines_of[0][e]
            if i == n - 1:
                got = got + L.yxw[e, 1] * lines_of[1][e]
            return jnp.where(my, got, 0.0)

        far = 2 * s * (n - 1)
        sideways = jnp.where(
            zi // (2 * s) % n == 0, roll(columns_of[0], -far, 1), roll(columns_of[1], far, 1)
        )
        toward, along_y, along_x = [combine(L, L.zst[0, k], L.zst[1, k]) for k in range(3)]
        c = combine(L, pz[r, 0], pz[r, 1]) + toward * own + along_y * cy + along_x * sideways
        c = jnp.where(zi < 2 * s * EQ * n, c, 0.0)
        y_ends = L.zs[1] * jnp.where(my, L.yzs[...] * cy, 0.0)
        return (
            lambda side, e: rx[side][e],
            ry,
            ends(L, L.zs[0] * c + y_ends),
        )

    def put(r, L, v):
        for e in every:
            for i in range(L.n):
                field[r, e, i] = v[e][i]

    def planes(f, L):
        return [[f(e, i) for i in range(L.n)] for e in every]

    def deep(r, L):
        get = lambda e, i: field[r, e, i]
        begin(plans[r]["d"], only=("xy",))
        zpack[r, 0] = pack(L, get)
        begin(plans[r]["d"], only=("xz", "yz"))
        begin(plans[r]["v"])
        for e in every:
            for i in range(L.n):
                pfield[r, e, i] = KEEP * get(e, i) + local(L, get, e, i)
        zpack[r, 1] = pack(L, lambda e, i: pfield[r, e, i])
        begin(plans[r]["p"])

        def finish():
            arrive(plans[r]["v"])
            halo = received(L, r, hx, hy, hz)[:3]
            new = planes(lambda e, i: border(L, pfield[r, e, i], halo, e, i), L)

            def outer():
                arrive(plans[r]["d"], plans[r]["p"])
                return ring(L, r, get, zpack[r, 0])

            return new, outer

        return finish

    def coarsen(a, s):
        n = a.shape[0]
        a = jnp.stack([a[2 * i] + a[2 * i + 1] for i in range(n // 2)])
        y, z = iota(a.shape, 1), iota(a.shape, 2)
        a = a + jnp.where((y // s) % 2 == 0, roll(a, -s, 1), roll(a, s, 1))
        a = a + jnp.where((z // s) % 2 == 0, roll(a, -s, 2), roll(a, s, 2))
        return a * 0.125

    def select(a, onehot):
        parts = []
        for _ in range(3):
            parts.append(a.astype(jnp.bfloat16))
            a = a - parts[-1].astype(jnp.float32)
        got = jnp.dot(jnp.concatenate(parts, axis=0), onehot, preferred_element_type=jnp.float32)
        m = a.shape[0]
        return (got[0:m] + got[m : 2 * m]) + got[2 * m :]

    groups = qx * qy
    source = iota((nz, nz), 0)
    target = iota((nz, nz), 1)
    squeeze = jnp.where(source == 4 * (target % qz), 1.0, 0.0).astype(jnp.bfloat16)
    squeeze_pairs = jnp.where(
        (source == 4 * (target % qz)) | (source == 4 * (target % qz) + 2), 1.0, 0.0
    ).astype(jnp.bfloat16)

    def to_rows(a, lanes):
        m = a.shape[0]
        c = select(a.reshape(m * qx * ny, nz), lanes).reshape(m, qx, ny, nz)
        place = iota((m, ny, nz), 2) // qz
        got = jnp.zeros((m, ny, nz), jnp.float32)
        for x in range(qx):
            for y in range(qy):
                part = roll(c[:, x], -4 * y, 1)
                got = jnp.where(place == (x * qy + y + gz) % groups, part, got)
        return got

    def own(small, whole, sem):
        return pltpu.make_async_copy(
            small.at[:, pl.ds(0, 1)], whole.at[X, core, :, pl.ds(row, 1)], sem
        )

    def stage(number, small, whole, rs):
        made = []
        if number == 0:
            for step in range(1, ngx):
                made.append((small.at[:, pl.ds(0, 1)], whole.at[X, core, :, pl.ds(row, 1)],
                             step, device(gx=(gx + step) % ngx)))
        elif number == 1:
            block = whole.at[X, core, :, pl.ds(gy * ngx, ngx)]
            for step in range(1, ngy):
                made.append((block, block, step, device(gy=(gy + step) % ngy)))
        elif number == 2:
            block = whole.at[X, core]
            for step in range(1, nX):
                made.append((block, block, step, device(gz=((X + step) % nX) * cores + core)))
        else:
            block = whole.at[:, core]
            for step in range(1, cores):
                made.append((block, block, step, device(gz=X * cores + (core + step) % cores)))
        return [
            remote(a, z, ws_sem.at[number], rs.at[number], where)
            for a, z, _, where in made
        ]

    wargs = (wsend, wall, wr_sem)

    def everyone():
        mirrored = all(count & (count - 1) == 0 for count in dims)

        def other(index, step, count):
            return index ^ step if mirrored else (index + step) % count

        made = []
        for ay in reversed(range(ngy)):
            for az in reversed(range(ngz)):
                for ax in reversed(range(ngx)):
                    if ax + ay + az == 0:
                        continue
                    made.append(remote(
                        bsend.at[:, pl.ds(0, 1)], ball.at[X, core, :, pl.ds(row, 1)],
                        bs_sem, br_sem,
                        (other(gx, ax, ngx), other(gy, ay, ngy), other(gz, az, ngz)),
                    ))
        return made

    def start(number):
        for copy in stage(number, *wargs):
            copy.start()

    def stage_rows(number):
        return 7 * EQ * (
            ngx - 1, ngx * (ngy - 1), rows * (nX - 1), nX * rows * (cores - 1)
        )[number]

    def done(number):
        await_rows(wr_sem.at[number], stage_rows(number))

    def scale(L, get_w, get_d, e, i):
        n, s = L.n, L.s
        raw = [get_w(e, k, i) for k in range(6)]
        total = get_d(e, i)
        for k in range(6):
            total = total + raw[k]
        c = DAMP / total
        w = [c * raw[k] for k in range(6)]
        L.tot[e, i] = (1.0 / DAMP) * total
        last_y, first_y, last_z, first_z = yi >= ny - s, yi < s, zi >= nz - s, zi < s
        L.cw[e, 0, i] = w[0]
        L.cw[e, 1, i] = w[1]
        L.cw[e, 2, i] = jnp.where(last_y, 0.0, w[2])
        L.cw[e, 3, i] = jnp.where(first_y, 0.0, w[3])
        L.cw[e, 4, i] = jnp.where(last_z, 0.0, w[4])
        L.cw[e, 5, i] = jnp.where(first_z, 0.0, w[5])
        L.st[e, 0, i] = jnp.where(last_y, w[2], jnp.where(first_y, w[3], 0.0))
        L.st[e, 1, i] = jnp.where(last_z, w[4], jnp.where(first_z, w[5], 0.0))
        if i == 0:
            L.xw[e, 0] = w[1]
        if i == n - 1:
            L.xw[e, 1] = w[0]
        if L is L1:
            odd_y, odd_z = yi // s % 2 == 1, zi // s % 2 == 1
            co[e, 1, i] = w[0] if i % 2 == 1 else w[1]
            co[e, 2, i] = jnp.where(odd_y, w[2], w[3])
            co[e, 3, i] = jnp.where(odd_z, w[4], w[5])
            co[e, 0, i] = (
                KEEP + (w[1] if i % 2 == 1 else w[0])
                + jnp.where(odd_y, w[3], w[2]) + jnp.where(odd_z, w[5], w[4])
            )
        return c

    def pack_constants(L):
        L.zs[0] = pack(L, lambda e, i: L.st[e, 1, i])
        L.zs[1] = pack(L, lambda e, i: L.st[e, 0, i])
        L.zs[2] = pack(L, lambda e, i: L.xw[e, 0 if i == 0 else 1], (0, L.n - 1))

    for load in guess_loads:
        load.wait()
    guess = lambda e, i: g_ref[e, i]
    zpack[0, 0] = pack(L0, guess)
    pl.semaphore_wait(barrier, awaited)
    begin(plans[0]["v"])
    hear = found[1] + found[2]

    def tell(k):
        for name, _, _ in axes[1:]:
            for side in range(2):
                @pl.when(there[name][side])
                def _():
                    pl.semaphore_signal(
                        know.at[k], inc=1, device_id=device(**{name: beside[name][side]}),
                        device_id_type=MESH,
                    )

    if close:
        tell(0)
    await_rows(i_sem.at[1], 8 * EQ * nx * ny)
    level2 = [None] * (7 * EQ)
    for e in every:
        d1 = coarsen(d_ref[e], 1)
        level2[6 * EQ + e] = coarsen(d1, 2)
        for k in range(6):
            w = 0.25 * coarsen(w_ref[6 * e + k], 1)
            w1[6 * e + k] = w
            level2[6 * e + k] = 0.25 * coarsen(w, 2)
        for i in range(half):
            c = scale(L1, lambda e, k, i: w1[6 * e + k, i], lambda e, i: d1[i], e, i)
            w1[6 * EQ + e, i] = c
    wsend[...] = to_rows(jnp.stack(level2), squeeze)
    own(wsend, wall, i_sem.at[0]).start()
    start(0)
    for e in every:
        for i in range(nx):
            c = scale(L0, lambda e, k, i: w_ref[6 * e + k, i], lambda e, i: d_ref[e, i], e, i)
            L0.cb[e, i] = c * b_ref[e, i]
    pack_constants(L0)
    begin(constants[0])
    for e in every:
        for i in range(nx):
            pfield[0, e, i] = KEEP * guess(e, i) + local(L0, guess, e, i)
    if close:
        pl.semaphore_wait(know.at[0], hear)
        tell(1)

    arrive(plans[0]["v"])
    halo = received(L0, 0, hx, hy, hz)[:3]
    put(1, L0, planes(lambda e, i: border(L0, pfield[0, e, i], halo, e, i), L0))
    if close:
        pl.semaphore_wait(know.at[1], hear)
    finish = deep(1, L0)
    own(wsend, wall, i_sem.at[0]).wait()
    done(0)
    start(1)
    pack_constants(L1)
    begin(constants[1])
    v, outer = finish()
    kept0 = field.at[0]
    for e in every:
        for i in range(nx):
            kept0[e, i] = v[e][i]
    get = lambda e, i: kept0[e, i]
    q = planes(lambda e, i: local(L0, get, e, i), L0)
    arrive(constants[0])
    halo = outer()
    first = []
    for e in every:
        r = jnp.stack([
            L0.tot[e, i] * (border(L0, q[e][i], halo, e, i) - DAMP * get(e, i)) for i in range(nx)
        ])
        b = coarsen(r, 1)
        first.append([])
        for i in range(half):
            u = w1[6 * EQ + e, i] * b[i]
            L1.cb[e, i] = u
            first[e].append(u)
    put(2, L1, first)
    finish = deep(2, L1)
    done(1)
    start(2)
    for m in range(4):
        cos[m] = pack(L1, lambda e, i: co[e, m, i])
    begin(spreads)
    u, outer = finish()
    kept1 = pfield.at[3]
    for e in every:
        for i in range(half):
            kept1[e, i] = u[e][i]
    get = lambda e, i: kept1[e, i]
    q = planes(lambda e, i: local(L1, get, e, i), L1)
    arrive(constants[1])
    halo = outer()
    rest = []
    for e in every:
        r = []
        for i in range(half):
            total = border(L1, q[e][i], halo, e, i)
            field[3, e, i] = KEEP * get(e, i) + total
            r.append(L1.tot[e, i] * (total - DAMP * get(e, i)))
        r = [r[2 * x] + r[2 * x + 1] for x in range(qx)]
        rest.append(jnp.stack([c + roll(c, -2, 0) for c in r]))
    bsend[...] = 0.125 * to_rows(jnp.stack(rest), squeeze_pairs)
    for copy in everyone():
        copy.start()
    own(bsend, ball, br_sem).start()
    zpack[3, 0] = pack(L1, lambda e, i: field[3, e, i])
    begin(plans[3]["v"])
    arrive(spreads)
    for m in range(4):
        c = combine(L1, coz[0, m], coz[1, m])
        for e in every:
            for i in range(half):
                zco[e, m, i] = unpack(L1, c, e, i)
    NX, NY, NZ = ngx * qx, ngy * qy, ngz * qz
    shape = (NZ, 3 * nz)
    kind, t = iota(shape, 1) // nz, iota(shape, 1) % nz
    base = gz * qz + t // 4
    wanted = jnp.where(
        kind == 0, base,
        jnp.where(
            kind == 1, base + jnp.where(t % 4 < 2, -1, 1),
            jnp.where(t < nz // 2, gz * qz - 1, gz * qz + qz),
        ),
    )
    widen[...] = jnp.where(iota(shape, 0) == wanted, 1.0, 0.0).astype(jnp.bfloat16)
    for e in every:
        for i in range(NX + 2):
            if i in (0, NX + 1):
                e2[e, i] = jnp.zeros((NY + 16, NZ), jnp.float32)
            else:
                e2[e, i, 0:8] = jnp.zeros((8, NZ), jnp.float32)
                e2[e, i, NY + 8 : NY + 16] = jnp.zeros((8, NZ), jnp.float32)
    done(2)
    start(3)
    done(3)
    def spread(ref, index):
        place, y_of = iota((rows, nz), 1) // qz, iota((NY, nz), 0) % qy
        parts = [[] for _ in range(NX)]
        for t in range(NZ // nz):
            moved = []
            for k in range(groups):
                got = None
                for p in range(groups):
                    g = t * groups + (p - k) % groups
                    a = ref[g // cores, g % cores, index]
                    got = a if got is None else jnp.where(place == p, a, got)
                moved.append(roll(got, -k * qz, 1))
            for x in range(qx):
                if ngx != qy:
                    for y in range(qy):
                        mix[...] = moved[x * qy + y]
                        for g in range(ngx):
                            mixed[g, pl.ds(y, ngy, stride=qy), :] = mix[pl.ds(g, ngy, stride=ngx), :]
                for g in range(ngx):
                    if ngx != qy:
                        got = mixed[g]
                    else:
                        got = roll(moved[x * qy], -g, 0)
                        for y in range(1, qy):
                            got = jnp.where(y_of == y, roll(moved[x * qy + y], y - g, 0), got)
                    parts[g * qx + x].append(got)
        return [p[0] if len(p) == 1 else jnp.concatenate(p, axis=1) for p in parts]

    Y, Z = iota((NY, NZ), 0), iota((NY, NZ), 1)
    even_y, even_z = Y % 2 == 0, Z % 2 == 0
    pairs = NX // 4

    def halve(a):
        made = []
        for p in range(pairs):
            two = []
            for x in (2 * p, 2 * p + 1):
                c = a[2 * x] + a[2 * x + 1]
                two.append(c + jnp.where(even_y, roll(c, -1, 0), roll(c, 1, 0)))
            c = jnp.where(even_y, two[0], two[1])
            made.append(0.125 * (c + jnp.where(even_z, roll(c, -1, 1), roll(c, 1, 1))))
        return made

    def double(a, x):
        c = a[x // 4]
        if x // 2 % 2 == 0:
            return jnp.where(even_y, c, roll(c, 1, 0))
        return jnp.where(even_y, roll(c, -1, 0), c)

    def tree(terms):
        while len(terms) > 1:
            terms = [
                terms[k] + terms[k + 1] if k + 1 < len(terms) else terms[k]
                for k in range(0, len(terms), 2)
            ]
        return terms[0]

    def around2(w, v):
        made = []
        for x in range(NX):
            terms = [
                w[4][x] * roll(v[x], -1, 1), w[5][x] * roll(v[x], 1, 1),
                w[2][x] * roll(v[x], -1, 0), w[3][x] * roll(v[x], 1, 0),
            ]
            if x < NX - 1:
                terms.append(w[0][x] * v[x + 1])
            if x > 0:
                terms.append(w[1][x] * v[x - 1])
            made.append(tree(terms))
        return made

    def around3(w, v):
        made = []
        for p in range(pairs):
            up, down = roll(v[p], -1, 0), roll(v[p], 1, 0)
            if p < pairs - 1:
                up = jnp.where(even_y, up, roll(v[p + 1], 1, 0))
            if p > 0:
                down = jnp.where(even_y, roll(v[p - 1], -1, 0), down)
            made.append(tree([
                w[4][p] * roll(v[p], -2, 1), w[5][p] * roll(v[p], 2, 1),
                w[0][p] * up, w[1][p] * down,
                w[2][p] * roll(v[p], -2, 0), w[3][p] * roll(v[p], 2, 0),
            ]))
        return made

    steps3 = ((-1, 0), (1, 0), (-2, 0), (2, 0), (0, -2), (0, 2))

    def shifted(v, dr, dl):
        return roll(roll(v, dl, 1), dr, 0)

    def twice(w):
        got = {(0, 0): KEEP * KEEP}

        def add(at, value):
            at = (at[0] % NY, at[1] % NZ)
            got[at] = got[at] + value if at in got else value

        for k, (dr, dl) in enumerate(steps3):
            add((dr, dl), 2.0 * KEEP * w[k])
            for m, (er, el) in enumerate(steps3):
                if k == m and k < 2:
                    continue
                add((dr + er, dl + el), w[k] * shifted(w[m], dr, dl))
        return got

    def apply_twice(w, v):
        turned = {dl: roll(v, dl, 1) for dl in sorted({at[1] for at in w})}
        return tree([c * roll(turned[dl], dr, 0) for (dr, dl), c in w.items()])

    def inner(w, k, at, last, step):
        if k == 0 and step == 2:
            return jnp.where(even_y, w, 0.0) if at == last else w
        if k == 1 and step == 2:
            return jnp.where(even_y, 0.0, w) if at == 0 else w
        if k < 2:
            return w
        return jnp.where((Y >= NY - step, Y < step, Z >= NZ - step, Z < step)[k - 2], 0.0, w)

    def constants_of(plain, diagonal, count, step):
        scaled, totals, weights = [], [], [[] for _ in range(6)]
        for at in range(count):
            total = diagonal[at] + tree([plain[k][at] for k in range(6)])
            scaled.append(DAMP / total)
            totals.append((1.0 / DAMP) * total)
            for k in range(6):
                weights[k].append(inner(scaled[at] * plain[k][at], k, at, count - 1, step))
        return scaled, totals, weights

    c2, t2, w2, c3, w3, ww3 = [], [], [], [], [], []
    by_two = pairs == 1 and NY >= 8 and COARSE_SWEEPS % 2 == 0
    for e in every:
        plain = [spread(wall, 6 * e + k) for k in range(6)]
        diagonal = spread(wall, 6 * EQ + e)
        scaled, totals, weights = constants_of(plain, diagonal, NX, 1)
        c2.append(scaled)
        t2.append(totals)
        w2.append(weights)
        coarse = [[0.25 * c for c in halve(plain[k])] for k in range(6)]
        scaled, _, weights = constants_of(coarse, halve(diagonal), pairs, 2)
        c3.append(scaled)
        w3.append(weights)
        if by_two:
            ww3.append(twice([weights[k][0] for k in range(6)]))

    arrive(plans[3]["v"])
    pltpu.make_async_copy(ball, ball, br_sem).wait()
    rhs = []
    for e in every:
        got = spread(ball, e)
        rhs.append([c2[e][x] * got[x] for x in range(NX)])

    def smooth2(v):
        made = []
        for e in every:
            sums = around2(w2[e], v[e])
            made.append([(KEEP * v[e][x] + rhs[e][x]) + sums[x] for x in range(NX)])
        return made

    v2 = rhs
    for step in range(SWEEPS - 1):
        v2 = smooth2(v2)
    rhs3 = []
    for e in every:
        sums = around2(w2[e], v2[e])
        got = halve([t2[e][x] * ((rhs[e][x] - DAMP * v2[e][x]) + sums[x]) for x in range(NX)])
        rhs3.append([c3[e][p] * got[p] for p in range(pairs)])
    v3 = rhs3
    for step in range(1 if by_two else COARSE_SWEEPS - 1):
        sums = [around3(w3[e], v3[e]) for e in every]
        v3 = [
            [(KEEP * v3[e][p] + rhs3[e][p]) + sums[e][p] for p in range(pairs)] for e in every
        ]
    if by_two:
        once = v3
        for step in range(COARSE_SWEEPS // 2 - 1):
            v3 = [[apply_twice(ww3[e], v3[e][0]) + once[e][0]] for e in every]
    v2 = [[v2[e][x] + double(v3[e], x) for x in range(NX)] for e in every]
    for step in range(SWEEPS):
        v2 = smooth2(v2)
    for e in every:
        for x in range(NX):
            e2[e, x + 1, 8 : 8 + NY] = v2[e][x]

    wx, wy = qx + 2, qy + 2
    for e in every:
        for i in range(wx):
            for j in range(wy):
                at = (e * wx + i) * wy + j
                lines[at : at + 1, :] = e2[e, gx * qx + i, pl.ds(7 + gy * qy + j, 1), :]
    broad[...] = select(lines[...], widen[...])
    CENTER, BEYOND_Z, OUTSIDE_Z = range(3)
    ysel, yhalf = yi // 4, yi // 2 % 2

    def strip(kind, e, x, y):
        at = (e * wx + x + 1) * wy + y + 1
        return jnp.broadcast_to(broad[at : at + 1, kind * nz : kind * nz + nz], tile)

    def plane(kind, e, x):
        got = strip(kind, e, x, 0)
        for y in range(1, qy):
            got = jnp.where(ysel == y, strip(kind, e, x, y), got)
        return got

    def across_y(kind, e, x):
        got = None
        for y in range(qy):
            both = jnp.where(yhalf == 0, strip(kind, e, x, y - 1), strip(kind, e, x, y + 1))
            got = both if got is None else jnp.where(ysel == y, both, got)
        return got

    def across_x(kind, e, i):
        return plane(kind, e, i // 2 + (1 if i % 2 == 1 else -1))

    def rows_y(kind, e, x):
        return jnp.where(yi < ny // 2, strip(kind, e, x, -1), strip(kind, e, x, qy))

    left, behind, _, columns = received(L1, 3, hx, hy, hz)
    mine = edge_rows(L1.s, *there["gy"])

    def add_x(side, e):
        face, near = (-1, 0) if side == 0 else (qx, qx - 1)
        got = left(side, e) + cox[side, e, 0] * plane(CENTER, e, face)
        got = got + cox[side, e, 1] * plane(CENTER, e, near)
        got = got + cox[side, e, 2] * across_y(CENTER, e, face)
        got = got + cox[side, e, 3] * plane(BEYOND_Z, e, face)
        return jnp.where(there["gx"][side], got, 0.0)

    def add_y(e, i):
        x = i // 2
        got = behind(e, i) + coy[e, 0, i] * rows_y(CENTER, e, x)
        got = got + coy[e, 1, i] * rows_y(CENTER, e, x + 1 if i % 2 == 1 else x - 1)
        got = got + coy[e, 2, i] * plane(CENTER, e, x)
        got = got + coy[e, 3, i] * rows_y(BEYOND_Z, e, x)
        return jnp.where(mine, got, 0.0)

    def add_z(e, i):
        x = i // 2
        got = unpack(L1, columns, e, i) + zco[e, 0, i] * plane(OUTSIDE_Z, e, x)
        got = got + zco[e, 1, i] * across_x(OUTSIDE_Z, e, i)
        got = got + zco[e, 2, i] * across_y(OUTSIDE_Z, e, x)
        return L1.st[e, 1, i] * (got + zco[e, 3, i] * plane(CENTER, e, x))

    swept = pfield.at[3]
    for e in every:
        for i in range(half):
            x = i // 2
            got = field[3, e, i] + co[e, 0, i] * plane(CENTER, e, x)
            got = got + co[e, 1, i] * across_x(CENTER, e, i)
            got = got + co[e, 2, i] * across_y(CENTER, e, x)
            swept[e, i] = got + co[e, 3, i] * plane(BEYOND_Z, e, x)
    get = lambda e, i: swept[e, i]
    halo = (add_x, add_y, add_z)
    u = planes(lambda e, i: KEEP * get(e, i) + border(L1, local(L1, get, e, i), halo, e, i), L1)
    put(4, L0, planes(lambda e, i: kept0[e, i] + u[e][i // 2], L0))
    finish = deep(4, L0)
    v, outer = finish()
    last = pfield.at[0]
    for e in every:
        for i in range(nx):
            last[e, i] = v[e][i]
    get = lambda e, i: last[e, i]
    q = planes(lambda e, i: KEEP * get(e, i) + local(L0, get, e, i), L0)
    halo = outer()
    for e in every:
        for i in range(nx):
            out_ref[e, i] = border(L0, q[e][i], halo, e, i)
    await_all(s_sem, [g for p in plans for g in p.values()] + constants + [spreads])
    for number in range(4):
        await_rows(ws_sem.at[number], stage_rows(number))
    await_rows(bs_sem, EQ * (rows * ngz - 1))


def per_device(dims, cores, couplings, diagonal, right_side, guess):
    ngx, ngy, ngz = dims
    brick = guess.shape[1:]
    nx, ny, nz = brick
    half = nx // 2
    qx, qy, qz = nx // 4, ny // 4, nz // 4
    rows = ngx * ngy
    nX = ngz // cores
    rounds = len(DEEP)
    f32 = jnp.float32
    vmem = pltpu.VMEM
    dma = pltpu.SemaphoreType.DMA

    def level(n):
        return [
            vmem((EQ, 6, n, ny, nz), f32),
            vmem((EQ, 2, n, ny, nz), f32),
            vmem((EQ, 2, ny, nz), f32),
            vmem((EQ, n, ny, nz), f32),
            vmem((EQ, n, ny, nz), f32),
            vmem((3, ny, nz), f32),
            vmem((2, EQ, ny, nz), f32),
            vmem((2, EQ, 2, ny, nz), f32),
            vmem((EQ, n, ny, nz), f32),
            vmem((ny, nz), f32),
            vmem((EQ, 2, ny, nz), f32),
            vmem((2, 3, ny, nz), f32),
            dma,
        ]

    faces = [
        vmem((rounds, 2, EQ, ny, nz), f32),
        vmem((rounds, EQ) + brick, f32),
        vmem((rounds, 2, ny, nz), f32),
    ]
    return pl.pallas_call(
        functools.partial(kernel, dims, cores),
        out_shape=vmem(guess.shape, f32),
        in_specs=[pl.BlockSpec(memory_space=pl.ANY)] * 4,
        out_specs=pl.BlockSpec(memory_space=vmem),
        scratch_shapes=[
            vmem(couplings.shape, f32),
            vmem(diagonal.shape, f32),
            vmem(right_side.shape, f32),
            vmem(guess.shape, f32),
            vmem((max(2048, nX * rows * 7 * EQ * (cores - 1) // 8, rows * (nX - 1) * 7 * EQ // 8), 8, nz), f32),
            vmem((rounds, EQ) + brick, f32),
            vmem((rounds, EQ) + brick, f32),
            vmem((rounds, 2, ny, nz), f32),
            *faces,
            *faces,
            vmem((rounds, 2, EQ, ny, nz), f32),
            vmem((rounds, 2, 2, ny, nz), f32),
            vmem((rounds, 2, ny, nz), f32),
            vmem((7 * EQ, half, ny, nz), f32),
            vmem((EQ, 4, half, ny, nz), f32),
            vmem((4, ny, nz), f32),
            vmem((2, EQ, 4, ny, nz), f32),
            vmem((EQ, 4, half, ny, nz), f32),
            vmem((2, 4, ny, nz), f32),
            vmem((EQ, 4, half, ny, nz), f32),
            *level(nx),
            *level(half),
            vmem((7 * EQ, ny, nz), f32),
            vmem((nX, cores, 7 * EQ, rows, nz), f32),
            vmem((EQ, ny, nz), f32),
            vmem((nX, cores, EQ, rows, nz), f32),
            vmem((EQ, ngx * qx + 2, ngy * qy + 16, ngz * qz), f32),
            vmem((EQ * (qx + 2) * (qy + 2), ngz * qz), f32),
            vmem((EQ * (qx + 2) * (qy + 2), 3 * nz), f32),
            vmem((ngz * qz, 3 * nz), jnp.bfloat16),
            vmem((rows, nz), f32),
            vmem((ngx, ngy * qy, nz), f32),
            dma,
            dma((4,)),
            dma,
            dma((4,)),
            dma((4,)),
            dma,
            dma,
            dma((2,)),
            dma((3,)),
            pltpu.SemaphoreType.REGULAR((2,)),
        ],
        compiler_params=pltpu.CompilerParams(
            collective_id=0, has_side_effects=True, vmem_limit_bytes=60 * 1024 * 1024
        ),
    )(couplings, diagonal, right_side, guess)


def solution(mesh):
    dims = (mesh.shape["gx"], mesh.shape["gy"], mesh.shape["gz"])
    cores = 2 if dims[2] % 2 == 0 else 1
    spec = P(None, "gx", "gy", "gz")
    return jax.shard_map(
        functools.partial(per_device, dims, cores),
        mesh=mesh,
        in_specs=(spec,) * 4,
        out_specs=spec,
        check_vma=False,
    )
```
